128 devices in a mesh: batch: 16 (over y, x), slab: 8 (over z, core).
Axes of the slice: x: 4, y: 4, z: 4, core: 2. Of those that a mesh axis runs over, the one named last changes fastest.
Arguments:
- images: bfloat16 [1024, 384, 384], P(('batch', 'slab')), may hold values from -6 to 6
- classes: int32 [1024], P(('batch', 'slab')), may hold values from 0 to 767
- shifts: int32 [1024, 2], P(('batch', 'slab')), may hold values from -16 to 16
- defocus_class: int32 [1024], P(('batch', 'slab')), may hold values from 0 to 15
- defocus: float32 [16], replicated, may hold values from 150 to 600
- run_counts: int32 [1024, 8], P(('batch', 'slab')), may hold values from 1 to 96, 384 in all within a row
- dest_map: int32 [768, 384], replicated, may hold values from 0 to 15
- ref: bfloat16 [384, 128, 768], P('batch', 'slab'), may hold values from -6 to 6
Outputs:
- updated: bfloat16 [384, 128, 768], P('batch', 'slab')
The draws below stay inside these ranges and needn't reach their ends.
Inputs may be any that keep to these rules, and one draw needn't show every extreme that they name: `run_counts`: each particle's counts sum to 384; in every particle's row the largest count is exactly 96.
All inputs are finite; a program needn't handle non-finite values.
Results may differ from the reference program's by a relative error of at most 0.0065.
Values may be sent and summed in bfloat16 or wider, within the bound.
A program may use at most 128 MiB of HBM per device.

```python
import math
import jax
import jax.numpy as jnp
import numpy as np
from jax import lax

K = 384
PL_DEV = 16
NCLS = 768
NDEF = 16
SHIFT = 16
PARTICLES = 1024
PLANES = 128
MOST = 96
N_SLAB = 8


def place_ends(entries, rng, least, largest):
    dims = entries.shape
    spot = [jax.random.randint(jax.random.fold_in(rng, axis), (), 0, dims[axis]) for axis in range(len(dims))]
    entries = entries.at[tuple(spot)].set(least)
    longest = dims.index(max(dims))
    spot[longest] = (spot[longest] + 1) % dims[longest]
    return entries.at[tuple(spot)].set(largest)


def shard_levels(key, extent, shards, low, top_value):
    loudness, own = 1.0, jax.random.fold_in(key, 6)
    for position, blocks in shards:
        draws = jnp.exp(jax.random.uniform(jax.random.fold_in(own, position), (blocks,), jnp.float32, low / len(shards), top_value / len(shards)))
        loudness = loudness * jnp.repeat(draws, extent[position] // blocks).reshape([-1 if axis == position else 1 for axis in range(len(extent))])
    return loudness


def length_profile(number_of, total, reach, lean):
    weights = [(1 << 20) // math.isqrt(standing ** lean) + 1 for standing in range(2, number_of + 1)]
    surplus, holding = total - reach - (number_of - 1), [1] * (number_of - 1)
    while surplus > 0:
        movable = [i for i in range(number_of - 1) if holding[i] < reach]
        whole, left = sum([weights[i] for i in movable]), surplus
        for i in movable:
            addition = min(reach - holding[i], max(1, left * weights[i] // whole), surplus)
            holding[i] = holding[i] + addition
            surplus = surplus - addition
    return np.array([reach] + holding)


def uneven_parts(rng, amount, total, bound, slope):
    if amount == 2:
        one = jax.random.randint(rng, (), max(1, total - bound), min(bound, total - 1) + 1)
        return jnp.stack([one, total - one])
    lengths = jnp.asarray(length_profile(amount, total, bound, slope), jnp.int32)
    pairs = (amount - 1) // 2
    source_of, receiver = lengths[1:1 + 2 * pairs:2], lengths[2:2 + 2 * pairs:2]
    room = jnp.minimum(source_of - 1, bound - receiver)
    passed = jax.random.randint(jax.random.fold_in(rng, 1), (pairs,), 0, 1 << 20) % (room + 1)
    lengths = lengths.at[1:1 + 2 * pairs:2].set(source_of - passed).at[2:2 + 2 * pairs:2].set(receiver + passed)
    return lengths[jax.random.permutation(jax.random.fold_in(rng, 2), amount)]


def scatter_about(rng, extent, spread, most, split=(), held_as=jnp.bfloat16):
    drawn = spread * jax.random.normal(rng, extent, jnp.float32)
    if split:
        drawn = drawn * shard_levels(rng, extent, split, -0.22, 0.18)
    return jnp.clip(drawn, -most, most).astype(held_as)


def setup_inputs(seed: int = 0) -> dict:
    arg_keys = jax.random.split(jax.random.key(seed), 9)
    return {
        "images": scatter_about(arg_keys[0], (PARTICLES, K, K), 1.0, 6.0, ((0, 128),)),
        "classes": place_ends(jax.random.randint(arg_keys[1], (PARTICLES,), 0, NCLS), jax.random.fold_in(arg_keys[1], 1), 0, NCLS - 1).astype(jnp.int32),
        "shifts": place_ends(jax.random.randint(arg_keys[2], (PARTICLES, 2), 0 - SHIFT, SHIFT + 1), jax.random.fold_in(arg_keys[2], 1), 0 - SHIFT, SHIFT).astype(jnp.int32),
        "defocus_class": place_ends(jax.random.randint(arg_keys[3], (PARTICLES,), 0, NDEF), jax.random.fold_in(arg_keys[3], 1), 0, NDEF - 1).astype(jnp.int32),
        "defocus": jnp.clip(jnp.exp(jax.random.uniform(arg_keys[4], (NDEF,), jnp.float32, math.log(150.0), math.log(600.0))), 150.0, 600.0),
        "run_counts": jax.vmap(lambda own: uneven_parts(own, N_SLAB, K, MOST, 2))(jax.random.split(arg_keys[5], PARTICLES)).reshape((PARTICLES, N_SLAB)).astype(jnp.int32),
        "dest_map": place_ends(jax.random.randint(arg_keys[6], (NCLS, K), 0, PL_DEV), jax.random.fold_in(arg_keys[6], 1), 0, PL_DEV - 1).astype(jnp.int32),
        "ref": scatter_about(arg_keys[7], (K, PLANES, 2 * K), 1.0, 6.0, ((0, 16), (1, 8))),
    }


TAU_PRIOR = 4.0
PHASE_OFFSET = 0.1

def dft_tables(length):
    index = jnp.arange(length, dtype=jnp.int32)
    turns = index[:, None] * index[None, :] % length
    angle = 2.0 * math.pi / length * turns.astype(jnp.float32)
    factor = 1.0 / math.sqrt(length)
    cosine = jnp.cos(angle) * factor
    sine = jnp.sin(angle) * factor
    table_left = jnp.concatenate([cosine, -sine], axis=0).astype(jnp.bfloat16)
    upper_rows = jnp.concatenate([cosine, -sine], axis=1)
    lower_rows = jnp.concatenate([sine, cosine], axis=1)
    table_right = jnp.concatenate([upper_rows, lower_rows], axis=0).astype(jnp.bfloat16)
    return (table_left, table_right)

def contrast(focus_value, freq_row, freq_col, length):
    half_length = length // 2
    spatial_row = ((freq_row + half_length) % length - half_length).astype(jnp.float32) / length
    spatial_col = ((freq_col + half_length) % length - half_length).astype(jnp.float32) / length
    return -jnp.sin(focus_value * (spatial_row * spatial_row + spatial_col * spatial_col) + PHASE_OFFSET)

def shifted_parts(real_part, imag_part, shift_x, shift_y, freq_row, freq_col, length):
    turns = (freq_col * shift_x + freq_row * shift_y) % length
    angle = 2.0 * math.pi / length * turns.astype(jnp.float32)
    cosine = jnp.cos(angle)
    sine = jnp.sin(angle)
    return (real_part * cosine + imag_part * sine, imag_part * cosine - real_part * sine)

def reference(images, classes, shifts, defocus_class, defocus, run_counts, dest_map, ref):
    table_left, table_right = dft_tables(K)
    left_wide = table_left.astype(jnp.float32)
    right_wide = table_right.astype(jnp.float32)
    rows_all = jnp.arange(K, dtype=jnp.int32)
    freq_row = rows_all[:, None]
    freq_col = rows_all[None, :]

    def insert(carry, inputs):
        numerator, weights = carry
        image, orient, shift, focus, counts = inputs
        section = jnp.dot(left_wide, image.astype(jnp.float32), precision=lax.Precision.HIGHEST).astype(jnp.bfloat16)
        section = lax.optimization_barrier(section)
        joined = jnp.concatenate([section[:K], section[K:]], axis=1).astype(jnp.float32)
        spectrum = jnp.dot(joined, right_wide, precision=lax.Precision.HIGHEST)
        real_part, imag_part = shifted_parts(spectrum[:, :K], spectrum[:, K:], shift[0], shift[1], freq_row, freq_col, K)
        transfer = contrast(defocus[focus], freq_row, freq_col, K)
        weighted = jnp.concatenate([transfer * real_part, transfer * imag_part], axis=1).astype(jnp.bfloat16)
        weighted = lax.optimization_barrier(weighted)
        run_ends = jnp.cumsum(counts)
        owner = lax.optimization_barrier(jnp.sum((rows_all[:, None] >= run_ends[None, :]).astype(jnp.int32), axis=1))
        plane = (owner * PL_DEV + dest_map[orient]).astype(jnp.int32)
        numerator = numerator.at[rows_all, plane].add(weighted.astype(jnp.float32))
        weights = weights.at[rows_all, plane].add(transfer * transfer)
        return ((numerator, weights), None)
    start = (jnp.zeros((K, PLANES, 2 * K), jnp.float32), jnp.zeros((K, PLANES, K), jnp.float32))
    (numerator, weights), unused = lax.scan(insert, start, (images, classes, shifts, defocus_class, run_counts))
    prior = ref.astype(jnp.float32)
    denom = weights + TAU_PRIOR
    real_new = (TAU_PRIOR * prior[..., :K] + numerator[..., :K]) / denom
    imag_new = (TAU_PRIOR * prior[..., K:] + numerator[..., K:]) / denom
    return jnp.concatenate([real_new, imag_new], axis=2).astype(jnp.bfloat16)
```

```python
import functools
import math

import jax
import jax.numpy as jnp
import ml_dtypes
import numpy as np
from jax import lax
from jax.experimental import pallas as pl
from jax.experimental.pallas import tpu as pltpu
from jax.sharding import PartitionSpec as P

TAU_PRIOR = 4.0
PHASE_OFFSET = 0.1
MESH = pl.DeviceIdType.MESH

K = 384
NB = 16
NS = 8
PP = 8
KYB = K // NB
CH = 3
KYC = KYB // CH
PAIRS = KYC // 2
PL = 16
NDEF = 16
BF = jnp.bfloat16
F32 = jnp.float32


def chunk_rows():
    rows = [
        KYB * b + KYC * c + i for c in range(CH) for b in range(NB) for i in range(KYC)
    ]
    return np.array(rows, np.int32).reshape(CH, NB * KYC)


def tables():
    index = np.arange(K)
    angle = 2.0 * np.pi / K * ((index[:, None] * index[None, :]) % K)
    cosine = (np.cos(angle) / math.sqrt(K)).astype(np.float32)
    sine = (np.sin(angle) / math.sqrt(K)).astype(np.float32)
    rows = chunk_rows()
    left = np.stack(
        [np.concatenate([cosine[r], -sine[r]], axis=0) for r in rows], axis=0
    ).astype(ml_dtypes.bfloat16)
    right = np.concatenate(
        [np.concatenate([cosine, -sine], 1), np.concatenate([sine, cosine], 1)], 0
    ).astype(ml_dtypes.bfloat16)
    return left, right


def split3(x):
    high = lax.reduce_precision(x, 8, 7)
    rest = x - high
    mid = lax.reduce_precision(rest, 8, 7)
    low = rest - mid
    return high, mid, low


def kernel(
    img, left, right, uu, vv, codes, tw, rw, ref,
    out,
    scr, sendb, recvb, crecv, zsend, zrecv, nsend, nrecv, wts,
    code_s, code_r, row_s, row_r, z_s, z_r, n_s, n_r,
):
    mb = lax.axis_index("batch")
    ms = lax.axis_index("slab")
    core = lax.rem(ms, 2)
    zbase = ms - core
    mz = ms // 2
    me = mb * 2 + core

    barrier = pltpu.get_barrier_semaphore()

    def greet_plane(q, carry):
        i = lax.rem(me + q, 32)
        pl.semaphore_signal(
            barrier, inc=1, device_id=(i // 2, zbase + lax.rem(i, 2)), device_id_type=MESH
        )
        return carry

    def greet_slab(q, carry):
        pl.semaphore_signal(
            barrier, inc=1, device_id=(mb, lax.rem(ms + q, NS)), device_id_type=MESH
        )
        return carry

    lax.fori_loop(1, 32, greet_plane, 0)
    lax.fori_loop(1, NS, greet_slab, 0)

    def compute(c):
        def two(pp, carry):
            lc = left[c]
            for j in range(2):
                p = pp * 2 + j
                sec = jnp.dot(lc, img[p], preferred_element_type=F32).astype(BF)
                joined = jnp.concatenate([sec[:128], sec[128:]], axis=1)
                spec = jnp.dot(joined, right[...], preferred_element_type=F32)
                factor = jnp.dot(
                    uu[p, pl.ds(pl.multiple_of(c * 128, 128), 128), :],
                    vv[p],
                    preferred_element_type=F32,
                )
                sr, si = spec[:, :K], spec[:, K:]
                fr, fi = factor[:, :K], factor[:, K:]
                wr = sr * fr - si * fi
                wi = sr * fi + si * fr
                for g in range(3):
                    cols = slice(g * 128, (g + 1) * 128)
                    scr[g, pl.ds(p, 128, stride=8), :] = wr[:, cols]
                    scr[3 + g, pl.ds(p, 128, stride=8), :] = wi[:, cols]
            return carry

        lax.fori_loop(0, PP // 2, two, 0)

    def send_rows(c):
        def one(q, carry):
            b = lax.rem(mb + q, NB)
            start = pl.multiple_of(b * 64, 64)
            for h in range(2):
                for g in range(3):
                    sendb[c, b * 2 + h, :, pl.ds(g * 128, 128)] = scr[
                        3 * h + g, pl.ds(start, 64), :
                    ].astype(BF)
            for h in range(2):
                def remote(h=h):
                    pltpu.make_async_remote_copy(
                        src_ref=sendb.at[c, b * 2 + h],
                        dst_ref=recvb.at[c, me],
                        send_sem=row_s.at[c],
                        recv_sem=row_r.at[c],
                        device_id=(b, zbase + h),
                        device_id_type=MESH,
                    ).start()

                def local(h=h):
                    pltpu.make_async_copy(
                        sendb.at[c, b * 2 + h], recvb.at[c, me], row_r.at[c]
                    ).start()

                own = jnp.logical_and(q == 0, core == h)
                pl.when(own)(local)
                pl.when(jnp.logical_not(own))(remote)
            return carry

        lax.fori_loop(0, NB, one, 0)

    compute(0)
    pl.semaphore_wait(barrier, 31 + NS - 1)

    def send_codes(q, carry):
        i = lax.rem(me + q, 32)
        pltpu.make_async_remote_copy(
            src_ref=codes.at[i // 2],
            dst_ref=crecv.at[pl.ds(pl.multiple_of(me * 16, 16), 16), :],
            send_sem=code_s,
            recv_sem=code_r,
            device_id=(i // 2, zbase + lax.rem(i, 2)),
            device_id_type=MESH,
        ).start()
        return carry

    pltpu.make_async_copy(
        codes.at[mb], crecv.at[pl.ds(pl.multiple_of(me * 16, 16), 16), :], code_r
    ).start()
    lax.fori_loop(1, 32, send_codes, 0)
    send_rows(0)

    def produce(c, carry):
        compute(c)
        send_rows(c)
        return carry

    lax.fori_loop(1, CH, produce, 0)

    pltpu.make_async_copy(crecv, crecv, code_r).wait()

    lane = lax.broadcasted_iota(jnp.int32, (32, 128), 1)
    sub = lax.broadcasted_iota(jnp.int32, (32, 128), 0)
    mine = (lane // 16) == lax.rem(sub, 8)

    def pair_codes(pair):
        got = crecv[pl.ds(pair, 32, stride=16), :]
        return jnp.sum(jnp.where(mine, got, 0).reshape(4, 8, 128), axis=1)

    spot = lax.broadcasted_iota(jnp.int32, (256, 128), 0)

    def one_hot(code4):
        place = code4 & 255
        return jnp.concatenate(
            [
                jnp.where(spot == place[g : g + 1, :], 1.0, 0.0).astype(BF)
                for g in range(4)
            ],
            axis=1,
        )

    row_id = lax.broadcasted_iota(jnp.int32, (128, 128), 0)
    row_class = jnp.where(row_id < 3 * NDEF, lax.rem(row_id, NDEF), -1)

    def count(pair, carry):
        code4 = pair_codes(pair)
        kind = code4 >> 8
        kinds = jnp.concatenate(
            [
                jnp.where(row_class == kind[g : g + 1, :], 1.0, 0.0).astype(BF)
                for g in range(4)
            ],
            axis=1,
        )
        tally = lax.dot_general(
            one_hot(code4), kinds, (((1,), (1,)), ((), ())), preferred_element_type=F32
        )
        start = pl.multiple_of(pair * 32, 32)
        nsend[:, pl.ds(start, 32), :] = tally.astype(BF).reshape(NS, 32, 128)
        return carry

    lax.fori_loop(0, CH * PAIRS, count, 0)

    pltpu.make_async_copy(nsend.at[ms], nrecv.at[mz], n_r).start()

    def send_counts(q, carry):
        peer = lax.rem(ms + 2 * q, NS)
        pltpu.make_async_remote_copy(
            src_ref=nsend.at[peer],
            dst_ref=nrecv.at[mz],
            send_sem=n_s,
            recv_sem=n_r,
            device_id=(mb, peer),
            device_id_type=MESH,
        ).start()
        return carry

    lax.fori_loop(1, NS // 2, send_counts, 0)

    def scatter(c, carry):
        pltpu.make_async_copy(recvb.at[c], recvb.at[c], row_r.at[c]).wait()

        def one(j, inner):
            start = pl.multiple_of(j * 16, 16)
            rows = recvb[c, :, pl.ds(start, 16), :].reshape(512, K)
            hot = one_hot(pair_codes(c * PAIRS + j))
            part = jnp.dot(hot, rows, preferred_element_type=F32)
            zsend[c, :, pl.ds(pl.multiple_of(j * 32, 32), 32), :] = part.astype(
                BF
            ).reshape(NS, 32, K)
            return inner

        lax.fori_loop(0, PAIRS, one, 0)

        pltpu.make_async_copy(zsend.at[c, ms], zrecv.at[c, ms], z_r.at[c]).start()

        def send(q, inner):
            peer = lax.rem(ms + q, NS)
            pltpu.make_async_remote_copy(
                src_ref=zsend.at[c, peer],
                dst_ref=zrecv.at[c, ms],
                send_sem=z_s.at[c],
                recv_sem=z_r.at[c],
                device_id=(mb, peer),
                device_id_type=MESH,
            ).start()
            return inner

        lax.fori_loop(1, NS, send, 0)
        return carry

    lax.fori_loop(0, CH, scatter, 0)

    pltpu.make_async_copy(nrecv, nrecv, n_r).wait()
    totals = (
        nrecv[0].astype(F32) + nrecv[1].astype(F32) + nrecv[2].astype(F32) + nrecv[3].astype(F32)
    )
    wts[...] = (
        jnp.dot(
            totals * tw[...], rw[...], precision=lax.Precision.HIGHEST,
            preferred_element_type=F32,
        )
        + TAU_PRIOR
    )

    def finish(c, carry):
        pltpu.make_async_copy(zrecv.at[c], zrecv.at[c], z_r.at[c]).wait()
        start = pl.multiple_of(c * 128, 128)
        denom = wts[pl.ds(start, 128), :]
        for h in range(2):
            total = TAU_PRIOR * ref[pl.ds(start, 128), pl.ds(h * K, K)].astype(F32)
            for z in range(NS // 2):
                total += zrecv[c, 2 * z + h].astype(F32)
            out[pl.ds(start, 128), pl.ds(h * K, K)] = (total / denom).astype(BF)
        return carry

    lax.fori_loop(0, CH, finish, 0)

    def drain(src, dst, send_sem, recv_sem):
        pltpu.make_async_remote_copy(
            src_ref=src, dst_ref=dst, send_sem=send_sem, recv_sem=recv_sem,
            device_id=(mb, ms), device_id_type=MESH,
        ).wait_send()

    drain(crecv.at[pl.ds(0, 31 * 16), :], crecv.at[pl.ds(0, 31 * 16), :], code_s, code_r)
    drain(nsend.at[pl.ds(0, 3)], nsend.at[pl.ds(0, 3)], n_s, n_r)

    def drain_chunk(c, carry):
        drain(sendb.at[c, pl.ds(0, 31)], recvb.at[c, pl.ds(0, 31)], row_s.at[c], row_r.at[c])
        drain(zsend.at[c, pl.ds(0, 7)], zrecv.at[c, pl.ds(0, 7)], z_s.at[c], z_r.at[c])
        return carry

    lax.fori_loop(0, CH, drain_chunk, 0)


def per_device(images, classes, shifts, defocus_class, defocus, run_counts, dest_map, ref):
    left, right = tables()
    rows = jnp.asarray(chunk_rows().reshape(-1))
    freq = jnp.arange(K, dtype=jnp.int32)

    def square(k):
        half = ((k + K // 2) % K - K // 2).astype(F32) / K
        return half * half

    own_focus = jnp.sum(
        jnp.where(defocus_class[:, None] == jnp.arange(NDEF)[None, :], defocus[None, :], 0.0),
        axis=1,
    )
    step = 2.0 * math.pi / K
    turn_y = step * ((rows[None, :] * shifts[:, 1:2]) % K).astype(F32)
    turn_x = step * ((freq[None, :] * shifts[:, 0:1]) % K).astype(F32)
    eyr, eyi = jnp.cos(turn_y), -jnp.sin(turn_y)
    exr, exi = jnp.cos(turn_x), -jnp.sin(turn_x)
    arg_y = own_focus[:, None] * square(rows)[None, :] + PHASE_OFFSET
    arg_x = own_focus[:, None] * square(freq)[None, :]
    say, cay = -jnp.sin(arg_y), -jnp.cos(arg_y)
    cbx, sbx = jnp.cos(arg_x), jnp.sin(arg_x)
    u = jnp.stack([say * eyr, say * eyi, cay * eyr, cay * eyi], axis=-1)
    v1r, v1i, v2r, v2i = cbx * exr, cbx * exi, sbx * exr, sbx * exi
    v = jnp.stack(
        [
            jnp.concatenate([v1r, v1i], 1),
            jnp.concatenate([-v1i, v1r], 1),
            jnp.concatenate([v2r, v2i], 1),
            jnp.concatenate([-v2i, v2r], 1),
        ],
        axis=1,
    )
    uh, um, ul = split3(u)
    vh, vm, vl = split3(v)
    zu = jnp.zeros(u.shape[:2] + (8,), F32)
    zv = jnp.zeros((v.shape[0], 8, v.shape[2]), F32)
    uu = jnp.concatenate([uh, uh, um, uh, ul, um, zu], axis=2).astype(BF)
    vv = jnp.concatenate([vh, vm, vh, vl, vh, vm, zv], axis=1).astype(BF)

    ends = jnp.cumsum(run_counts, axis=1)
    slab = jnp.sum((freq[None, :, None] >= ends[:, None, :]).astype(jnp.int32), axis=2)
    inner = dest_map[classes]
    code = (
        (defocus_class[:, None] << 8) + slab * 32 + (freq % 2 * 16)[None, :] + inner
    )
    code = code.reshape(PP, NB, CH * PAIRS, 2).transpose(1, 2, 3, 0).reshape(NB, CH * PAIRS, 16)
    code = jnp.tile(code, (1, 1, 8))
    codes = jnp.concatenate([code, jnp.zeros((NB, 16 - CH * PAIRS, 128), jnp.int32)], axis=1)

    own_rows = lax.axis_index("batch") * KYB + jnp.arange(KYB, dtype=jnp.int32)
    arg2_y = 2.0 * (defocus[None, :] * square(own_rows)[:, None] + PHASE_OFFSET)
    arg2_x = 2.0 * (defocus[:, None] * square(freq)[None, :])
    tw = jnp.concatenate(
        [
            -0.5 * jnp.cos(arg2_y),
            0.5 * jnp.sin(arg2_y),
            jnp.full((KYB, NDEF), 0.5, F32),
            jnp.zeros((KYB, 128 - 3 * NDEF), F32),
        ],
        axis=1,
    )
    tw = jnp.broadcast_to(tw[:, None, :], (KYB, PL, 128)).reshape(KYB * PL, 128)
    rw = jnp.concatenate(
        [
            jnp.cos(arg2_x),
            jnp.sin(arg2_x),
            jnp.ones((NDEF, K), F32),
            jnp.zeros((128 - 3 * NDEF, K), F32),
        ],
        axis=0,
    )

    vmem = pl.BlockSpec(memory_space=pltpu.VMEM)
    dma = pltpu.SemaphoreType.DMA
    out = pl.pallas_call(
        kernel,
        out_shape=jax.ShapeDtypeStruct((KYB * PL, 2 * K), BF),
        in_specs=[vmem] * 9,
        out_specs=vmem,
        scratch_shapes=[
            pltpu.VMEM((6, NB * KYC * PP, 128), F32),
            pltpu.VMEM((CH, 32, KYC * PP, K), BF),
            pltpu.VMEM((CH, 32, KYC * PP, K), BF),
            pltpu.VMEM((32 * 16, 128), jnp.int32),
            pltpu.VMEM((CH, NS, KYC * PL, K), BF),
            pltpu.VMEM((CH, NS, KYC * PL, K), BF),
            pltpu.VMEM((NS, KYB * PL, 128), BF),
            pltpu.VMEM((NS // 2, KYB * PL, 128), BF),
            pltpu.VMEM((KYB * PL, K), F32),
            dma, dma, dma((CH,)), dma((CH,)), dma((CH,)), dma((CH,)), dma, dma,
        ],
        compiler_params=pltpu.CompilerParams(
            collective_id=0, has_side_effects=True, vmem_limit_bytes=60 * 1024 * 1024
        ),
    )(
        images, jnp.asarray(left), jnp.asarray(right), uu, vv, codes, tw, rw,
        ref.reshape(KYB * PL, 2 * K),
    )
    return out.reshape(KYB, PL, 2 * K)


def solution(mesh):
    placed = (
        P(("batch", "slab"), None, None),
        P(("batch", "slab")),
        P(("batch", "slab"), None),
        P(("batch", "slab")),
        P(),
        P(("batch", "slab"), None),
        P(),
        P("batch", "slab", None),
    )
    return jax.shard_map(
        per_device, mesh=mesh, in_specs=placed, out_specs=P("batch", "slab", None), check_vma=False
    )
```

```python
import functools
import math

import jax
import jax.numpy as jnp
import ml_dtypes
import numpy as np
from jax import lax
from jax.experimental import pallas as pl
from jax.experimental.pallas import tpu as pltpu
from jax.sharding import PartitionSpec as P

TAU_PRIOR = 4.0
PHASE_OFFSET = 0.1
MESH = pl.DeviceIdType.MESH

K = 384
NB = 16
NS = 8
PP = 8
KYB = K // NB
CH = 6
KYC = KYB // CH
PAIRS = KYC // 2
ROWS = NB * KYC
BLK = KYC * PP
PL = 16
NDEF = 16
BF = jnp.bfloat16
F32 = jnp.float32
TURNS = (
    (0, 1), (1, 0), (0, 3), (3, 0), (1, 1), (1, 3), (3, 3), (3, 1),
    (1, 2), (2, 1), (3, 2), (2, 3), (0, 2), (2, 0), (2, 2),
)


def chunk_rows():
    rows = [
        KYB * b + KYC * c + i for c in range(CH) for b in range(NB) for i in range(KYC)
    ]
    return np.array(rows, np.int32).reshape(CH, NB * KYC)


def tables():
    index = np.arange(K)
    angle = 2.0 * np.pi / K * ((index[:, None] * index[None, :]) % K)
    cosine = (np.cos(angle) / math.sqrt(K)).astype(np.float32)
    sine = (np.sin(angle) / math.sqrt(K)).astype(np.float32)
    rows = chunk_rows()
    left = np.stack(
        [np.concatenate([cosine[r], -sine[r]], axis=0) for r in rows], axis=0
    ).astype(ml_dtypes.bfloat16)
    right = np.concatenate(
        [np.concatenate([cosine, -sine], 1), np.concatenate([sine, cosine], 1)], 0
    ).astype(ml_dtypes.bfloat16)
    return left, right


def kernel(
    img, left, right, u1r, u1i, u2r, u2i, v1r, v1i, v2r, v2i, code, tw, rw, ref,
    out,
    ub, vb, uu, secs, scr, cscr, codes, sendb, recvb, crecv, zsend, zrecv, nsend, nrecv, wts,
    code_s, code_r, row_s, row_r, z_s, z_r, n_s, n_r,
):
    mb = lax.axis_index("batch")
    ms = lax.axis_index("slab")
    core = lax.rem(ms, 2)
    zbase = ms - core
    mz = ms // 2
    me = mb * 2 + core
    my = mb // 4
    mx = lax.rem(mb, 4)

    def peer_of(turn):
        dy, dx = turn
        py = lax.rem(my + jnp.where(core == 0, dy, dx), 4)
        px = lax.rem(mx + jnp.where(core == 0, dx, 4 - dy), 4)
        return py * 4 + px

    barrier = pltpu.get_barrier_semaphore()

    def greet_plane(q, carry):
        i = lax.rem(me + q, 32)
        pl.semaphore_signal(
            barrier, inc=1, device_id=(i // 2, zbase + lax.rem(i, 2)), device_id_type=MESH
        )
        return carry

    def greet_slab(q, carry):
        pl.semaphore_signal(
            barrier, inc=1, device_id=(mb, lax.rem(ms + q, NS)), device_id_type=MESH
        )
        return carry

    lax.fori_loop(1, 32, greet_plane, 0)
    lax.fori_loop(1, NS, greet_slab, 0)

    def parts(x):
        high = x.astype(BF).astype(F32)
        return high, x - high

    zero = jnp.zeros((PP, K), F32)
    for k, x in enumerate((u1r, u1i, u2r, u2i)):
        high, rest = parts(x[...])
        ub[:, k, :] = high
        ub[:, 4 + k, :] = high
        ub[:, 8 + k, :] = rest
        ub[:, 12 + k, :] = zero
    plus = {n: parts(x[...]) for n, x in (("1r", v1r), ("1i", v1i), ("2r", v2r), ("2i", v2i))}
    sides = ((("1r", 1), ("1i", 1)), (("1i", -1), ("1r", 1)), (("2r", 1), ("2i", 1)), (("2i", -1), ("2r", 1)))
    for k, both in enumerate(sides):
        for h, (name, sign) in enumerate(both):
            high, rest = plus[name]
            cols = pl.ds(h * K, K)
            vb[:, k, cols] = high * sign
            vb[:, 4 + k, cols] = rest * sign
            vb[:, 8 + k, cols] = high * sign
            vb[:, 12 + k, cols] = zero
    for p in range(PP):
        uu[p] = ub[p].T.astype(BF)

    def compute(c):
        lc = left[c]

        def one_left(p, carry):
            sec = jnp.dot(lc, img[p], preferred_element_type=F32).astype(BF)
            start = pl.multiple_of(p * ROWS, ROWS)
            secs[pl.ds(start, ROWS), pl.ds(0, K)] = sec[:ROWS]
            secs[pl.ds(start, ROWS), pl.ds(K, K)] = sec[ROWS:]
            return carry

        lax.fori_loop(0, PP, one_left, 0, unroll=2)

        def four(t, carry):
            start = pl.multiple_of(t * 4 * ROWS, 4 * ROWS)
            spec = jnp.dot(
                secs[pl.ds(start, 4 * ROWS), :], right[...], preferred_element_type=F32
            )
            for j in range(4):
                p = t * 4 + j
                factor = jnp.dot(
                    uu[p, pl.ds(pl.multiple_of(c * ROWS, ROWS), ROWS), :],
                    vb[p].astype(BF),
                    preferred_element_type=F32,
                )
                rows = slice(j * ROWS, (j + 1) * ROWS)
                sr, si = spec[rows, :K], spec[rows, K:]
                fr, fi = factor[:, :K], factor[:, K:]
                wr = sr * fr - si * fi
                wi = sr * fi + si * fr
                for g in range(3):
                    cols = slice(g * 128, (g + 1) * 128)
                    scr[g, pl.ds(p, ROWS, stride=8), :] = wr[:, cols]
                    scr[3 + g, pl.ds(p, ROWS, stride=8), :] = wi[:, cols]
            return carry

        lax.fori_loop(0, PP // 4, four, 0)

        def pack(b, carry):
            start = pl.multiple_of(b * BLK, BLK)
            for h in range(2):
                for g in range(3):
                    sendb[c, b * 2 + h, :, pl.ds(g * 128, 128)] = scr[
                        3 * h + g, pl.ds(start, BLK), :
                    ].astype(BF)
            return carry

        lax.fori_loop(0, NB, pack, 0)

    def to_plane(b, h, src, dst, send_sem, recv_sem):
        pltpu.make_async_remote_copy(
            src_ref=src, dst_ref=dst, send_sem=send_sem, recv_sem=recv_sem,
            device_id=(b, zbase + h), device_id_type=MESH,
        ).start()

    def send_rows(c):
        other = 1 - core
        to_plane(mb, other, sendb.at[c, mb * 2 + other], recvb.at[c, me], row_s.at[c], row_r.at[c])
        pltpu.make_async_copy(sendb.at[c, me], recvb.at[c, me], row_r.at[c]).start()
        for flip in range(2):
            h = core if flip == 0 else other
            for turn in TURNS:
                b = peer_of(turn)
                to_plane(b, h, sendb.at[c, b * 2 + h], recvb.at[c, me], row_s.at[c], row_r.at[c])

    compute(0)

    row8 = lax.broadcasted_iota(jnp.int32, (PP, 128), 0)
    lane8 = lax.broadcasted_iota(jnp.int32, (PP, 128), 1)
    spread = jnp.where(lax.rem(lane8, PP) == row8, 1.0, 0.0)
    raw = code[...]

    def turned(x):
        return lax.dot_general(
            x.astype(F32), spread, (((0,), (0,)), ((), ())),
            precision=lax.Precision.HIGHEST, preferred_element_type=F32,
        ).astype(jnp.int32)

    cscr[...] = turned(raw & 255) + (turned(raw >> 8) << 8)
    even_lane = lax.rem(lax.broadcasted_iota(jnp.int32, (12, 128), 1) // PP, 2) == 0

    def arrange(b, carry):
        codes[b, pl.ds(0, 12), :] = jnp.where(
            even_lane,
            cscr[pl.ds(b * KYB, 12, stride=2), :],
            cscr[pl.ds(b * KYB + 1, 12, stride=2), :],
        )
        codes[b, pl.ds(12, 4), :] = jnp.zeros((4, 128), jnp.int32)
        return carry

    lax.fori_loop(0, NB, arrange, 0)

    pl.semaphore_wait(barrier, 31 + NS - 1)

    def send_codes(q, carry):
        i = lax.rem(me + q, 32)
        to_plane(
            i // 2, lax.rem(i, 2), codes.at[i // 2],
            crecv.at[pl.ds(pl.multiple_of(me * 16, 16), 16), :], code_s, code_r,
        )
        return carry

    send_rows(0)
    pltpu.make_async_copy(
        codes.at[mb], crecv.at[pl.ds(pl.multiple_of(me * 16, 16), 16), :], code_r
    ).start()
    lax.fori_loop(1, 32, send_codes, 0)

    def produce(c, carry):
        compute(c)
        send_rows(c)
        return carry

    lax.fori_loop(1, CH, produce, 0)

    pltpu.make_async_copy(crecv, crecv, code_r).wait()

    lane = lax.broadcasted_iota(jnp.int32, (32, 128), 1)
    sub = lax.broadcasted_iota(jnp.int32, (32, 128), 0)
    mine = (lane // 16) == lax.rem(sub, 8)

    def pair_codes(pair):
        got = crecv[pl.ds(pair, 32, stride=16), :]
        return jnp.sum(jnp.where(mine, got, 0).reshape(4, 8, 128), axis=1)

    spot = lax.broadcasted_iota(jnp.int32, (256, 128), 0)

    def one_hot(code4):
        place = code4 & 255
        return jnp.concatenate(
            [
                jnp.where(spot == place[g : g + 1, :], 1.0, 0.0).astype(BF)
                for g in range(4)
            ],
            axis=1,
        )

    row_id = lax.broadcasted_iota(jnp.int32, (128, 128), 0)
    row_class = jnp.where(row_id < 3 * NDEF, lax.rem(row_id, NDEF), -1)

    def count(pair, carry):
        code4 = pair_codes(pair)
        kind = code4 >> 8
        kinds = jnp.concatenate(
            [
                jnp.where(row_class == kind[g : g + 1, :], 1.0, 0.0).astype(BF)
                for g in range(4)
            ],
            axis=1,
        )
        tally = lax.dot_general(
            one_hot(code4), kinds, (((1,), (1,)), ((), ())), preferred_element_type=F32
        )
        start = pl.multiple_of(pair * 32, 32)
        nsend[:, pl.ds(start, 32), :] = tally.astype(BF).reshape(NS, 32, 128)
        return carry

    lax.fori_loop(0, CH * PAIRS, count, 0)

    pltpu.make_async_copy(nsend.at[ms], nrecv.at[mz], n_r).start()

    def send_counts(q, carry):
        peer = lax.rem(ms + 2 * q, NS)
        pltpu.make_async_remote_copy(
            src_ref=nsend.at[peer], dst_ref=nrecv.at[mz], send_sem=n_s, recv_sem=n_r,
            device_id=(mb, peer), device_id_type=MESH,
        ).start()
        return carry

    lax.fori_loop(1, NS // 2, send_counts, 0)

    def scatter(c, carry):
        pltpu.make_async_copy(recvb.at[c], recvb.at[c], row_r.at[c]).wait()

        def one(j, inner):
            pair = c * PAIRS + j
            start = pl.multiple_of(j * 16, 16)
            rows = recvb[c, :, pl.ds(start, 16), :].reshape(512, K)
            hot = one_hot(pair_codes(pair))
            part = jnp.dot(hot, rows, preferred_element_type=F32)
            zsend[pair] = part.astype(BF).reshape(NS, 32, K)
            for q in range(1, NS):
                peer = lax.rem(ms + q, NS)
                pltpu.make_async_remote_copy(
                    src_ref=zsend.at[pair, peer], dst_ref=zrecv.at[pair, ms],
                    send_sem=z_s.at[pair], recv_sem=z_r.at[pair],
                    device_id=(mb, peer), device_id_type=MESH,
                ).start()
            pltpu.make_async_copy(zsend.at[pair, ms], zrecv.at[pair, ms], z_r.at[pair]).start()
            return inner

        lax.fori_loop(0, PAIRS, one, 0)
        return carry

    lax.fori_loop(0, CH, scatter, 0)

    pltpu.make_async_copy(nrecv, nrecv, n_r).wait()
    totals = (
        nrecv[0].astype(F32) + nrecv[1].astype(F32) + nrecv[2].astype(F32) + nrecv[3].astype(F32)
    )
    scaled = (totals.reshape(KYB, PL, 128) * tw[...][:, None, :]).reshape(KYB * PL, 128)
    wts[...] = (
        jnp.dot(scaled, rw[...], precision=lax.Precision.HIGHEST, preferred_element_type=F32)
        + TAU_PRIOR
    )

    def finish(pair, carry):
        pltpu.make_async_copy(zrecv.at[pair], zrecv.at[pair], z_r.at[pair]).wait()
        start = pl.multiple_of(pair * 32, 32)
        inverse = 1.0 / wts[pl.ds(start, 32), :]
        for h in range(2):
            total = TAU_PRIOR * ref[pl.ds(start, 32), pl.ds(h * K, K)].astype(F32)
            for z in range(NS // 2):
                total += zrecv[pair, 2 * z + h].astype(F32)
            out[pl.ds(start, 32), pl.ds(h * K, K)] = (total * inverse).astype(BF)
        return carry

    lax.fori_loop(0, CH * PAIRS, finish, 0)

    def drain(src, dst, send_sem, recv_sem):
        pltpu.make_async_remote_copy(
            src_ref=src, dst_ref=dst, send_sem=send_sem, recv_sem=recv_sem,
            device_id=(mb, ms), device_id_type=MESH,
        ).wait_send()

    drain(crecv.at[pl.ds(0, 31 * 16), :], crecv.at[pl.ds(0, 31 * 16), :], code_s, code_r)
    drain(nsend.at[pl.ds(0, 3)], nsend.at[pl.ds(0, 3)], n_s, n_r)

    def drain_rows(c, carry):
        drain(sendb.at[c, pl.ds(0, 31)], recvb.at[c, pl.ds(0, 31)], row_s.at[c], row_r.at[c])
        return carry

    def drain_sums(pair, carry):
        drain(zsend.at[pair, pl.ds(0, 7)], zrecv.at[pair, pl.ds(0, 7)], z_s.at[pair], z_r.at[pair])
        return carry

    lax.fori_loop(0, CH, drain_rows, 0)
    lax.fori_loop(0, CH * PAIRS, drain_sums, 0)


def per_device(images, classes, shifts, defocus_class, defocus, run_counts, dest_map, ref):
    left, right = tables()
    order = chunk_rows().reshape(-1)
    freq = np.arange(K)

    def square(k):
        half = ((k + K // 2) % K - K // 2).astype(np.float32) / np.float32(K)
        return half * half

    own_focus = jnp.sum(
        jnp.where(defocus_class[:, None] == jnp.arange(NDEF)[None, :], defocus[None, :], 0.0),
        axis=1,
    )
    step = 2.0 * math.pi / K
    turn_y = step * ((jnp.asarray(order, jnp.int32)[None, :] * shifts[:, 1:2]) % K).astype(F32)
    turn_x = step * ((jnp.asarray(freq, jnp.int32)[None, :] * shifts[:, 0:1]) % K).astype(F32)
    eyr, eyi = jnp.cos(turn_y), -jnp.sin(turn_y)
    exr, exi = jnp.cos(turn_x), -jnp.sin(turn_x)
    arg_y = own_focus[:, None] * jnp.asarray(square(order))[None, :] + PHASE_OFFSET
    arg_x = own_focus[:, None] * jnp.asarray(square(freq))[None, :]
    say, cay = -jnp.sin(arg_y), -jnp.cos(arg_y)
    cbx, sbx = jnp.cos(arg_x), jnp.sin(arg_x)
    factors = (
        say * eyr, say * eyi, cay * eyr, cay * eyi,
        cbx * exr, cbx * exi, sbx * exr, sbx * exi,
    )

    freq = jnp.arange(K, dtype=jnp.int32)
    ends = jnp.cumsum(run_counts, axis=1)
    slab = jnp.sum((freq[None, :, None] >= ends[:, None, :]).astype(jnp.int32), axis=2)
    code = (
        (defocus_class[:, None] << 8) + slab * 32 + (freq % 2 * 16)[None, :] + dest_map[classes]
    )

    def by_class(lane_of, arg, scale_cos):
        group = lane_of // NDEF
        return jnp.where(
            group == 0,
            scale_cos[0] * jnp.cos(arg),
            jnp.where(
                group == 1, scale_cos[1] * jnp.sin(arg), jnp.where(group == 2, scale_cos[2], 0.0)
            ),
        )

    many = jnp.tile(defocus, 128 // NDEF)
    own_rows = lax.axis_index("batch") * KYB + jnp.arange(KYB, dtype=jnp.int32)
    own_half = ((own_rows + K // 2) % K - K // 2).astype(F32) / K
    arg2_y = 2.0 * (many[None, :] * (own_half * own_half)[:, None] + PHASE_OFFSET)
    arg2_x = 2.0 * (many[:, None] * jnp.asarray(square(np.arange(K)))[None, :])
    lanes = jnp.arange(128, dtype=jnp.int32)
    tw = by_class(lanes[None, :], arg2_y, (-0.5, 0.5, 0.5))
    rw = by_class(lanes[:, None], arg2_x, (1.0, 1.0, 1.0))

    vmem = pl.BlockSpec(memory_space=pltpu.VMEM)
    dma = pltpu.SemaphoreType.DMA
    pairs = CH * PAIRS
    out = pl.pallas_call(
        kernel,
        out_shape=jax.ShapeDtypeStruct((KYB * PL, 2 * K), BF),
        in_specs=[vmem] * 15,
        out_specs=vmem,
        scratch_shapes=[
            pltpu.VMEM((PP, 16, K), F32),
            pltpu.VMEM((PP, 16, 2 * K), F32),
            pltpu.VMEM((PP, K, 16), BF),
            pltpu.VMEM((PP * ROWS, 2 * K), BF),
            pltpu.VMEM((6, PP * ROWS, 128), F32),
            pltpu.VMEM((K, 128), jnp.int32),
            pltpu.VMEM((NB, 16, 128), jnp.int32),
            pltpu.VMEM((CH, 32, BLK, K), BF),
            pltpu.VMEM((CH, 32, BLK, K), BF),
            pltpu.VMEM((32 * 16, 128), jnp.int32),
            pltpu.VMEM((pairs, NS, 2 * PL, K), BF),
            pltpu.VMEM((pairs, NS, 2 * PL, K), BF),
            pltpu.VMEM((NS, KYB * PL, 128), BF),
            pltpu.VMEM((NS // 2, KYB * PL, 128), BF),
            pltpu.VMEM((KYB * PL, K), F32),
            dma, dma, dma((CH,)), dma((CH,)), dma((pairs,)), dma((pairs,)), dma, dma,
        ],
        compiler_params=pltpu.CompilerParams(
            collective_id=0, has_side_effects=True, vmem_limit_bytes=60 * 1024 * 1024
        ),
    )(
        images, jnp.asarray(left), jnp.asarray(right), *factors, code, tw, rw,
        ref.reshape(KYB * PL, 2 * K),
    )
    return out.reshape(KYB, PL, 2 * K)


def solution(mesh):
    placed = (
        P(("batch", "slab"), None, None),
        P(("batch", "slab")),
        P(("batch", "slab"), None),
        P(("batch", "slab")),
        P(),
        P(("batch", "slab"), None),
        P(),
        P("batch", "slab", None),
    )
    return jax.shard_map(
        per_device, mesh=mesh, in_specs=placed, out_specs=P("batch", "slab", None), check_vma=False
    )
```

```python
import math

import jax
import jax.numpy as jnp
import ml_dtypes
import numpy as np
from jax import lax
from jax.experimental import pallas as pl
from jax.experimental.pallas import tpu as pltpu
from jax.sharding import PartitionSpec as P

TAU_PRIOR = 4.0
PHASE_OFFSET = 0.1
MESH = pl.DeviceIdType.MESH

K = 384
NB = 16
NS = 8
PP = 8
KYB = K // NB
CH = 6
KYC = KYB // CH
PAIRS = KYC // 2
ROWS = NB * KYC
BLK = KYC * PP
PL = 16
NDEF = 16
BF = jnp.bfloat16
F32 = jnp.float32
TURNS = (
    (0, 1), (1, 0), (0, 3), (3, 0), (1, 1), (1, 3), (3, 3), (3, 1),
    (1, 2), (2, 1), (3, 2), (2, 3), (0, 2), (2, 0), (2, 2),
)


def chunk_rows():
    rows = [
        KYB * b + KYC * c + i for c in range(CH) for b in range(NB) for i in range(KYC)
    ]
    return np.array(rows, np.int32).reshape(CH, NB * KYC)


def tables():
    index = np.arange(K)
    angle = 2.0 * np.pi / K * ((index[:, None] * index[None, :]) % K)
    cosine = (np.cos(angle) / math.sqrt(K)).astype(np.float32)
    sine = (np.sin(angle) / math.sqrt(K)).astype(np.float32)
    rows = chunk_rows()
    left = np.stack(
        [np.concatenate([cosine[r], -sine[r]], axis=0) for r in rows], axis=0
    ).astype(ml_dtypes.bfloat16)
    right = np.concatenate(
        [np.concatenate([cosine, -sine], 1), np.concatenate([sine, cosine], 1)], 0
    ).astype(ml_dtypes.bfloat16)
    return left, right


def kernel(
    classes, kinds_in, defocus, shifts, counts, left, img_in, right_in, dest_in, ref_in,
    out,
    img, right, dest, ref, ub, vb, uu, secs, scr, cscr, codes, sendb, recvb, crecv, zsend, zrecv, nsend, nrecv, wts,
    img_m, right_m, dest_m, ref_m, code_s, code_r, row_s, row_r, z_s, z_r, n_s, n_r,
):
    mb = lax.axis_index("batch")
    ms = lax.axis_index("slab")
    core = lax.rem(ms, 2)
    zbase = ms - core
    mz = ms // 2
    me = mb * 2 + core
    my = mb // 4
    mx = lax.rem(mb, 4)

    def peer_of(turn):
        dy, dx = turn
        py = lax.rem(my + jnp.where(core == 0, dy, dx), 4)
        px = lax.rem(mx + jnp.where(core == 0, dx, 4 - dy), 4)
        return py * 4 + px

    barrier = pltpu.get_barrier_semaphore()
    loads = [pltpu.make_async_copy(img_in.at[p], img.at[p], img_m.at[p]) for p in range(PP)]
    load_right = pltpu.make_async_copy(right_in, right, right_m)
    load_dest = pltpu.make_async_copy(dest_in, dest, dest_m)
    load_ref = pltpu.make_async_copy(ref_in, ref, ref_m)
    for load in (*loads, load_right, load_dest, load_ref):
        load.start()

    def greet_plane(q, carry):
        i = lax.rem(me + q, 32)
        pl.semaphore_signal(
            barrier, inc=1, device_id=(i // 2, zbase + lax.rem(i, 2)), device_id_type=MESH
        )
        return carry

    def greet_slab(q, carry):
        pl.semaphore_signal(
            barrier, inc=1, device_id=(mb, lax.rem(ms + q, NS)), device_id_type=MESH
        )
        return carry

    lax.fori_loop(1, 32, greet_plane, 0)
    lax.fori_loop(1, NS, greet_slab, 0)

    def parts(x):
        high = x.astype(BF).astype(F32)
        return high, x - high

    sub_p = lax.broadcasted_iota(jnp.int32, (PP, K), 0)
    col = lax.broadcasted_iota(jnp.int32, (PP, K), 1)
    order = ((col // KYC) & (NB - 1)) * KYB + (col // ROWS) * KYC + (col & (KYC - 1))

    def pick(index, values):
        got = jnp.full(index.shape, values[0])
        for i, value in enumerate(values[1:], 1):
            got = jnp.where(index == i, value, got)
        return got

    def square(k):
        half = jnp.where(k >= K // 2, k - K, k).astype(F32) * (1.0 / K)
        return half * half

    def wave(k, shift):
        turn = (k * shift).astype(F32)
        turn = turn - K * jnp.floor((turn + 0.5) * (1.0 / K))
        angle = turn * (2.0 * math.pi / K)
        return jnp.cos(angle), -jnp.sin(angle)

    eyr, eyi = wave(order, pick(sub_p, [shifts[1, p] for p in range(PP)]))
    exr, exi = wave(col, pick(sub_p, [shifts[0, p] for p in range(PP)]))
    focus = pick(sub_p, [defocus[kinds_in[p]] for p in range(PP)])
    arg_y = focus * square(order) + PHASE_OFFSET
    arg_x = focus * square(col)
    say, cay = -jnp.sin(arg_y), -jnp.cos(arg_y)
    cbx, sbx = jnp.cos(arg_x), jnp.sin(arg_x)

    zero = jnp.zeros((PP, K), F32)
    for k, x in enumerate((say * eyr, say * eyi, cay * eyr, cay * eyi)):
        high, rest = parts(x)
        ub[:, k, :] = high
        ub[:, 4 + k, :] = high
        ub[:, 8 + k, :] = rest
        ub[:, 12 + k, :] = zero
    side = [parts(x) for x in (cbx * exr, cbx * exi, sbx * exr, sbx * exi)]
    sides = (((0, 1), (1, 1)), ((1, -1), (0, 1)), ((2, 1), (3, 1)), ((3, -1), (2, 1)))
    for k, both in enumerate(sides):
        for h, (name, sign) in enumerate(both):
            high, rest = side[name]
            cols = pl.ds(h * K, K)
            vb[:, k, cols] = high * sign
            vb[:, 4 + k, cols] = rest * sign
            vb[:, 8 + k, cols] = high * sign
            vb[:, 12 + k, cols] = zero
    for p in range(PP):
        uu[p] = ub[p].T.astype(BF)

    def compute(c, first=False):
        lc = left[c]

        def one_left(p, carry):
            if first:
                pltpu.make_async_copy(img_in.at[p], img.at[p], img_m.at[p]).wait()
            sec = jnp.dot(lc, img[p], preferred_element_type=F32).astype(BF)
            start = pl.multiple_of(p * ROWS, ROWS)
            secs[pl.ds(start, ROWS), pl.ds(0, K)] = sec[:ROWS]
            secs[pl.ds(start, ROWS), pl.ds(K, K)] = sec[ROWS:]
            return carry

        lax.fori_loop(0, PP, one_left, 0, unroll=2)
        if first:
            load_right.wait()

        def four(t, carry):
            start = pl.multiple_of(t * 4 * ROWS, 4 * ROWS)
            spec = jnp.dot(
                secs[pl.ds(start, 4 * ROWS), :], right[...], preferred_element_type=F32
            )
            for j in range(4):
                p = t * 4 + j
                factor = jnp.dot(
                    uu[p, pl.ds(pl.multiple_of(c * ROWS, ROWS), ROWS), :],
                    vb[p].astype(BF),
                    preferred_element_type=F32,
                )
                rows = slice(j * ROWS, (j + 1) * ROWS)
                sr, si = spec[rows, :K], spec[rows, K:]
                fr, fi = factor[:, :K], factor[:, K:]
                wr = sr * fr - si * fi
                wi = sr * fi + si * fr
                for g in range(3):
                    cols = slice(g * 128, (g + 1) * 128)
                    scr[g, pl.ds(p, ROWS, stride=8), :] = wr[:, cols]
                    scr[3 + g, pl.ds(p, ROWS, stride=8), :] = wi[:, cols]
            return carry

        lax.fori_loop(0, PP // 4, four, 0)

        def pack(b, carry):
            start = pl.multiple_of(b * BLK, BLK)
            for h in range(2):
                for g in range(3):
                    sendb[c, b * 2 + h, :, pl.ds(g * 128, 128)] = scr[
                        3 * h + g, pl.ds(start, BLK), :
                    ].astype(BF)
            return carry

        lax.fori_loop(0, NB, pack, 0)

    def to_plane(b, h, src, dst, send_sem, recv_sem):
        pltpu.make_async_remote_copy(
            src_ref=src, dst_ref=dst, send_sem=send_sem, recv_sem=recv_sem,
            device_id=(b, zbase + h), device_id_type=MESH,
        ).start()

    def send_rows(c):
        other = 1 - core
        to_plane(mb, other, sendb.at[c, mb * 2 + other], recvb.at[c, me], row_s.at[c], row_r.at[c])
        pltpu.make_async_copy(sendb.at[c, me], recvb.at[c, me], row_r.at[c]).start()
        for flip in range(2):
            h = core if flip == 0 else other
            for turn in TURNS:
                b = peer_of(turn)
                to_plane(b, h, sendb.at[c, b * 2 + h], recvb.at[c, me], row_s.at[c], row_r.at[c])

    compute(0, first=True)

    pl.semaphore_wait(barrier, 31 + NS - 1)

    def send_codes(q, carry):
        i = lax.rem(me + q, 32)
        to_plane(
            i // 2, lax.rem(i, 2), codes.at[i // 2],
            crecv.at[pl.ds(pl.multiple_of(me * 16, 16), 16), :], code_s, code_r,
        )
        return carry

    send_rows(0)
    row8 = lax.broadcasted_iota(jnp.int32, (PP, 128), 0)
    lane8 = lax.broadcasted_iota(jnp.int32, (PP, 128), 1)
    spread = jnp.where(lax.rem(lane8, PP) == row8, 1.0, 0.0)
    load_dest.wait()
    end = counts[:, 0:1]
    slab = jnp.zeros((PP, K), jnp.int32)
    for i in range(1, NS):
        slab = slab + jnp.where(col >= end, 1, 0)
        end = end + counts[:, i : i + 1]
    plane = pick(sub_p, [dest[pl.ds(classes[p], 1), :] for p in range(PP)])
    place = slab * 32 + (col & 1) * PL + plane
    kind_p = pick(sub_p, [kinds_in[p] for p in range(PP)])

    def turned(x):
        return lax.dot_general(
            x.astype(F32), spread, (((0,), (0,)), ((), ())),
            precision=lax.Precision.HIGHEST, preferred_element_type=F32,
        ).astype(jnp.int32)

    cscr[...] = turned(place) + (turned(kind_p) << 8)
    even_lane = lax.rem(lax.broadcasted_iota(jnp.int32, (12, 128), 1) // PP, 2) == 0

    def arrange(b, carry):
        codes[b, pl.ds(0, 12), :] = jnp.where(
            even_lane,
            cscr[pl.ds(b * KYB, 12, stride=2), :],
            cscr[pl.ds(b * KYB + 1, 12, stride=2), :],
        )
        codes[b, pl.ds(12, 4), :] = jnp.zeros((4, 128), jnp.int32)
        return carry

    lax.fori_loop(0, NB, arrange, 0)

    pltpu.make_async_copy(
        codes.at[mb], crecv.at[pl.ds(pl.multiple_of(me * 16, 16), 16), :], code_r
    ).start()
    lax.fori_loop(1, 32, send_codes, 0)

    def produce(c, carry):
        compute(c)
        send_rows(c)
        return carry

    lax.fori_loop(1, CH, produce, 0)

    pltpu.make_async_copy(crecv, crecv, code_r).wait()

    lane = lax.broadcasted_iota(jnp.int32, (32, 128), 1)
    sub = lax.broadcasted_iota(jnp.int32, (32, 128), 0)
    mine = (lane // 16) == lax.rem(sub, 8)

    def pair_codes(pair):
        got = crecv[pl.ds(pair, 32, stride=16), :]
        return jnp.sum(jnp.where(mine, got, 0).reshape(4, 8, 128), axis=1)

    spot = lax.broadcasted_iota(jnp.int32, (256, 128), 0)

    def one_hot(code4):
        place = code4 & 255
        return jnp.concatenate(
            [
                jnp.where(spot == place[g : g + 1, :], 1.0, 0.0).astype(BF)
                for g in range(4)
            ],
            axis=1,
        )

    row_id = lax.broadcasted_iota(jnp.int32, (128, 128), 0)
    row_class = jnp.where(row_id < 3 * NDEF, lax.rem(row_id, NDEF), -1)

    def count(pair, carry):
        code4 = pair_codes(pair)
        kind = code4 >> 8
        kinds = jnp.concatenate(
            [
                jnp.where(row_class == kind[g : g + 1, :], 1.0, 0.0).astype(BF)
                for g in range(4)
            ],
            axis=1,
        )
        tally = lax.dot_general(
            one_hot(code4), kinds, (((1,), (1,)), ((), ())), preferred_element_type=F32
        )
        start = pl.multiple_of(pair * 32, 32)
        nsend[:, pl.ds(start, 32), :] = tally.astype(BF).reshape(NS, 32, 128)
        return carry

    lax.fori_loop(0, CH * PAIRS, count, 0)

    pltpu.make_async_copy(nsend.at[ms], nrecv.at[mz], n_r).start()

    def send_counts(q, carry):
        peer = lax.rem(ms + 2 * q, NS)
        pltpu.make_async_remote_copy(
            src_ref=nsend.at[peer], dst_ref=nrecv.at[mz], send_sem=n_s, recv_sem=n_r,
            device_id=(mb, peer), device_id_type=MESH,
        ).start()
        return carry

    lax.fori_loop(1, NS // 2, send_counts, 0)

    lane_k = lax.broadcasted_iota(jnp.int32, (KYB, 128), 1)
    own_ky = mb * KYB + lax.broadcasted_iota(jnp.int32, (KYB, 128), 0)
    every = [defocus[i] for i in range(NDEF)]
    arg2_y = 2.0 * (pick(lane_k & (NDEF - 1), every) * square(own_ky) + PHASE_OFFSET)
    group = lane_k // NDEF
    tw = jnp.where(
        group == 0,
        -0.5 * jnp.cos(arg2_y),
        jnp.where(group == 1, 0.5 * jnp.sin(arg2_y), jnp.where(group == 2, 0.5, 0.0)),
    )
    row_k = lax.broadcasted_iota(jnp.int32, (NDEF, K), 0)
    col_k = lax.broadcasted_iota(jnp.int32, (NDEF, K), 1)
    arg2_x = 2.0 * (pick(row_k, every) * square(col_k))
    rw = jnp.concatenate(
        [
            jnp.cos(arg2_x),
            jnp.sin(arg2_x),
            jnp.ones((NDEF, K), F32),
            jnp.zeros((128 - 3 * NDEF, K), F32),
        ],
        axis=0,
    )

    def scatter(c, carry):
        pltpu.make_async_copy(recvb.at[c], recvb.at[c], row_r.at[c]).wait()

        def one(j, inner):
            pair = c * PAIRS + j
            start = pl.multiple_of(j * 16, 16)
            rows = recvb[c, :, pl.ds(start, 16), :].reshape(512, K)
            hot = one_hot(pair_codes(pair))
            part = jnp.dot(hot, rows, preferred_element_type=F32)
            zsend[pair] = part.astype(BF).reshape(NS, 32, K)
            for q in range(1, NS):
                peer = lax.rem(ms + q, NS)
                pltpu.make_async_remote_copy(
                    src_ref=zsend.at[pair, peer], dst_ref=zrecv.at[pair, ms],
                    send_sem=z_s.at[pair], recv_sem=z_r.at[pair],
                    device_id=(mb, peer), device_id_type=MESH,
                ).start()
            pltpu.make_async_copy(zsend.at[pair, ms], zrecv.at[pair, ms], z_r.at[pair]).start()
            return inner

        lax.fori_loop(0, PAIRS, one, 0)
        return carry

    lax.fori_loop(0, CH, scatter, 0)

    load_ref.wait()
    pltpu.make_async_copy(nrecv, nrecv, n_r).wait()
    totals = (
        nrecv[0].astype(F32) + nrecv[1].astype(F32) + nrecv[2].astype(F32) + nrecv[3].astype(F32)
    )
    scaled = (totals.reshape(KYB, PL, 128) * tw[:, None, :]).reshape(KYB * PL, 128)
    wts[...] = (
        jnp.dot(scaled, rw, precision=lax.Precision.HIGHEST, preferred_element_type=F32)
        + TAU_PRIOR
    )

    def finish(pair, carry):
        pltpu.make_async_copy(zrecv.at[pair], zrecv.at[pair], z_r.at[pair]).wait()
        start = pl.multiple_of(pair * 32, 32)
        inverse = 1.0 / wts[pl.ds(start, 32), :]
        for h in range(2):
            total = TAU_PRIOR * ref[pl.ds(start, 32), pl.ds(h * K, K)].astype(F32)
            for z in range(NS // 2):
                total += zrecv[pair, 2 * z + h].astype(F32)
            out[pl.ds(start, 32), pl.ds(h * K, K)] = (total * inverse).astype(BF)
        return carry

    lax.fori_loop(0, CH * PAIRS, finish, 0)

    def drain(src, dst, send_sem, recv_sem):
        pltpu.make_async_remote_copy(
            src_ref=src, dst_ref=dst, send_sem=send_sem, recv_sem=recv_sem,
            device_id=(mb, ms), device_id_type=MESH,
        ).wait_send()

    drain(crecv.at[pl.ds(0, 31 * 16), :], crecv.at[pl.ds(0, 31 * 16), :], code_s, code_r)
    drain(nsend.at[pl.ds(0, 3)], nsend.at[pl.ds(0, 3)], n_s, n_r)

    def drain_rows(c, carry):
        drain(sendb.at[c, pl.ds(0, 31)], recvb.at[c, pl.ds(0, 31)], row_s.at[c], row_r.at[c])
        return carry

    def drain_sums(pair, carry):
        drain(zsend.at[pair, pl.ds(0, 7)], zrecv.at[pair, pl.ds(0, 7)], z_s.at[pair], z_r.at[pair])
        return carry

    lax.fori_loop(0, CH, drain_rows, 0)
    lax.fori_loop(0, CH * PAIRS, drain_sums, 0)


def per_device(images, classes, shifts, defocus_class, defocus, run_counts, dest_map, ref):
    left, right = tables()
    vmem = pl.BlockSpec(memory_space=pltpu.VMEM)
    smem = pl.BlockSpec(memory_space=pltpu.SMEM)
    far = pl.BlockSpec(memory_space=pl.ANY)
    dma = pltpu.SemaphoreType.DMA
    pairs = CH * PAIRS
    out = pl.pallas_call(
        kernel,
        out_shape=jax.ShapeDtypeStruct((KYB * PL, 2 * K), BF),
        in_specs=[smem] * 4 + [vmem] * 2 + [far] * 4,
        out_specs=vmem,
        scratch_shapes=[
            pltpu.VMEM((PP, K, K), BF),
            pltpu.VMEM((2 * K, 2 * K), BF),
            pltpu.VMEM(dest_map.shape, jnp.int32),
            pltpu.VMEM((KYB * PL, 2 * K), BF),
            pltpu.VMEM((PP, 16, K), F32),
            pltpu.VMEM((PP, 16, 2 * K), F32),
            pltpu.VMEM((PP, K, 16), BF),
            pltpu.VMEM((PP * ROWS, 2 * K), BF),
            pltpu.VMEM((6, PP * ROWS, 128), F32),
            pltpu.VMEM((K, 128), jnp.int32),
            pltpu.VMEM((NB, 16, 128), jnp.int32),
            pltpu.VMEM((CH, 32, BLK, K), BF),
            pltpu.VMEM((CH, 32, BLK, K), BF),
            pltpu.VMEM((32 * 16, 128), jnp.int32),
            pltpu.VMEM((pairs, NS, 2 * PL, K), BF),
            pltpu.VMEM((pairs, NS, 2 * PL, K), BF),
            pltpu.VMEM((NS, KYB * PL, 128), BF),
            pltpu.VMEM((NS // 2, KYB * PL, 128), BF),
            pltpu.VMEM((KYB * PL, K), F32),
            dma((PP,)), dma, dma, dma, dma, dma, dma((CH,)), dma((CH,)), dma((pairs,)), dma((pairs,)), dma, dma,
        ],
        compiler_params=pltpu.CompilerParams(
            collective_id=0, has_side_effects=True, vmem_limit_bytes=60 * 1024 * 1024
        ),
    )(
        classes, defocus_class, defocus, shifts.T, run_counts, jnp.asarray(left), images,
        jnp.asarray(right), dest_map, ref.reshape(KYB * PL, 2 * K),
    )
    return out.reshape(KYB, PL, 2 * K)


def solution(mesh):
    placed = (
        P(("batch", "slab"), None, None),
        P(("batch", "slab")),
        P(("batch", "slab"), None),
        P(("batch", "slab")),
        P(),
        P(("batch", "slab"), None),
        P(),
        P("batch", "slab", None),
    )
    return jax.shard_map(
        per_device, mesh=mesh, in_specs=placed, out_specs=P("batch", "slab", None), check_vma=False
    )
```

```python
import math

import jax
import jax.numpy as jnp
import ml_dtypes
import numpy as np
from jax import lax
from jax.experimental import pallas as pl
from jax.experimental.pallas import tpu as pltpu
from jax.sharding import PartitionSpec as P

TAU_PRIOR = 4.0
PHASE_OFFSET = 0.1
MESH = pl.DeviceIdType.MESH

K = 384
NB = 16
NS = 8
PP = 8
KYB = K // NB
SHARED = 3
TILES = SHARED + 1
PL = 16
NDEF = 16
BF = jnp.bfloat16
F32 = jnp.float32
SLOTS = (
    ((1, 2), (3, 4), (11, 11), (0, 12)),
    ((5, 6), (7, 8), (9, 10), (5, 6)),
)
EXTRA = (((13, 14), (15, 16), (17, 17)), ((18, 19), (20, 21), (22, 23)))
COUNTED = tuple(SLOTS[h] + EXTRA[h] for h in range(2))
NCNT = len(COUNTED[0])
TURNS = (
    (0, 1), (1, 0), (0, 3), (3, 0), (1, 1), (1, 3), (3, 3), (3, 1),
    (1, 2), (2, 1), (3, 2), (2, 3), (0, 2), (2, 0), (2, 2),
)


def tables():
    index = np.arange(K)
    angle = 2.0 * np.pi / K * ((index[:, None] * index[None, :]) % K)
    cosine = (np.cos(angle) / math.sqrt(K)).astype(np.float32)
    sine = (np.sin(angle) / math.sqrt(K)).astype(np.float32)

    def left(t, cores):
        rows = [KYB * b + i for h in cores for b in range(NB) for i in SLOTS[h][t]]
        return np.concatenate([cosine[rows], -sine[rows]], axis=0)

    both = np.stack([left(t, (0, 1)) for t in range(SHARED)], axis=0)
    right = np.concatenate(
        [np.concatenate([cosine, -sine], 1), np.concatenate([sine, cosine], 1)], 0
    )
    kind = ml_dtypes.bfloat16
    return both.astype(kind), left(SHARED, (0,)).astype(kind), right.astype(kind)


def kernel(
    classes, kinds_in, defocus, shifts, counts, left, left_last, img_in, right_in, dest_in, ref_in,
    out,
    img, right, dest, ref, scr, cscr, cwide, codes, cf, sc, vx, pq, wp, wm,
    sendb, recvb, crecv, zsend, zrecv, zlast, zgot, nsend, nrecv, msend, mrecv, wts,
    img_m, right_m, dest_m, ref_m, code_s, code_r, row_s, row_r, z_s, z_r, n_s, n_r, m_s, m_r,
):
    mb = lax.axis_index("batch")
    ms = lax.axis_index("slab")
    core = lax.rem(ms, 2)
    zbase = ms - core
    mz = ms // 2
    me = mb * 2 + core
    my = mb // 4
    mx = lax.rem(mb, 4)

    def peer_of(turn):
        dy, dx = turn
        py = lax.rem(my + jnp.where(core == 0, dy, dx), 4)
        px = lax.rem(mx + jnp.where(core == 0, dx, 4 - dy), 4)
        return py * 4 + px

    barrier = pltpu.get_barrier_semaphore()
    loads = [pltpu.make_async_copy(img_in.at[p], img.at[p], img_m.at[p]) for p in range(PP)]
    load_right = pltpu.make_async_copy(right_in, right, right_m)
    load_dest = pltpu.make_async_copy(dest_in, dest, dest_m)
    load_ref = pltpu.make_async_copy(ref_in, ref, ref_m)
    for load in (*loads, load_dest, load_right, load_ref):
        load.start()

    def greet_plane(q, carry):
        i = lax.rem(me + q, 32)
        pl.semaphore_signal(
            barrier, inc=1, device_id=(i // 2, zbase + lax.rem(i, 2)), device_id_type=MESH
        )
        return carry

    def greet_slab(q, carry):
        pl.semaphore_signal(
            barrier, inc=1, device_id=(mb, lax.rem(ms + q, NS)), device_id_type=MESH
        )
        return carry

    lax.fori_loop(1, 32, greet_plane, 0)
    lax.fori_loop(1, NS, greet_slab, 0)

    def pick(index, values):
        got = jnp.full(index.shape, values[0])
        for i, value in enumerate(values[1:], 1):
            got = jnp.where(index == i, value, got)
        return got

    def square(k):
        half = jnp.where(k >= K // 2, k - K, k).astype(F32) * (1.0 / K)
        return half * half

    def phase(k, shift):
        turn = k.astype(F32) * shift
        turn = turn - K * jnp.floor((turn + 0.5) * (1.0 / K))
        return turn * (2.0 * math.pi / K)

    def to_plane(b, h, src, dst, send_sem, recv_sem):
        pltpu.make_async_remote_copy(
            src_ref=src, dst_ref=dst, send_sem=send_sem, recv_sem=recv_sem,
            device_id=(b, zbase + h), device_id_type=MESH,
        ).start()

    def compute(t, table, size, first=False):
        def one(p, carry):
            if first:
                pltpu.make_async_copy(img_in.at[p], img.at[p], img_m.at[p]).wait()
            sec = jnp.dot(table, img[p], preferred_element_type=F32)
            for g in range(3):
                cols = slice(g * 128, (g + 1) * 128)
                scr[g, pl.ds(p, size, stride=8), :] = sec[:size, cols]
                scr[3 + g, pl.ds(p, size, stride=8), :] = sec[size:, cols]
            return carry

        lax.fori_loop(0, PP, one, 0, unroll=2)

        def pack(i, carry):
            start = pl.multiple_of(i * 16, 16)
            target = lax.rem(i, NB) * 2 + i // NB
            for g in range(6):
                sendb[t, target, :, pl.ds(g * 128, 128)] = scr[g, pl.ds(start, 16), :].astype(BF)
            return carry

        lax.fori_loop(0, size // 2, pack, 0)

    other = 1 - core

    def send_rows(t):
        to_plane(mb, other, sendb.at[t, mb * 2 + other], recvb.at[t, me], row_s.at[t], row_r.at[t])
        pltpu.make_async_copy(sendb.at[t, me], recvb.at[t, me], row_r.at[t]).start()
        for flip in range(2):
            h = core if flip == 0 else other
            for turn in TURNS:
                b = peer_of(turn)
                to_plane(b, h, sendb.at[t, b * 2 + h], recvb.at[t, me], row_s.at[t], row_r.at[t])

    def send_last():
        t = SHARED

        @pl.when(core == 0)
        def _():
            pltpu.make_async_copy(sendb.at[t, me], recvb.at[t, me], row_r.at[t]).start()

        @pl.when(core == 1)
        def _():
            to_plane(mb, 0, sendb.at[t, mb * 2], recvb.at[t, me], row_s.at[t], row_r.at[t])

        for turn in TURNS:
            b = peer_of(turn)
            to_plane(b, 0, sendb.at[t, b * 2], recvb.at[t, me], row_s.at[t], row_r.at[t])

    compute(0, left[0], 64, first=True)
    pl.semaphore_wait(barrier, 31 + NS - 1)
    send_rows(0)

    load_dest.wait()
    sub_p = lax.broadcasted_iota(jnp.int32, (PP, K), 0)
    col = lax.broadcasted_iota(jnp.int32, (PP, K), 1)
    end = counts[:, 0:1]
    slab = jnp.zeros((PP, K), jnp.int32)
    for i in range(1, NS):
        slab = slab + jnp.where(col >= end, 1, 0)
        end = end + counts[:, i : i + 1]
    plane = pick(sub_p, [dest[pl.ds(classes[p], 1), :] for p in range(PP)])
    place = slab * 32 + plane
    row8 = lax.broadcasted_iota(jnp.int32, (PP, 128), 0)
    lane8 = lax.broadcasted_iota(jnp.int32, (PP, 128), 1)
    spread = jnp.where(lax.rem(lane8, PP) == row8, 1.0, 0.0)
    kind8 = pick(row8, [kinds_in[p] for p in range(PP)])

    def turned(x):
        return lax.dot_general(
            x.astype(F32), spread, (((0,), (0,)), ((), ())),
            precision=lax.Precision.HIGHEST, preferred_element_type=F32,
        )

    cscr[...] = turned(place)
    kind_row = turned(kind8)[0:1]
    shift_x = pick(row8, [shifts[0, p] for p in range(PP)])
    shift_y = pick(row8, [shifts[1, p] for p in range(PP)])
    person = pick(lane8, [shift_x, shift_y, kind8, jnp.zeros_like(kind8)])
    person = jnp.where(lane8 < 3, person, 0).astype(F32)
    slot_one = (lax.broadcasted_iota(jnp.int32, (1, 128), 1) // PP) & 1

    def arrange(b, carry):
        base = b * KYB
        for h in range(2):
            rows = [(base + i, base + j) for i, j in SLOTS[h]]
            rows += [(K - base - i, K - base - j) for i, j in SLOTS[h][:SHARED]]
            rows += [(base + i, base + j) for i, j in EXTRA[h]]
            for n, (i, j) in enumerate(rows):
                cwide[n : n + 1, :] = jnp.where(
                    slot_one == 0, cscr[pl.ds(i, 1), :], cscr[pl.ds(j, 1), :] + PL
                )
            cwide[10:11, :] = kind_row
            cwide[16:24, :] = person
            codes[b * 2 + h] = cwide[...].astype(BF)
        return carry

    cwide[...] = jnp.zeros_like(cwide)
    lax.fori_loop(0, NB, arrange, 0)

    def send_codes(q, carry):
        i = lax.rem(me + q, 32)
        to_plane(i // 2, lax.rem(i, 2), codes.at[i], crecv.at[me], code_s, code_r)
        return carry

    pltpu.make_async_copy(codes.at[me], crecv.at[me], code_r).start()
    lax.fori_loop(1, 32, send_codes, 0)

    for t in range(1, SHARED):
        compute(t, left[t], 64)
        send_rows(t)
    compute(SHARED, left_last[...], 32)
    send_last()

    pltpu.make_async_copy(crecv, crecv, code_r).wait()

    def widen(i, carry):
        cf[pl.ds(pl.multiple_of(i * 32, 32), 32), :] = crecv[i].astype(F32)
        return carry

    lax.fori_loop(0, 32, widen, 0)

    lane = lax.broadcasted_iota(jnp.int32, (32, 128), 1)
    sub = lax.broadcasted_iota(jnp.int32, (32, 128), 0)
    mine = (lane // 16) == lax.rem(sub, 8)

    def pair_codes(row):
        got = cf[pl.ds(row, 32, stride=32), :]
        return jnp.sum(jnp.where(mine, got, 0.0).reshape(4, 8, 128), axis=1)

    spot = lax.broadcasted_iota(jnp.int32, (256, 128), 0).astype(F32)

    def one_hot(code4):
        return jnp.concatenate(
            [
                jnp.where(spot == code4[g : g + 1, :], 1.0, 0.0).astype(BF)
                for g in range(4)
            ],
            axis=1,
        )

    row_id = lax.broadcasted_iota(jnp.int32, (128, 128), 0)
    row_class = jnp.where(row_id < 3 * NDEF, lax.rem(row_id, NDEF), -1).astype(F32)
    kind4 = pair_codes(10)
    kinds = jnp.concatenate(
        [jnp.where(row_class == kind4[g : g + 1, :], 1.0, 0.0).astype(BF) for g in range(4)],
        axis=1,
    )

    def count(n, carry):
        tally = lax.dot_general(
            one_hot(pair_codes(jnp.where(n < TILES, n, n + SHARED))), kinds,
            (((1,), (1,)), ((), ())), preferred_element_type=F32,
        )
        start = pl.multiple_of(n * 32, 32)
        nsend[:, pl.ds(start, 32), :] = tally.astype(BF).reshape(NS, 32, 128)
        return carry

    lax.fori_loop(0, NCNT, count, 0)

    def to_slab(q, src, dst, send_sem, recv_sem):
        peer = lax.rem(ms + q, NS)
        pltpu.make_async_remote_copy(
            src_ref=src(peer), dst_ref=dst, send_sem=send_sem, recv_sem=recv_sem,
            device_id=(mb, peer), device_id_type=MESH,
        ).start()

    pltpu.make_async_copy(nsend.at[ms], nrecv.at[ms], n_r).start()
    for q in range(1, NS):
        to_slab(q, lambda peer: nsend.at[peer], nrecv.at[ms], n_s, n_r)

    slot_of = lane8 & 7
    part = lane8 // 8
    flat = [[i for two in SLOTS[h] for i in two] for h in range(2)]
    slot_ky = mb * KYB + jnp.where(core == 0, pick(slot_of, flat[0]), pick(slot_of, flat[1]))
    slot_sq = square(slot_ky)
    col_sq = square(col)
    every = [defocus[i] for i in range(NDEF)]
    quarter = 0.5 * math.pi

    def prepare(i, carry):
        own = cf[pl.ds(pl.multiple_of(i * 32 + 16, 16), 8), :]
        sx, sy, kind = own[:, 0:1], own[:, 1:2], own[:, 2:3]
        focus = jnp.full((PP, 1), every[0])
        for n in range(1, NDEF):
            focus = jnp.where(kind == n, every[n], focus)
        arg = focus * slot_sq + PHASE_OFFSET
        turn = phase(slot_ky, sy)
        sc[i] = jnp.sin(
            jnp.where(
                part == 0,
                arg,
                jnp.where(part == 1, arg + quarter, jnp.where(part == 2, turn - quarter, turn)),
            )
        )
        arg_x = focus * col_sq
        turn_x = phase(col, sx)
        vx[0, i] = jnp.sin(arg_x)
        vx[1, i] = jnp.cos(arg_x)
        vx[2, i] = jnp.cos(turn_x)
        vx[3, i] = -jnp.sin(turn_x)
        return carry

    lax.fori_loop(0, 32, prepare, 0)

    load_right.wait()

    def process(t, mirrored):
        pltpu.make_async_copy(recvb.at[t], recvb.at[t], row_r.at[t]).wait()

        def half(m, carry):
            block = recvb[t, pl.ds(m * 16, 16)].reshape(256, 2 * K)
            start = pl.multiple_of(m * 256, 256)
            pq[0, pl.ds(start, 256), :] = jnp.dot(
                block[:, :K], right[pl.ds(0, K), :], preferred_element_type=F32
            )
            pq[1, pl.ds(start, 256), :] = jnp.dot(
                block[:, K:], right[pl.ds(K, K), :], preferred_element_type=F32
            )
            return carry

        lax.fori_loop(0, 2, half, 0)

        def weigh(i, carry):
            scal = sc[i]
            got = [[], [], [], []]
            for j in range(2):
                lane_j = t * 2 + j
                sa, ca, er, ei = [scal[:, lane_j + 8 * n : lane_j + 8 * n + 1] for n in range(4)]
                rows = pl.ds(pl.multiple_of(i * 16 + j * 8, 8), 8)
                pr, pi = pq[0, rows, pl.ds(0, K)], pq[0, rows, pl.ds(K, K)]
                qr, qi = pq[1, rows, pl.ds(0, K)], pq[1, rows, pl.ds(K, K)]
                ctf = sa * vx[1, i] + ca * vx[0, i]
                gr, gi = ctf * vx[2, i], ctf * vx[3, i]
                fa, fb, fc, fd = er * gr, ei * gi, er * gi, ei * gr
                sr, si = pr + qr, pi + qi
                fr, fi = fa - fb, fc + fd
                got[0].append(sr * fr - si * fi)
                got[1].append(sr * fi + si * fr)
                if mirrored:
                    sr, si = pr - qr, pi - qi
                    fr, fi = fa + fb, fc - fd
                    got[2].append(sr * fr - si * fi)
                    got[3].append(sr * fi + si * fr)
            rows = pl.ds(pl.multiple_of(i * 16, 16), 16)
            for n in range(4 if mirrored else 2):
                to = wp if n < 2 else wm
                to[rows, pl.ds((n % 2) * K, K)] = jnp.concatenate(got[n], axis=0).astype(BF)
            return carry

        lax.fori_loop(0, 32, weigh, 0)

        def total(hot, rows):
            return jnp.dot(hot, rows, preferred_element_type=F32).astype(BF).reshape(NS, 32, 2 * K)

        if mirrored:
            zsend[t, :, pl.ds(0, 32), :] = total(one_hot(pair_codes(t)), wp[...])
            zsend[t, :, pl.ds(32, 32), :] = total(one_hot(pair_codes(TILES + t)), wm[...])
            for q in range(1, NS):
                to_slab(q, lambda peer: zsend.at[t, peer], zrecv.at[t, ms], z_s.at[t], z_r.at[t])
            pltpu.make_async_copy(zsend.at[t, ms], zrecv.at[t, ms], z_r.at[t]).start()
        else:
            zlast[...] = total(one_hot(pair_codes(t)), wp[...])
            for q in range(1, NS):
                to_slab(q, lambda peer: zlast.at[peer], zgot.at[mz], z_s.at[t], z_r.at[t])
            pltpu.make_async_copy(zlast.at[ms], zgot.at[mz], z_r.at[t]).start()

    def weights():
        lane_k = lax.broadcasted_iota(jnp.int32, (KYB, 128), 1)
        own_ky = mb * KYB + lax.broadcasted_iota(jnp.int32, (KYB, 128), 0)
        arg2_y = 2.0 * (pick(lane_k & (NDEF - 1), every) * square(own_ky) + PHASE_OFFSET)
        group = lane_k // NDEF
        tw = jnp.where(
            group == 0,
            -0.5 * jnp.cos(arg2_y),
            jnp.where(group == 1, 0.5 * jnp.sin(arg2_y), jnp.where(group == 2, 0.5, 0.0)),
        )
        row_k = lax.broadcasted_iota(jnp.int32, (NDEF, K), 0)
        col_k = lax.broadcasted_iota(jnp.int32, (NDEF, K), 1)
        arg2_x = 2.0 * (pick(row_k, every) * square(col_k))
        rw = jnp.concatenate(
            [
                jnp.cos(arg2_x),
                jnp.sin(arg2_x),
                jnp.ones((NDEF, K), F32),
                jnp.zeros((128 - 3 * NDEF, K), F32),
            ],
            axis=0,
        )
        pltpu.make_async_copy(nrecv, nrecv, n_r).wait()
        for h in range(2):
            scaled, names = [], []
            for n, two in enumerate(COUNTED[h]):
                if h == 1 and n == SHARED:
                    continue
                for j, i in enumerate(two):
                    if j == 1 and two[0] == two[1]:
                        continue
                    rows = pl.ds(n * 32 + j * PL, PL)
                    x = nrecv[h, rows, :].astype(F32)
                    for z in range(1, NS // 2):
                        x += nrecv[2 * z + h, rows, :].astype(F32)
                    scaled.append(x * tw[i : i + 1, :])
                    names.append(i)
            res = jnp.dot(
                jnp.concatenate(scaled, axis=0), rw,
                precision=lax.Precision.HIGHEST, preferred_element_type=F32,
            )
            res = 1.0 / (res + TAU_PRIOR)
            for m, i in enumerate(names):
                wts[pl.ds(i * PL, PL), :] = res[m * PL : (m + 1) * PL]

    def finish(i, sums):
        rows = pl.ds(i * PL, PL)
        inverse = wts[rows, :]
        for h in range(2):
            cols = pl.ds(h * K, K)
            top = TAU_PRIOR * ref[rows, cols].astype(F32) + sums[:, h * K : (h + 1) * K]
            out[rows, cols] = (top * inverse).astype(BF)

    def mirror_rows(t):
        return [(h, j) for h in (1, 0) for j in range(2) if j == 0 or SLOTS[h][t][0] != SLOTS[h][t][1]]

    def gather(t):
        pltpu.make_async_copy(zrecv.at[t], zrecv.at[t], z_r.at[t]).wait()

        def over_z(h, start):
            rows = pl.ds(start, PL)
            x = zrecv[t, h, rows, :].astype(F32)
            for z in range(1, NS // 2):
                x += zrecv[t, 2 * z + h, rows, :].astype(F32)
            return x

        rows = mirror_rows(t)
        for m, (h, j) in enumerate(rows):
            msend[t, m] = over_z(h, 32 + j * PL).astype(BF)
        pltpu.make_async_remote_copy(
            src_ref=msend.at[t, pl.ds(0, len(rows))], dst_ref=mrecv.at[t, pl.ds(0, len(rows))],
            send_sem=m_s.at[t], recv_sem=m_r.at[t],
            device_id=(NB - 1 - mb, ms), device_id_type=MESH,
        ).start()
        for h, j in rows:
            finish(SLOTS[h][t][j], over_z(h, j * PL))

    process(0, True)
    load_ref.wait()
    weights()
    process(1, True)
    gather(0)
    process(2, True)
    gather(1)

    @pl.when(core == 0)
    def _():
        process(SHARED, False)

    gather(2)

    pltpu.make_async_copy(zgot, zgot, z_r.at[SHARED]).wait()
    for j in range(2):
        rows = pl.ds(j * PL, PL)
        x = zgot[0, rows, :].astype(F32)
        for z in range(1, NS // 2):
            x += zgot[z, rows, :].astype(F32)
        finish(SLOTS[0][SHARED][j], x)

    def drain(src, send_sem, recv_sem):
        return pltpu.make_async_remote_copy(
            src_ref=src, dst_ref=src, send_sem=send_sem, recv_sem=recv_sem,
            device_id=(mb, ms), device_id_type=MESH,
        )

    for t in range(SHARED):
        rows = mirror_rows(t)
        drain(msend.at[t, pl.ds(0, len(rows))], m_s.at[t], m_r.at[t]).wait()
        for m, (h, j) in enumerate(rows):
            finish(KYB - SLOTS[h][t][j], mrecv[t, m].astype(F32))

    drain(crecv.at[pl.ds(0, 31)], code_s, code_r).wait_send()
    drain(nsend.at[pl.ds(0, 7)], n_s, n_r).wait_send()
    for t in range(SHARED):
        drain(sendb.at[t, pl.ds(0, 31)], row_s.at[t], row_r.at[t]).wait_send()
        drain(zsend.at[t, pl.ds(0, 7)], z_s.at[t], z_r.at[t]).wait_send()

    @pl.when(core == 0)
    def _():
        drain(sendb.at[SHARED, pl.ds(0, 15)], row_s.at[SHARED], row_r.at[SHARED]).wait_send()
        drain(zlast.at[pl.ds(0, 7)], z_s.at[SHARED], z_r.at[SHARED]).wait_send()

    @pl.when(core == 1)
    def _():
        drain(sendb.at[SHARED, pl.ds(0, 16)], row_s.at[SHARED], row_r.at[SHARED]).wait_send()


def per_device(images, classes, shifts, defocus_class, defocus, run_counts, dest_map, ref):
    left, left_last, right = tables()
    vmem = pl.BlockSpec(memory_space=pltpu.VMEM)
    smem = pl.BlockSpec(memory_space=pltpu.SMEM)
    far = pl.BlockSpec(memory_space=pl.ANY)
    dma = pltpu.SemaphoreType.DMA
    out = pl.pallas_call(
        kernel,
        out_shape=jax.ShapeDtypeStruct((KYB * PL, 2 * K), BF),
        in_specs=[smem] * 4 + [vmem] * 3 + [far] * 4,
        out_specs=vmem,
        scratch_shapes=[
            pltpu.VMEM((PP, K, K), BF),
            pltpu.VMEM((2 * K, 2 * K), BF),
            pltpu.VMEM(dest_map.shape, jnp.int32),
            pltpu.VMEM((KYB * PL, 2 * K), BF),
            pltpu.VMEM((6, 64 * PP, 128), F32),
            pltpu.VMEM((K, 128), F32),
            pltpu.VMEM((32, 128), F32),
            pltpu.VMEM((32, 32, 128), BF),
            pltpu.VMEM((32 * 32, 128), F32),
            pltpu.VMEM((32, PP, 128), F32),
            pltpu.VMEM((4, 32, PP, K), F32),
            pltpu.VMEM((2, 512, 2 * K), F32),
            pltpu.VMEM((512, 2 * K), BF),
            pltpu.VMEM((512, 2 * K), BF),
            pltpu.VMEM((TILES, 32, 16, 2 * K), BF),
            pltpu.VMEM((TILES, 32, 16, 2 * K), BF),
            pltpu.VMEM((32, 32, 128), BF),
            pltpu.VMEM((SHARED, NS, 64, 2 * K), BF),
            pltpu.VMEM((SHARED, NS, 64, 2 * K), BF),
            pltpu.VMEM((NS, 32, 2 * K), BF),
            pltpu.VMEM((NS // 2, 32, 2 * K), BF),
            pltpu.VMEM((NS, NCNT * 32, 128), BF),
            pltpu.VMEM((NS, NCNT * 32, 128), BF),
            pltpu.VMEM((SHARED, 4, PL, 2 * K), BF),
            pltpu.VMEM((SHARED, 4, PL, 2 * K), BF),
            pltpu.VMEM((KYB * PL, K), F32),
            dma((PP,)), dma, dma, dma, dma, dma, dma((TILES,)), dma((TILES,)),
            dma((TILES,)), dma((TILES,)), dma, dma, dma((SHARED,)), dma((SHARED,)),
        ],
        compiler_params=pltpu.CompilerParams(
            collective_id=0, has_side_effects=True, vmem_limit_bytes=60 * 1024 * 1024
        ),
    )(
        classes, defocus_class, defocus, shifts.T, run_counts, jnp.asarray(left),
        jnp.asarray(left_last), images, jnp.asarray(right), dest_map,
        ref.reshape(KYB * PL, 2 * K),
    )
    return out.reshape(KYB, PL, 2 * K)


def solution(mesh):
    placed = (
        P(("batch", "slab"), None, None),
        P(("batch", "slab")),
        P(("batch", "slab"), None),
        P(("batch", "slab")),
        P(),
        P(("batch", "slab"), None),
        P(),
        P("batch", "slab", None),
    )
    return jax.shard_map(
        per_device, mesh=mesh, in_specs=placed, out_specs=P("batch", "slab", None), check_vma=False
    )
```

```python
import math

import jax
import jax.numpy as jnp
import ml_dtypes
import numpy as np
from jax import lax
from jax.experimental import pallas as pl
from jax.experimental.pallas import tpu as pltpu
from jax.sharding import PartitionSpec as P

TAU_PRIOR = 4.0
PHASE_OFFSET = 0.1
MESH = pl.DeviceIdType.MESH

K = 384
NB = 16
NS = 8
PP = 8
KYB = K // NB
SHARED = 3
TILES = SHARED + 1
PL = 16
NDEF = 16
BF = jnp.bfloat16
F32 = jnp.float32
LAST = SHARED
EXTRA = 13
NCNT = TILES + 3
TURNS = (
    (0, 1), (1, 0), (0, 3), (3, 0), (1, 1), (1, 3), (3, 3), (3, 1),
    (1, 2), (2, 1), (3, 2), (2, 3), (0, 2), (2, 0), (2, 2),
)


def tables():
    index = np.arange(K)
    angle = 2.0 * np.pi / K * ((index[:, None] * index[None, :]) % K)
    cosine = (np.cos(angle) / math.sqrt(K)).astype(np.float32)
    sine = (np.sin(angle) / math.sqrt(K)).astype(np.float32)

    def left(t):
        rows = [
            KYB * b + (6 * h + 2 * t + 1 + j if t < LAST else 0)
            for h in range(2)
            for b in range(NB)
            for j in range(2)
        ]
        return np.concatenate([cosine[rows], -sine[rows]], axis=0)

    both = np.stack([left(t) for t in range(TILES)], axis=0)
    right = np.concatenate(
        [np.concatenate([cosine, -sine], 1), np.concatenate([sine, cosine], 1)], 0
    )
    kind = ml_dtypes.bfloat16
    return both.astype(kind), right.astype(kind)


def kernel(
    classes, kinds_in, defocus, shifts, counts, left, img_in, right_in, dest_in, ref_in,
    out,
    img, right, dest, ref, scr, cscr, cwide, codes, cf, sc, vx, pq, wp, wm,
    sendb, recvb, crecv, zsend, zrecv, zgot, nsend, nrecv, msend, mrecv, wts, tws,
    img_m, right_m, dest_m, ref_m, code_s, code_r, row_s, row_r, z_s, z_r, n_s, n_r, m_s, m_r,
):
    mb = lax.axis_index("batch")
    ms = lax.axis_index("slab")
    core = lax.rem(ms, 2)
    zbase = ms - core
    mz = ms // 2
    me = mb * 2 + core
    my = mb // 4
    mx = lax.rem(mb, 4)

    def peer_of(turn):
        dy, dx = turn
        py = lax.rem(my + jnp.where(core == 0, dy, dx), 4)
        px = lax.rem(mx + jnp.where(core == 0, dx, 4 - dy), 4)
        return py * 4 + px

    barrier = pltpu.get_barrier_semaphore()
    loads = [pltpu.make_async_copy(img_in.at[p], img.at[p], img_m.at[p]) for p in range(PP)]
    load_right = pltpu.make_async_copy(right_in, right, right_m)
    load_dest = pltpu.make_async_copy(dest_in, dest, dest_m)
    load_ref = pltpu.make_async_copy(ref_in, ref, ref_m)
    for load in (*loads, load_dest, load_right, load_ref):
        load.start()

    def greet_plane(q, carry):
        i = lax.rem(me + q, 32)
        pl.semaphore_signal(
            barrier, inc=1, device_id=(i // 2, zbase + lax.rem(i, 2)), device_id_type=MESH
        )
        return carry

    def greet_slab(q, carry):
        pl.semaphore_signal(
            barrier, inc=1, device_id=(mb, lax.rem(ms + q, NS)), device_id_type=MESH
        )
        return carry

    lax.fori_loop(1, 32, greet_plane, 0)
    lax.fori_loop(1, NS, greet_slab, 0)

    def pick(index, values):
        got = jnp.full(index.shape, values[0])
        for i, value in enumerate(values[1:], 1):
            got = jnp.where(index == i, value, got)
        return got

    def square(k):
        half = jnp.where(k >= K // 2, k - K, k).astype(F32) * (1.0 / K)
        return half * half

    def phase(k, shift):
        turn = k.astype(F32) * shift
        turn = turn - K * jnp.floor((turn + 0.5) * (1.0 / K))
        return turn * (2.0 * math.pi / K)

    def to_plane(b, h, src, dst, send_sem, recv_sem):
        pltpu.make_async_remote_copy(
            src_ref=src, dst_ref=dst, send_sem=send_sem, recv_sem=recv_sem,
            device_id=(b, zbase + h), device_id_type=MESH,
        ).start()

    def compute(t):
        table = left[t]

        def one(p, carry):
            @pl.when(t == 0)
            def _():
                pltpu.make_async_copy(img_in.at[p], img.at[p], img_m.at[p]).wait()

            sec = jnp.dot(table, img[p], preferred_element_type=F32)
            for g in range(3):
                cols = slice(g * 128, (g + 1) * 128)
                scr[g, pl.ds(p, 64, stride=8), :] = sec[:64, cols]
                scr[3 + g, pl.ds(p, 64, stride=8), :] = sec[64:, cols]
            return carry

        lax.fori_loop(0, PP, one, 0)

        def pack(i, carry):
            start = pl.multiple_of(i * 16, 16)
            target = lax.rem(i, NB) * 2 + i // NB
            for g in range(6):
                sendb[t, target, :, pl.ds(g * 128, 128)] = scr[g, pl.ds(start, 16), :].astype(BF)
            return carry

        lax.fori_loop(0, 32, pack, 0)

    other = 1 - core

    def send_rows(t):
        to_plane(mb, other, sendb.at[t, mb * 2 + other], recvb.at[t, me], row_s.at[t], row_r.at[t])
        pltpu.make_async_copy(sendb.at[t, me], recvb.at[t, me], row_r.at[t]).start()
        for flip in range(2):
            h = core if flip == 0 else other
            for turn in TURNS:
                b = peer_of(turn)
                to_plane(b, h, sendb.at[t, b * 2 + h], recvb.at[t, me], row_s.at[t], row_r.at[t])

    def send_last():
        t = LAST

        @pl.when(core == 0)
        def _():
            pltpu.make_async_copy(sendb.at[t, me], recvb.at[t, me], row_r.at[t]).start()

        @pl.when(core == 1)
        def _():
            to_plane(mb, 0, sendb.at[t, mb * 2], recvb.at[t, me], row_s.at[t], row_r.at[t])

        for turn in TURNS:
            b = peer_of(turn)
            to_plane(b, 0, sendb.at[t, b * 2], recvb.at[t, me], row_s.at[t], row_r.at[t])

    sub_p = lax.broadcasted_iota(jnp.int32, (PP, K), 0)
    col = lax.broadcasted_iota(jnp.int32, (PP, K), 1)
    row8 = lax.broadcasted_iota(jnp.int32, (PP, 128), 0)
    lane8 = lax.broadcasted_iota(jnp.int32, (PP, 128), 1)

    def tell():
        load_dest.wait()
        end = counts[:, 0:1]
        slab = jnp.zeros((PP, K), jnp.int32)
        for i in range(1, NS):
            slab = slab + jnp.where(col >= end, 1, 0)
            end = end + counts[:, i : i + 1]
        plane = pick(sub_p, [dest[pl.ds(classes[p], 1), :] for p in range(PP)])
        place = slab * 32 + plane
        spread = jnp.where(lax.rem(lane8, PP) == row8, 1.0, 0.0)
        kind8 = pick(row8, [kinds_in[p] for p in range(PP)])

        def turned(x):
            return lax.dot_general(
                x.astype(F32), spread, (((0,), (0,)), ((), ())),
                precision=lax.Precision.HIGHEST, preferred_element_type=F32,
            )

        cscr[...] = turned(place)
        kind_row = turned(kind8)[0:1]
        shift_x = pick(row8, [shifts[0, p] for p in range(PP)])
        shift_y = pick(row8, [shifts[1, p] for p in range(PP)])
        person = pick(lane8, [shift_x, shift_y, kind8, jnp.zeros_like(kind8)])
        person = jnp.where(lane8 < 3, person, 0).astype(F32)
        slot_one = (lax.broadcasted_iota(jnp.int32, (1, 128), 1) // PP) & 1

        def arrange(d, carry):
            base = d // 2 * KYB
            step = 6 * lax.rem(d, 2)
            for n in range(TILES + SHARED + 3):
                for_two = []
                for j in range(2):
                    if n < SHARED:
                        ky = base + step + 2 * n + 1 + j
                    elif n == LAST:
                        ky = base
                    elif n < TILES + SHARED:
                        ky = K - (base + step + 2 * (n - TILES) + 1 + j)
                    else:
                        ky = jnp.minimum(base + EXTRA + step + 2 * (n - TILES - SHARED) + j, K - 1)
                    for_two.append(cscr[pl.ds(ky, 1), :])
                cwide[n : n + 1, :] = jnp.where(slot_one == 0, for_two[0], for_two[1] + PL)
            codes[d] = cwide[...].astype(BF)
            return carry

        cwide[...] = jnp.zeros_like(cwide)
        cwide[10:11, :] = kind_row
        cwide[16:24, :] = person
        lax.fori_loop(0, 2 * NB, arrange, 0)

        def send_codes(q, carry):
            i = lax.rem(me + q, 32)
            to_plane(i // 2, lax.rem(i, 2), codes.at[i], crecv.at[me], code_s, code_r)
            return carry

        pltpu.make_async_copy(codes.at[me], crecv.at[me], code_r).start()
        lax.fori_loop(1, 32, send_codes, 0)


    def produce(t, carry):
        compute(t)

        @pl.when(t == 0)
        def _():
            pl.semaphore_wait(barrier, 31 + NS - 1)

        @pl.when(t < LAST)
        def _():
            send_rows(t)

        pl.when(t == LAST)(send_last)
        pl.when(t == 0)(tell)
        return carry

    lax.fori_loop(0, TILES, produce, 0)

    pltpu.make_async_copy(crecv, crecv, code_r).wait()

    def widen(i, carry):
        cf[pl.ds(pl.multiple_of(i * 32, 32), 32), :] = crecv[i].astype(F32)
        return carry

    lax.fori_loop(0, 32, widen, 0)

    lane = lax.broadcasted_iota(jnp.int32, (32, 128), 1)
    sub = lax.broadcasted_iota(jnp.int32, (32, 128), 0)
    mine = (lane // 16) == lax.rem(sub, 8)

    def pair_codes(row):
        got = cf[pl.ds(row, 32, stride=32), :]
        return jnp.sum(jnp.where(mine, got, 0.0).reshape(4, 8, 128), axis=1)

    spot = lax.broadcasted_iota(jnp.int32, (256, 128), 0).astype(F32)

    def one_hot(code4):
        return jnp.concatenate(
            [
                jnp.where(spot == code4[g : g + 1, :], 1.0, 0.0).astype(BF)
                for g in range(4)
            ],
            axis=1,
        )

    row_id = lax.broadcasted_iota(jnp.int32, (128, 128), 0)
    row_class = jnp.where(row_id < 3 * NDEF, lax.rem(row_id, NDEF), -1).astype(F32)
    kind4 = pair_codes(10)
    kinds = jnp.concatenate(
        [jnp.where(row_class == kind4[g : g + 1, :], 1.0, 0.0).astype(BF) for g in range(4)],
        axis=1,
    )

    def count(n, carry):
        tally = lax.dot_general(
            one_hot(pair_codes(jnp.where(n < TILES, n, n + SHARED))), kinds,
            (((1,), (1,)), ((), ())), preferred_element_type=F32,
        )
        start = pl.multiple_of(n * 32, 32)
        nsend[:, pl.ds(start, 32), :] = tally.astype(BF).reshape(NS, 32, 128)
        return carry

    lax.fori_loop(0, NCNT, count, 0)

    def to_slab(q, src, dst, send_sem, recv_sem):
        peer = lax.rem(ms + q, NS)
        pltpu.make_async_remote_copy(
            src_ref=src(peer), dst_ref=dst, send_sem=send_sem, recv_sem=recv_sem,
            device_id=(mb, peer), device_id_type=MESH,
        ).start()

    pltpu.make_async_copy(nsend.at[ms], nrecv.at[ms], n_r).start()
    def send_counts(q, carry):
        to_slab(q, lambda peer: nsend.at[peer], nrecv.at[ms], n_s, n_r)
        return carry

    lax.fori_loop(1, NS, send_counts, 0)

    slot_of = (lane8 // 8) * 2 + (lane8 & 1)
    part = (lane8 // 2) & 3
    slot_ky = mb * KYB + jnp.where(slot_of < 2 * SHARED, 6 * core + 1 + slot_of, 0)
    slot_sq = square(slot_ky)
    col_sq = square(col)
    every = [defocus[i] for i in range(NDEF)]
    quarter = 0.5 * math.pi

    def prepare(i, carry):
        own = cf[pl.ds(pl.multiple_of(i * 32 + 16, 16), 8), :]
        sx, sy, kind = own[:, 0:1], own[:, 1:2], own[:, 2:3]
        focus = jnp.full((PP, 1), every[0])
        for n in range(1, NDEF):
            focus = jnp.where(kind == n, every[n], focus)
        arg = focus * slot_sq + PHASE_OFFSET
        turn = phase(slot_ky, sy)
        scal = jnp.sin(
            jnp.where(
                part == 0,
                arg,
                jnp.where(part == 1, arg + quarter, jnp.where(part == 2, turn - quarter, turn)),
            )
        )
        sc[0, i] = scal
        for t in range(1, TILES):
            sc[t, i] = pltpu.roll(scal, 128 - 8 * t, 1)
        arg_x = focus * col_sq
        turn_x = phase(col, sx)
        vx[0, i] = jnp.sin(arg_x)
        vx[1, i] = jnp.cos(arg_x)
        vx[2, i] = jnp.cos(turn_x)
        vx[3, i] = -jnp.sin(turn_x)
        return carry

    lax.fori_loop(0, 32, prepare, 0)

    load_right.wait()

    def process(t):
        pltpu.make_async_copy(recvb.at[t], recvb.at[t], row_r.at[t]).wait()

        def half(m, carry):
            block = recvb[t, pl.ds(m * 16, 16)].reshape(256, 2 * K)
            start = pl.multiple_of(m * 256, 256)
            pq[0, pl.ds(start, 256), :] = jnp.dot(
                block[:, :K], right[pl.ds(0, K), :], preferred_element_type=F32
            )
            pq[1, pl.ds(start, 256), :] = jnp.dot(
                block[:, K:], right[pl.ds(K, K), :], preferred_element_type=F32
            )
            return carry

        lax.fori_loop(0, 2, half, 0)

        def weigh(i, carry):
            scal = sc[t, i]
            got = [[], [], [], []]
            for j in range(2):
                sa, ca, er, ei = [scal[:, 2 * n + j : 2 * n + j + 1] for n in range(4)]
                rows = pl.ds(pl.multiple_of(i * 16 + j * 8, 8), 8)
                pr, pi = pq[0, rows, pl.ds(0, K)], pq[0, rows, pl.ds(K, K)]
                qr, qi = pq[1, rows, pl.ds(0, K)], pq[1, rows, pl.ds(K, K)]
                ctf = sa * vx[1, i] + ca * vx[0, i]
                gr, gi = ctf * vx[2, i], ctf * vx[3, i]
                fa, fb, fc, fd = er * gr, ei * gi, er * gi, ei * gr
                sr, si = pr + qr, pi + qi
                fr, fi = fa - fb, fc + fd
                got[0].append(sr * fr - si * fi)
                got[1].append(sr * fi + si * fr)
                sr, si = pr - qr, pi - qi
                fr, fi = fa + fb, fc - fd
                got[2].append(sr * fr - si * fi)
                got[3].append(sr * fi + si * fr)
            rows = pl.ds(pl.multiple_of(i * 16, 16), 16)
            for n in range(4):
                to = wp if n < 2 else wm
                to[rows, pl.ds((n % 2) * K, K)] = jnp.concatenate(got[n], axis=0).astype(BF)
            return carry

        lax.fori_loop(0, 32, weigh, 0)

        def total(hot, rows):
            return jnp.dot(hot, rows, preferred_element_type=F32).astype(BF).reshape(NS, 32, 2 * K)

        zsend[t, :, pl.ds(0, 32), :] = total(one_hot(pair_codes(t)), wp[...])

        @pl.when(t < LAST)
        def _():
            zsend[t, :, pl.ds(32, 32), :] = total(one_hot(pair_codes(TILES + t)), wm[...])

            def send(q, carry):
                to_slab(q, lambda peer: zsend.at[t, peer], zrecv.at[t, ms], z_s.at[t], z_r.at[t])
                return carry

            lax.fori_loop(1, NS, send, 0)
            pltpu.make_async_copy(zsend.at[t, ms], zrecv.at[t, ms], z_r.at[t]).start()

        @pl.when(t == LAST)
        def _():
            top = pl.ds(0, PL)

            def send(q, carry):
                to_slab(q, lambda peer: zsend.at[t, peer, top], zgot.at[mz], z_s.at[t], z_r.at[t])
                return carry

            lax.fori_loop(1, NS, send, 0)
            pltpu.make_async_copy(zsend.at[t, ms, top], zgot.at[mz], z_r.at[t]).start()

    def weights():
        lane_k = lax.broadcasted_iota(jnp.int32, (32, 128), 1)
        own_ky = mb * KYB + lax.broadcasted_iota(jnp.int32, (32, 128), 0)
        arg2_y = 2.0 * (pick(lane_k & (NDEF - 1), every) * square(own_ky) + PHASE_OFFSET)
        group = lane_k // NDEF
        tws[...] = jnp.where(
            group == 0,
            -0.5 * jnp.cos(arg2_y),
            jnp.where(group == 1, 0.5 * jnp.sin(arg2_y), jnp.where(group == 2, 0.5, 0.0)),
        )
        row_k = lax.broadcasted_iota(jnp.int32, (NDEF, K), 0)
        col_k = lax.broadcasted_iota(jnp.int32, (NDEF, K), 1)
        arg2_x = 2.0 * (pick(row_k, every) * square(col_k))
        rw = jnp.concatenate(
            [
                jnp.cos(arg2_x),
                jnp.sin(arg2_x),
                jnp.ones((NDEF, K), F32),
                jnp.zeros((128 - 3 * NDEF, K), F32),
            ],
            axis=0,
        )
        pltpu.make_async_copy(nrecv, nrecv, n_r).wait()

        def one(h, carry):
            x = nrecv[h].astype(F32)
            for z in range(1, NS // 2):
                x += nrecv[2 * z + h].astype(F32)
            own, more = 6 * h + 1, 6 * h + EXTRA

            def times(part, i, rows):
                return (part.reshape(rows, PL, 128) * tws[pl.ds(i, rows), :][:, None, :]).reshape(
                    rows * PL, 128
                )

            scaled = jnp.concatenate(
                [times(x[:96], own, 6), times(x[96:128], 0, 2), times(x[128:], more, 6)], axis=0
            )
            res = jnp.dot(
                scaled, rw, precision=lax.Precision.HIGHEST, preferred_element_type=F32
            )
            res = 1.0 / (res + TAU_PRIOR)
            wts[pl.ds(pl.multiple_of(own * PL, PL), 96), :] = res[:96]
            wts[pl.ds(pl.multiple_of(more * PL, PL), 96), :] = res[128:]

            @pl.when(h == 0)
            def _():
                wts[pl.ds(0, PL), :] = res[96:112]

            return carry

        lax.fori_loop(0, 2, one, 0)

    def finish(i, sums):
        rows = pl.ds(pl.multiple_of(i * PL, PL), PL)
        inverse = wts[rows, :]
        for h in range(2):
            cols = pl.ds(h * K, K)
            top = TAU_PRIOR * ref[rows, cols].astype(F32) + sums[:, h * K : (h + 1) * K]
            out[rows, cols] = (top * inverse).astype(BF)

    def gather(t):
        pltpu.make_async_copy(zrecv.at[t], zrecv.at[t], z_r.at[t]).wait()

        def over_z(h, start):
            rows = pl.ds(pl.multiple_of(start, PL), PL)
            x = zrecv[t, h, rows, :].astype(F32)
            for z in range(1, NS // 2):
                x += zrecv[t, 2 * z + h, rows, :].astype(F32)
            return x

        def mirror(m, carry):
            msend[t, m] = over_z(m // 2, 2 * PL + lax.rem(m, 2) * PL).astype(BF)
            return carry

        lax.fori_loop(0, 4, mirror, 0)
        pltpu.make_async_remote_copy(
            src_ref=msend.at[t], dst_ref=mrecv.at[t], send_sem=m_s.at[t], recv_sem=m_r.at[t],
            device_id=(NB - 1 - mb, ms), device_id_type=MESH,
        ).start()

        def own(m, carry):
            h, j = m // 2, lax.rem(m, 2)
            finish(6 * h + 2 * t + 1 + j, over_z(h, j * PL))
            return carry

        lax.fori_loop(0, 4, own, 0)

    def consume(t, carry):
        @pl.when(jnp.logical_or(t < LAST, core == 0))
        def _():
            process(t)

        pl.when(t == 0)(weights)

        @pl.when(t > 0)
        def _():
            gather(t - 1)

        return carry

    load_ref.wait()
    lax.fori_loop(0, TILES, consume, 0)

    pltpu.make_async_copy(zgot, zgot, z_r.at[LAST]).wait()
    x = zgot[0].astype(F32)
    for z in range(1, NS // 2):
        x += zgot[z].astype(F32)
    finish(0, x)

    def drain(src, send_sem, recv_sem):
        return pltpu.make_async_remote_copy(
            src_ref=src, dst_ref=src, send_sem=send_sem, recv_sem=recv_sem,
            device_id=(mb, ms), device_id_type=MESH,
        )

    def mirrored(t, carry):
        drain(msend.at[t], m_s.at[t], m_r.at[t]).wait()

        def one(m, inner):
            i = 6 * (m // 2) + 2 * t + 1 + lax.rem(m, 2)

            @pl.when(i < KYB // 2)
            def _():
                finish(KYB - i, mrecv[t, m].astype(F32))

            return inner

        lax.fori_loop(0, 4, one, 0)
        return carry

    lax.fori_loop(0, SHARED, mirrored, 0)

    drain(crecv.at[pl.ds(0, 31)], code_s, code_r).wait_send()
    drain(nsend.at[pl.ds(0, 7)], n_s, n_r).wait_send()
    def drain_tile(t, carry):
        drain(sendb.at[t, pl.ds(0, 31)], row_s.at[t], row_r.at[t]).wait_send()
        drain(zsend.at[t, pl.ds(0, 7)], z_s.at[t], z_r.at[t]).wait_send()
        return carry

    lax.fori_loop(0, SHARED, drain_tile, 0)

    @pl.when(core == 0)
    def _():
        drain(sendb.at[LAST, pl.ds(0, 15)], row_s.at[LAST], row_r.at[LAST]).wait_send()
        drain(zsend.at[LAST, pl.ds(0, 7), pl.ds(0, PL)], z_s.at[LAST], z_r.at[LAST]).wait_send()

    @pl.when(core == 1)
    def _():
        drain(sendb.at[LAST, pl.ds(0, 16)], row_s.at[LAST], row_r.at[LAST]).wait_send()


def per_device(images, classes, shifts, defocus_class, defocus, run_counts, dest_map, ref):
    left, right = tables()
    vmem = pl.BlockSpec(memory_space=pltpu.VMEM)
    smem = pl.BlockSpec(memory_space=pltpu.SMEM)
    far = pl.BlockSpec(memory_space=pl.ANY)
    dma = pltpu.SemaphoreType.DMA
    out = pl.pallas_call(
        kernel,
        out_shape=jax.ShapeDtypeStruct((KYB * PL, 2 * K), BF),
        in_specs=[smem] * 4 + [vmem] * 2 + [far] * 4,
        out_specs=vmem,
        scratch_shapes=[
            pltpu.VMEM((PP, K, K), BF),
            pltpu.VMEM((2 * K, 2 * K), BF),
            pltpu.VMEM(dest_map.shape, jnp.int32),
            pltpu.VMEM((KYB * PL, 2 * K), BF),
            pltpu.VMEM((6, 64 * PP, 128), F32),
            pltpu.VMEM((K, 128), F32),
            pltpu.VMEM((32, 128), F32),
            pltpu.VMEM((32, 32, 128), BF),
            pltpu.VMEM((32 * 32, 128), F32),
            pltpu.VMEM((TILES, 32, PP, 128), F32),
            pltpu.VMEM((4, 32, PP, K), F32),
            pltpu.VMEM((2, 512, 2 * K), F32),
            pltpu.VMEM((512, 2 * K), BF),
            pltpu.VMEM((512, 2 * K), BF),
            pltpu.VMEM((TILES, 32, 16, 2 * K), BF),
            pltpu.VMEM((TILES, 32, 16, 2 * K), BF),
            pltpu.VMEM((32, 32, 128), BF),
            pltpu.VMEM((TILES, NS, 64, 2 * K), BF),
            pltpu.VMEM((SHARED, NS, 64, 2 * K), BF),
            pltpu.VMEM((NS // 2, PL, 2 * K), BF),
            pltpu.VMEM((NS, NCNT * 32, 128), BF),
            pltpu.VMEM((NS, NCNT * 32, 128), BF),
            pltpu.VMEM((SHARED, 4, PL, 2 * K), BF),
            pltpu.VMEM((SHARED, 4, PL, 2 * K), BF),
            pltpu.VMEM(((KYB + 1) * PL, K), F32),
            pltpu.VMEM((32, 128), F32),
            dma((PP,)), dma, dma, dma, dma, dma, dma((TILES,)), dma((TILES,)),
            dma((TILES,)), dma((TILES,)), dma, dma, dma((SHARED,)), dma((SHARED,)),
        ],
        compiler_params=pltpu.CompilerParams(
            collective_id=0, has_side_effects=True, vmem_limit_bytes=60 * 1024 * 1024
        ),
    )(
        classes, defocus_class, defocus, shifts.T, run_counts, jnp.asarray(left),
        images, jnp.asarray(right), dest_map,
        ref.reshape(KYB * PL, 2 * K),
    )
    return out.reshape(KYB, PL, 2 * K)


def solution(mesh):
    placed = (
        P(("batch", "slab"), None, None),
        P(("batch", "slab")),
        P(("batch", "slab"), None),
        P(("batch", "slab")),
        P(),
        P(("batch", "slab"), None),
        P(),
        P("batch", "slab", None),
    )
    return jax.shard_map(
        per_device, mesh=mesh, in_specs=placed, out_specs=P("batch", "slab", None), check_vma=False
    )
```

```python
import math

import jax
import jax.numpy as jnp
import ml_dtypes
import numpy as np
from jax import lax
from jax.experimental import pallas as pl
from jax.experimental.pallas import tpu as pltpu
from jax.sharding import PartitionSpec as P

TAU_PRIOR = 4.0
PHASE_OFFSET = 0.1
MESH = pl.DeviceIdType.MESH

K = 384
NB = 16
NS = 8
PP = 8
KYB = K // NB
SHARED = 3
TILES = SHARED + 1
PL = 16
NDEF = 16
BF = jnp.bfloat16
F32 = jnp.float32
LAST = SHARED
EXTRA = 13
NCNT = TILES + 3
MOVES = 40
GROUP = 64
TURNS = (
    (0, 1), (1, 0), (0, 3), (3, 0), (1, 1), (1, 3), (3, 3), (3, 1),
    (1, 2), (2, 1), (3, 2), (2, 3), (0, 2), (2, 0), (2, 2),
)


def tables():
    index = np.arange(K)
    angle = 2.0 * np.pi / K * ((index[:, None] * index[None, :]) % K)
    cosine = (np.cos(angle) / math.sqrt(K)).astype(np.float32)
    sine = (np.sin(angle) / math.sqrt(K)).astype(np.float32)

    def left(t):
        rows = [
            KYB * b + (6 * h + 2 * t + 1 + j if t < LAST else 0)
            for h in range(2)
            for b in range(NB)
            for j in range(2)
        ]
        return np.concatenate([cosine[rows], -sine[rows]], axis=0)

    both = np.stack([left(t) for t in range(TILES)], axis=0)
    right = np.concatenate(
        [np.concatenate([cosine, -sine], 1), np.concatenate([sine, cosine], 1)], 0
    )
    kind = ml_dtypes.bfloat16
    return both.astype(kind), right.astype(kind)


def kernel(
    classes, kinds_in, defocus, shifts, counts, left, img_in, right_in, dest_in, ref_in,
    out,
    img, right, dest, ref, scr, cscr, cwide, codes, cf, sc, vx, table_x, table_s, pq, wp, wm,
    sendb, recvb, crecv, zsend, zrecv, zgot, nsend, nrecv, msend, mrecv, wts, tws,
    img_m, right_m, dest_m, ref_m, code_s, code_r, row_s, row_r, z_s, z_r, n_s, n_r, m_s, m_r,
):
    mb = lax.axis_index("batch")
    ms = lax.axis_index("slab")
    core = lax.rem(ms, 2)
    zbase = ms - core
    mz = ms // 2
    me = mb * 2 + core
    my = mb // 4
    mx = lax.rem(mb, 4)

    def peer_of(turn):
        dy, dx = turn
        py = lax.rem(my + jnp.where(core == 0, dy, dx), 4)
        px = lax.rem(mx + jnp.where(core == 0, dx, 4 - dy), 4)
        return py * 4 + px

    barrier = pltpu.get_barrier_semaphore()
    loads = [pltpu.make_async_copy(img_in.at[p], img.at[p], img_m.at[p]) for p in range(PP)]
    load_right = pltpu.make_async_copy(right_in, right, right_m)
    load_dest = pltpu.make_async_copy(dest_in, dest, dest_m)
    load_ref = pltpu.make_async_copy(ref_in, ref, ref_m)
    for load in (*loads, load_dest, load_right, load_ref):
        load.start()

    def greet_plane(q, carry):
        i = lax.rem(me + q, 32)
        pl.semaphore_signal(
            barrier, inc=1, device_id=(i // 2, zbase + lax.rem(i, 2)), device_id_type=MESH
        )
        return carry

    def greet_slab(q, carry):
        pl.semaphore_signal(
            barrier, inc=1, device_id=(mb, lax.rem(ms + q, NS)), device_id_type=MESH
        )
        return carry

    lax.fori_loop(1, 32, greet_plane, 0)
    lax.fori_loop(1, NS, greet_slab, 0)

    def pick(index, values):
        got = jnp.full(index.shape, values[0])
        for i, value in enumerate(values[1:], 1):
            got = jnp.where(index == i, value, got)
        return got

    def square(k):
        half = jnp.where(k >= K // 2, k - K, k).astype(F32) * (1.0 / K)
        return half * half

    def phase(k, shift):
        turn = k.astype(F32) * shift
        turn = turn - K * jnp.floor((turn + 0.5) * (1.0 / K))
        return turn * (2.0 * math.pi / K)

    def to_plane(b, h, src, dst, send_sem, recv_sem):
        pltpu.make_async_remote_copy(
            src_ref=src, dst_ref=dst, send_sem=send_sem, recv_sem=recv_sem,
            device_id=(b, zbase + h), device_id_type=MESH,
        ).start()

    def compute(t):
        table = left[t]

        def one(p, carry):
            @pl.when(t == 0)
            def _():
                pltpu.make_async_copy(img_in.at[p], img.at[p], img_m.at[p]).wait()

            sec = jnp.dot(table, img[p], preferred_element_type=F32)
            for g in range(3):
                cols = slice(g * 128, (g + 1) * 128)
                scr[g, pl.ds(p, 64, stride=8), :] = sec[:64, cols]
                scr[3 + g, pl.ds(p, 64, stride=8), :] = sec[64:, cols]
            return carry

        lax.fori_loop(0, PP, one, 0)

        def pack(i, carry):
            start = pl.multiple_of(i * 16, 16)
            target = lax.rem(i, NB) * 2 + i // NB
            for g in range(6):
                sendb[t, target, :, pl.ds(g * 128, 128)] = scr[g, pl.ds(start, 16), :].astype(BF)
            return carry

        lax.fori_loop(0, 32, pack, 0)

    other = 1 - core

    def send_rows(t):
        to_plane(mb, other, sendb.at[t, mb * 2 + other], recvb.at[t, me], row_s.at[t], row_r.at[t])
        pltpu.make_async_copy(sendb.at[t, me], recvb.at[t, me], row_r.at[t]).start()
        for flip in range(2):
            h = core if flip == 0 else other
            for turn in TURNS:
                b = peer_of(turn)
                to_plane(b, h, sendb.at[t, b * 2 + h], recvb.at[t, me], row_s.at[t], row_r.at[t])

    def send_last():
        t = LAST

        @pl.when(core == 0)
        def _():
            pltpu.make_async_copy(sendb.at[t, me], recvb.at[t, me], row_r.at[t]).start()

        @pl.when(core == 1)
        def _():
            to_plane(mb, 0, sendb.at[t, mb * 2], recvb.at[t, me], row_s.at[t], row_r.at[t])

        for turn in TURNS:
            b = peer_of(turn)
            to_plane(b, 0, sendb.at[t, b * 2], recvb.at[t, me], row_s.at[t], row_r.at[t])

    sub_p = lax.broadcasted_iota(jnp.int32, (PP, K), 0)
    col = lax.broadcasted_iota(jnp.int32, (PP, K), 1)
    row8 = lax.broadcasted_iota(jnp.int32, (PP, 128), 0)
    lane8 = lax.broadcasted_iota(jnp.int32, (PP, 128), 1)

    def tell():
        load_dest.wait()
        end = counts[:, 0:1]
        slab = jnp.zeros((PP, K), jnp.int32)
        for i in range(1, NS):
            slab = slab + jnp.where(col >= end, 1, 0)
            end = end + counts[:, i : i + 1]
        plane = pick(sub_p, [dest[pl.ds(classes[p], 1), :] for p in range(PP)])
        place = slab * 32 + plane
        spread = jnp.where(lax.rem(lane8, PP) == row8, 1.0, 0.0)
        kind8 = pick(row8, [kinds_in[p] for p in range(PP)])

        def turned(x):
            return lax.dot_general(
                x.astype(F32), spread, (((0,), (0,)), ((), ())),
                precision=lax.Precision.HIGHEST, preferred_element_type=F32,
            )

        cscr[...] = turned(place)
        shift_x = pick(row8, [shifts[0, p] for p in range(PP)])
        shift_y = pick(row8, [shifts[1, p] for p in range(PP)])
        person = turned(pick(lane8, [kind8, shift_x, shift_y]))
        slot_one = (lax.broadcasted_iota(jnp.int32, (1, 128), 1) // PP) & 1

        def arrange(d, carry):
            base = d // 2 * KYB
            step = 6 * lax.rem(d, 2)
            for n in range(TILES + SHARED + 3):
                for_two = []
                for j in range(2):
                    if n < SHARED:
                        ky = base + step + 2 * n + 1 + j
                    elif n == LAST:
                        ky = base
                    elif n < TILES + SHARED:
                        ky = K - (base + step + 2 * (n - TILES) + 1 + j)
                    else:
                        ky = jnp.minimum(base + EXTRA + step + 2 * (n - TILES - SHARED) + j, K - 1)
                    for_two.append(cscr[pl.ds(ky, 1), :])
                cwide[n : n + 1, :] = jnp.where(slot_one == 0, for_two[0], for_two[1] + PL)
            codes[d] = cwide[...].astype(BF)
            return carry

        cwide[...] = jnp.zeros_like(cwide)
        cwide[10:13, :] = person[0:3]
        lax.fori_loop(0, 2 * NB, arrange, 0)

        def send_codes(q, carry):
            i = lax.rem(me + q, 32)
            to_plane(i // 2, lax.rem(i, 2), codes.at[i], crecv.at[me], code_s, code_r)
            return carry

        pltpu.make_async_copy(codes.at[me], crecv.at[me], code_r).start()
        lax.fori_loop(1, 32, send_codes, 0)


    def produce(t, carry):
        compute(t)

        @pl.when(t == 0)
        def _():
            pl.semaphore_wait(barrier, 31 + NS - 1)

        @pl.when(t < LAST)
        def _():
            send_rows(t)

        pl.when(t == LAST)(send_last)
        pl.when(t == 0)(tell)
        return carry

    lax.fori_loop(0, TILES, produce, 0)

    pltpu.make_async_copy(crecv, crecv, code_r).wait()

    def widen(i, carry):
        cf[pl.ds(pl.multiple_of(i * 16, 16), 16), :] = crecv[i].astype(F32)
        return carry

    lax.fori_loop(0, 32, widen, 0)

    lane = lax.broadcasted_iota(jnp.int32, (32, 128), 1)
    sub = lax.broadcasted_iota(jnp.int32, (32, 128), 0)
    mine = (lane // 16) == lax.rem(sub, 8)

    def pair_codes(row):
        got = cf[pl.ds(row, 32, stride=16), :]
        return jnp.sum(jnp.where(mine, got, 0.0).reshape(4, 8, 128), axis=1)

    spot = lax.broadcasted_iota(jnp.int32, (256, 128), 0).astype(F32)

    def one_hot(code4):
        return jnp.concatenate(
            [
                jnp.where(spot == code4[g : g + 1, :], 1.0, 0.0).astype(BF)
                for g in range(4)
            ],
            axis=1,
        )

    row_id = lax.broadcasted_iota(jnp.int32, (128, 128), 0)
    row_class = jnp.where(row_id < 3 * NDEF, lax.rem(row_id, NDEF), -1).astype(F32)
    kind4 = pair_codes(10)
    kinds = jnp.concatenate(
        [jnp.where(row_class == kind4[g : g + 1, :], 1.0, 0.0).astype(BF) for g in range(4)],
        axis=1,
    )

    def count(n, carry):
        tally = lax.dot_general(
            one_hot(pair_codes(jnp.where(n < TILES, n, n + SHARED))), kinds,
            (((1,), (1,)), ((), ())), preferred_element_type=F32,
        )
        start = pl.multiple_of(n * 32, 32)
        nsend[:, pl.ds(start, 32), :] = tally.astype(BF).reshape(NS, 32, 128)
        return carry

    lax.fori_loop(0, NCNT, count, 0)

    def to_slab(q, src, dst, send_sem, recv_sem):
        peer = lax.rem(ms + q, NS)
        pltpu.make_async_remote_copy(
            src_ref=src(peer), dst_ref=dst, send_sem=send_sem, recv_sem=recv_sem,
            device_id=(mb, peer), device_id_type=MESH,
        ).start()

    pltpu.make_async_copy(nsend.at[ms], nrecv.at[ms], n_r).start()
    def send_counts(q, carry):
        to_slab(q, lambda peer: nsend.at[peer], nrecv.at[ms], n_s, n_r)
        return carry

    lax.fori_loop(1, NS, send_counts, 0)

    slot_of = (lane8 // 8) * 2 + (lane8 & 1)
    part = (lane8 // 2) & 3
    slot_ky = mb * KYB + jnp.where(slot_of < 2 * SHARED, 6 * core + 1 + slot_of, 0)
    slot_sq = square(slot_ky)
    every = [defocus[i] for i in range(NDEF)]

    def three(x):
        high = x.astype(BF)
        mid = (x - high.astype(F32)).astype(BF)
        low = (x - high.astype(F32) - mid.astype(F32)).astype(BF)
        return jnp.concatenate([high, mid, low], axis=0)

    def rows_of(shape, axis=0):
        return lax.broadcasted_iota(jnp.int32, shape, axis)

    def tabulate():
        turn = phase(rows_of((MOVES, K), 1), (rows_of((MOVES, K)) - 16).astype(F32))
        arg = pick(rows_of((NDEF, K)), every) * square(rows_of((NDEF, K), 1))
        spare = GROUP - MOVES - NDEF
        for n, (move, kind) in enumerate(
            (
                (jnp.cos(turn), None),
                (-jnp.sin(turn), None),
                (None, jnp.sin(arg)),
                (None, jnp.cos(arg)),
            )
        ):
            move = jnp.zeros((MOVES, K), F32) if move is None else move
            kind = jnp.zeros((NDEF, K), F32) if kind is None else kind
            full = jnp.concatenate([move, kind, jnp.zeros((spare, K), F32)], axis=0)
            table_x[:, pl.ds(n * K, K)] = three(full)
        turn = phase(slot_ky[0:1], (rows_of((MOVES, 128)) - 16).astype(F32))
        arg = pick(rows_of((NDEF, 128)), every) * slot_sq[0:1] + PHASE_OFFSET
        kind = part[0:1]
        move = jnp.where(kind == 2, -jnp.cos(turn), jnp.where(kind == 3, jnp.sin(turn), 0.0))
        tone = jnp.where(kind == 0, jnp.sin(arg), jnp.where(kind == 1, jnp.cos(arg), 0.0))
        table_s[...] = three(
            jnp.concatenate([move, tone, jnp.zeros((spare, 128), F32)], axis=0)
        )

    entry = (rows_of((3 * GROUP, 128)) & (GROUP - 1)).astype(F32)

    def chosen(move4, table):
        hot = jnp.concatenate(
            [
                jnp.where(
                    (entry == move4[g : g + 1, :] + 16.0)
                    | (entry == kind4[g : g + 1, :] + float(MOVES)),
                    1.0,
                    0.0,
                ).astype(BF)
                for g in range(4)
            ],
            axis=1,
        )
        return lax.dot_general(
            hot, table, (((0,), (0,)), ((), ())), preferred_element_type=F32
        )

    tabulate()
    vx[...] = chosen(pair_codes(11), table_x[...])
    scal = chosen(pair_codes(12), table_s[...])
    sc[0] = scal
    for t in range(1, TILES):
        sc[t] = pltpu.roll(scal, 128 - 8 * t, 1)

    load_right.wait()

    def process(t):
        pltpu.make_async_copy(recvb.at[t], recvb.at[t], row_r.at[t]).wait()

        def half(m, carry):
            block = recvb[t, pl.ds(m * 16, 16)].reshape(256, 2 * K)
            start = pl.multiple_of(m * 256, 256)
            pq[0, pl.ds(start, 256), :] = jnp.dot(
                block[:, :K], right[pl.ds(0, K), :], preferred_element_type=F32
            )
            pq[1, pl.ds(start, 256), :] = jnp.dot(
                block[:, K:], right[pl.ds(K, K), :], preferred_element_type=F32
            )
            return carry

        lax.fori_loop(0, 2, half, 0)

        def weigh(i, carry):
            got = [[], [], [], []]
            for j in range(2):
                rows = pl.ds(pl.multiple_of(i * 16 + j * 8, 8), 8)
                scal = sc[t, rows, :]
                sa, ca, er, ei = [scal[:, 2 * n + j : 2 * n + j + 1] for n in range(4)]
                exr, exi, sb, cb = [vx[rows, pl.ds(n * K, K)] for n in range(4)]
                pr, pi = pq[0, rows, pl.ds(0, K)], pq[0, rows, pl.ds(K, K)]
                qr, qi = pq[1, rows, pl.ds(0, K)], pq[1, rows, pl.ds(K, K)]
                ctf = sa * cb + ca * sb
                gr, gi = ctf * exr, ctf * exi
                fa, fb, fc, fd = er * gr, ei * gi, er * gi, ei * gr
                sr, si = pr + qr, pi + qi
                fr, fi = fa - fb, fc + fd
                got[0].append(sr * fr - si * fi)
                got[1].append(sr * fi + si * fr)
                sr, si = pr - qr, pi - qi
                fr, fi = fa + fb, fc - fd
                got[2].append(sr * fr - si * fi)
                got[3].append(sr * fi + si * fr)
            rows = pl.ds(pl.multiple_of(i * 16, 16), 16)
            for n in range(4):
                to = wp if n < 2 else wm
                to[rows, pl.ds((n % 2) * K, K)] = jnp.concatenate(got[n], axis=0).astype(BF)
            return carry

        lax.fori_loop(0, 32, weigh, 0, unroll=2)

        def total(hot, rows):
            return jnp.dot(hot, rows, preferred_element_type=F32).astype(BF).reshape(NS, 32, 2 * K)

        zsend[t, :, pl.ds(0, 32), :] = total(one_hot(pair_codes(t)), wp[...])

        @pl.when(t < LAST)
        def _():
            zsend[t, :, pl.ds(32, 32), :] = total(one_hot(pair_codes(TILES + t)), wm[...])

            def send(q, carry):
                to_slab(q, lambda peer: zsend.at[t, peer], zrecv.at[t, ms], z_s.at[t], z_r.at[t])
                return carry

            lax.fori_loop(1, NS, send, 0)
            pltpu.make_async_copy(zsend.at[t, ms], zrecv.at[t, ms], z_r.at[t]).start()

        @pl.when(t == LAST)
        def _():
            top = pl.ds(0, PL)

            def send(q, carry):
                to_slab(q, lambda peer: zsend.at[t, peer, top], zgot.at[mz], z_s.at[t], z_r.at[t])
                return carry

            lax.fori_loop(1, NS, send, 0)
            pltpu.make_async_copy(zsend.at[t, ms, top], zgot.at[mz], z_r.at[t]).start()

    def weights():
        lane_k = lax.broadcasted_iota(jnp.int32, (32, 128), 1)
        own_ky = mb * KYB + lax.broadcasted_iota(jnp.int32, (32, 128), 0)
        arg2_y = 2.0 * (pick(lane_k & (NDEF - 1), every) * square(own_ky) + PHASE_OFFSET)
        group = lane_k // NDEF
        tws[...] = jnp.where(
            group == 0,
            -0.5 * jnp.cos(arg2_y),
            jnp.where(group == 1, 0.5 * jnp.sin(arg2_y), jnp.where(group == 2, 0.5, 0.0)),
        )
        row_k = lax.broadcasted_iota(jnp.int32, (NDEF, K), 0)
        col_k = lax.broadcasted_iota(jnp.int32, (NDEF, K), 1)
        arg2_x = 2.0 * (pick(row_k, every) * square(col_k))
        rw = jnp.concatenate(
            [
                jnp.cos(arg2_x),
                jnp.sin(arg2_x),
                jnp.ones((NDEF, K), F32),
                jnp.zeros((128 - 3 * NDEF, K), F32),
            ],
            axis=0,
        )
        pltpu.make_async_copy(nrecv, nrecv, n_r).wait()

        def one(h, carry):
            x = nrecv[h].astype(F32)
            for z in range(1, NS // 2):
                x += nrecv[2 * z + h].astype(F32)
            own, more = 6 * h + 1, 6 * h + EXTRA

            def times(part, i, rows):
                return (part.reshape(rows, PL, 128) * tws[pl.ds(i, rows), :][:, None, :]).reshape(
                    rows * PL, 128
                )

            scaled = jnp.concatenate(
                [times(x[:96], own, 6), times(x[96:128], 0, 2), times(x[128:], more, 6)], axis=0
            )
            res = jnp.dot(
                scaled, rw, precision=lax.Precision.HIGHEST, preferred_element_type=F32
            )
            res = 1.0 / (res + TAU_PRIOR)
            wts[pl.ds(pl.multiple_of(own * PL, PL), 96), :] = res[:96]
            wts[pl.ds(pl.multiple_of(more * PL, PL), 96), :] = res[128:]

            @pl.when(h == 0)
            def _():
                wts[pl.ds(0, PL), :] = res[96:112]

            return carry

        lax.fori_loop(0, 2, one, 0)

    def finish(i, sums):
        rows = pl.ds(pl.multiple_of(i * PL, PL), PL)
        inverse = wts[rows, :]
        for h in range(2):
            cols = pl.ds(h * K, K)
            top = TAU_PRIOR * ref[rows, cols].astype(F32) + sums[:, h * K : (h + 1) * K]
            out[rows, cols] = (top * inverse).astype(BF)

    def gather(t):
        pltpu.make_async_copy(zrecv.at[t], zrecv.at[t], z_r.at[t]).wait()

        def over_z(h, start):
            rows = pl.ds(pl.multiple_of(start, PL), PL)
            x = zrecv[t, h, rows, :].astype(F32)
            for z in range(1, NS // 2):
                x += zrecv[t, 2 * z + h, rows, :].astype(F32)
            return x

        def mirror(m, carry):
            msend[t, m] = over_z(m // 2, 2 * PL + lax.rem(m, 2) * PL).astype(BF)
            return carry

        lax.fori_loop(0, 4, mirror, 0)
        pltpu.make_async_remote_copy(
            src_ref=msend.at[t], dst_ref=mrecv.at[t], send_sem=m_s.at[t], recv_sem=m_r.at[t],
            device_id=(NB - 1 - mb, ms), device_id_type=MESH,
        ).start()

        def own(m, carry):
            h, j = m // 2, lax.rem(m, 2)
            finish(6 * h + 2 * t + 1 + j, over_z(h, j * PL))
            return carry

        lax.fori_loop(0, 4, own, 0)

    def drain(src, send_sem, recv_sem):
        return pltpu.make_async_remote_copy(
            src_ref=src, dst_ref=src, send_sem=send_sem, recv_sem=recv_sem,
            device_id=(mb, ms), device_id_type=MESH,
        )

    def mirrored(t, carry):
        drain(msend.at[t], m_s.at[t], m_r.at[t]).wait()

        def one(m, inner):
            i = 6 * (m // 2) + 2 * t + 1 + lax.rem(m, 2)

            @pl.when(i < KYB // 2)
            def _():
                finish(KYB - i, mrecv[t, m].astype(F32))

            return inner

        lax.fori_loop(0, 4, one, 0)
        return carry

    def consume(t, carry):
        @pl.when(jnp.logical_or(t < LAST, core == 0))
        def _():
            process(t)

        pl.when(t == 0)(weights)

        @pl.when(t > 0)
        def _():
            gather(t - 1)

        @pl.when(t > 1)
        def _():
            mirrored(t - 2, 0)

        return carry

    load_ref.wait()
    lax.fori_loop(0, TILES, consume, 0)

    pltpu.make_async_copy(zgot, zgot, z_r.at[LAST]).wait()
    x = zgot[0].astype(F32)
    for z in range(1, NS // 2):
        x += zgot[z].astype(F32)
    finish(0, x)

    mirrored(SHARED - 1, 0)

    drain(crecv.at[pl.ds(0, 31)], code_s, code_r).wait_send()
    drain(nsend.at[pl.ds(0, 7)], n_s, n_r).wait_send()
    def drain_tile(t, carry):
        drain(sendb.at[t, pl.ds(0, 31)], row_s.at[t], row_r.at[t]).wait_send()
        drain(zsend.at[t, pl.ds(0, 7)], z_s.at[t], z_r.at[t]).wait_send()
        return carry

    lax.fori_loop(0, SHARED, drain_tile, 0)

    @pl.when(core == 0)
    def _():
        drain(sendb.at[LAST, pl.ds(0, 15)], row_s.at[LAST], row_r.at[LAST]).wait_send()
        drain(zsend.at[LAST, pl.ds(0, 7), pl.ds(0, PL)], z_s.at[LAST], z_r.at[LAST]).wait_send()

    @pl.when(core == 1)
    def _():
        drain(sendb.at[LAST, pl.ds(0, 16)], row_s.at[LAST], row_r.at[LAST]).wait_send()


def per_device(images, classes, shifts, defocus_class, defocus, run_counts, dest_map, ref):
    left, right = tables()
    vmem = pl.BlockSpec(memory_space=pltpu.VMEM)
    smem = pl.BlockSpec(memory_space=pltpu.SMEM)
    far = pl.BlockSpec(memory_space=pl.ANY)
    dma = pltpu.SemaphoreType.DMA
    out = pl.pallas_call(
        kernel,
        out_shape=jax.ShapeDtypeStruct((KYB * PL, 2 * K), BF),
        in_specs=[smem] * 4 + [vmem] * 2 + [far] * 4,
        out_specs=vmem,
        scratch_shapes=[
            pltpu.VMEM((PP, K, K), BF),
            pltpu.VMEM((2 * K, 2 * K), BF),
            pltpu.VMEM(dest_map.shape, jnp.int32),
            pltpu.VMEM((KYB * PL, 2 * K), BF),
            pltpu.VMEM((6, 64 * PP, 128), F32),
            pltpu.VMEM((K, 128), F32),
            pltpu.VMEM((16, 128), F32),
            pltpu.VMEM((32, 16, 128), BF),
            pltpu.VMEM((32 * 16, 128), F32),
            pltpu.VMEM((TILES, 512, 128), F32),
            pltpu.VMEM((512, 4 * K), F32),
            pltpu.VMEM((3 * GROUP, 4 * K), BF),
            pltpu.VMEM((3 * GROUP, 128), BF),
            pltpu.VMEM((2, 512, 2 * K), F32),
            pltpu.VMEM((512, 2 * K), BF),
            pltpu.VMEM((512, 2 * K), BF),
            pltpu.VMEM((TILES, 32, 16, 2 * K), BF),
            pltpu.VMEM((TILES, 32, 16, 2 * K), BF),
            pltpu.VMEM((32, 16, 128), BF),
            pltpu.VMEM((TILES, NS, 64, 2 * K), BF),
            pltpu.VMEM((SHARED, NS, 64, 2 * K), BF),
            pltpu.VMEM((NS // 2, PL, 2 * K), BF),
            pltpu.VMEM((NS, NCNT * 32, 128), BF),
            pltpu.VMEM((NS, NCNT * 32, 128), BF),
            pltpu.VMEM((SHARED, 4, PL, 2 * K), BF),
            pltpu.VMEM((SHARED, 4, PL, 2 * K), BF),
            pltpu.VMEM(((KYB + 1) * PL, K), F32),
            pltpu.VMEM((32, 128), F32),
            dma((PP,)), dma, dma, dma, dma, dma, dma((TILES,)), dma((TILES,)),
            dma((TILES,)), dma((TILES,)), dma, dma, dma((SHARED,)), dma((SHARED,)),
        ],
        compiler_params=pltpu.CompilerParams(
            collective_id=0, has_side_effects=True, vmem_limit_bytes=60 * 1024 * 1024
        ),
    )(
        classes, defocus_class, defocus, shifts.T, run_counts, jnp.asarray(left),
        images, jnp.asarray(right), dest_map,
        ref.reshape(KYB * PL, 2 * K),
    )
    return out.reshape(KYB, PL, 2 * K)


def solution(mesh):
    placed = (
        P(("batch", "slab"), None, None),
        P(("batch", "slab")),
        P(("batch", "slab"), None),
        P(("batch", "slab")),
        P(),
        P(("batch", "slab"), None),
        P(),
        P("batch", "slab", None),
    )
    return jax.shard_map(
        per_device, mesh=mesh, in_specs=placed, out_specs=P("batch", "slab", None), check_vma=False
    )
```

```python
import math

import jax
import jax.numpy as jnp
import ml_dtypes
import numpy as np
from jax import lax
from jax.experimental import pallas as pl
from jax.experimental.pallas import tpu as pltpu
from jax.sharding import PartitionSpec as P

TAU_PRIOR = 4.0
PHASE_OFFSET = 0.1
MESH = pl.DeviceIdType.MESH

K = 384
NB = 16
NS = 8
PP = 8
KYB = K // NB
SHARED = 3
TILES = SHARED + 1
PL = 16
NDEF = 16
BF = jnp.bfloat16
F32 = jnp.float32
LAST = SHARED
EXTRA = 13
HOPS = ((1, 0), (3, 1), (2, 0), (3, 0), (1, 1), (2, 1), (0, 1))
NCNT = TILES + 3
MOVES = 40
GROUP = 64
TURNS = (
    (0, 1), (1, 0), (0, 3), (3, 0), (1, 1), (1, 3), (3, 3), (3, 1),
    (1, 2), (2, 1), (3, 2), (2, 3), (0, 2), (2, 0), (2, 2),
)


def tables():
    index = np.arange(K)
    angle = 2.0 * np.pi / K * ((index[:, None] * index[None, :]) % K)
    cosine = (np.cos(angle) / math.sqrt(K)).astype(np.float32)
    sine = (np.sin(angle) / math.sqrt(K)).astype(np.float32)

    def left(t):
        rows = [
            KYB * b + (6 * h + 2 * t + 1 + j if t < LAST else 0)
            for h in range(2)
            for b in range(NB)
            for j in range(2)
        ]
        return np.concatenate([cosine[rows], -sine[rows]], axis=0)

    both = np.stack([left(t) for t in range(TILES)], axis=0)
    right = np.concatenate(
        [np.concatenate([cosine, -sine], 1), np.concatenate([sine, cosine], 1)], 0
    )
    kind = ml_dtypes.bfloat16
    return both.astype(kind), right.astype(kind)


def kernel(
    classes, kinds_in, defocus, shifts, counts, left, img_in, right_in, dest_in, ref_in,
    out,
    img, right, dest, ref, scr, cscr, cwide, codes, cf, sc, vx, table_x, table_s, pq, wp, wm,
    sendb, recvb, crecv, zsend, zrecv, zgot, nsend, nrecv, msend, mrecv, wts, tws,
    img_m, right_m, dest_m, ref_m, code_s, code_r, row_s, row_r, z_s, z_r, n_s, n_r, m_s, m_r,
):
    mb = lax.axis_index("batch")
    ms = lax.axis_index("slab")
    core = lax.rem(ms, 2)
    zbase = ms - core
    mz = ms // 2
    me = mb * 2 + core
    my = mb // 4
    mx = lax.rem(mb, 4)

    def peer_of(turn):
        dy, dx = turn
        py = lax.rem(my + jnp.where(core == 0, dy, dx), 4)
        px = lax.rem(mx + jnp.where(core == 0, dx, 4 - dy), 4)
        return py * 4 + px

    barrier = pltpu.get_barrier_semaphore()
    loads = [pltpu.make_async_copy(img_in.at[p], img.at[p], img_m.at[p]) for p in range(PP)]
    load_right = pltpu.make_async_copy(right_in, right, right_m)
    load_dest = pltpu.make_async_copy(dest_in, dest, dest_m)
    load_ref = pltpu.make_async_copy(ref_in, ref, ref_m)
    for load in (*loads, load_dest, load_right, load_ref):
        load.start()

    def greet_plane(q, carry):
        i = lax.rem(me + q, 32)
        pl.semaphore_signal(
            barrier, inc=1, device_id=(i // 2, zbase + lax.rem(i, 2)), device_id_type=MESH
        )
        return carry

    def greet_slab(q, carry):
        pl.semaphore_signal(
            barrier, inc=1, device_id=(mb, lax.rem(ms + q, NS)), device_id_type=MESH
        )
        return carry

    lax.fori_loop(1, 32, greet_plane, 0)
    lax.fori_loop(1, NS, greet_slab, 0)

    def pick(index, values):
        got = jnp.full(index.shape, values[0])
        for i, value in enumerate(values[1:], 1):
            got = jnp.where(index == i, value, got)
        return got

    def square(k):
        half = jnp.where(k >= K // 2, k - K, k).astype(F32) * (1.0 / K)
        return half * half

    def phase(k, shift):
        turn = k.astype(F32) * shift
        turn = turn - K * jnp.floor((turn + 0.5) * (1.0 / K))
        return turn * (2.0 * math.pi / K)

    def to_plane(b, h, src, dst, send_sem, recv_sem):
        pltpu.make_async_remote_copy(
            src_ref=src, dst_ref=dst, send_sem=send_sem, recv_sem=recv_sem,
            device_id=(b, zbase + h), device_id_type=MESH,
        ).start()

    def compute(t):
        table = left[t]

        def one(p, carry):
            @pl.when(t == 0)
            def _():
                pltpu.make_async_copy(img_in.at[p], img.at[p], img_m.at[p]).wait()

            sec = jnp.dot(table, img[p], preferred_element_type=F32)
            for g in range(3):
                cols = slice(g * 128, (g + 1) * 128)
                scr[g, pl.ds(p, 64, stride=8), :] = sec[:64, cols]
                scr[3 + g, pl.ds(p, 64, stride=8), :] = sec[64:, cols]
            return carry

        lax.fori_loop(0, PP, one, 0)

        def pack(i, carry):
            start = pl.multiple_of(i * 16, 16)
            target = lax.rem(i, NB) * 2 + i // NB
            for g in range(6):
                sendb[t, target, :, pl.ds(g * 128, 128)] = scr[g, pl.ds(start, 16), :].astype(BF)
            return carry

        lax.fori_loop(0, 32, pack, 0)

    other = 1 - core

    def send_rows(t):
        for h in range(2):
            own = recvb.at[t, me]

            @pl.when(core == h)
            def _():
                pltpu.make_async_copy(sendb.at[t, me], own, row_r.at[t]).start()

            @pl.when(core != h)
            def _():
                to_plane(mb, h, sendb.at[t, mb * 2 + h], own, row_s.at[t], row_r.at[t])

            for turn in TURNS:
                b = peer_of(turn)
                to_plane(b, h, sendb.at[t, b * 2 + h], own, row_s.at[t], row_r.at[t])

    def send_last():
        t = LAST

        @pl.when(core == 0)
        def _():
            pltpu.make_async_copy(sendb.at[t, me], recvb.at[t, me], row_r.at[t]).start()

        @pl.when(core == 1)
        def _():
            to_plane(mb, 0, sendb.at[t, mb * 2], recvb.at[t, me], row_s.at[t], row_r.at[t])

        for turn in TURNS:
            b = peer_of(turn)
            to_plane(b, 0, sendb.at[t, b * 2], recvb.at[t, me], row_s.at[t], row_r.at[t])

    sub_p = lax.broadcasted_iota(jnp.int32, (PP, K), 0)
    col = lax.broadcasted_iota(jnp.int32, (PP, K), 1)
    row8 = lax.broadcasted_iota(jnp.int32, (PP, 128), 0)
    lane8 = lax.broadcasted_iota(jnp.int32, (PP, 128), 1)

    def tell():
        load_dest.wait()
        end = counts[:, 0:1]
        slab = jnp.zeros((PP, K), jnp.int32)
        for i in range(1, NS):
            slab = slab + jnp.where(col >= end, 1, 0)
            end = end + counts[:, i : i + 1]
        plane = pick(sub_p, [dest[pl.ds(classes[p], 1), :] for p in range(PP)])
        place = slab * 32 + plane
        spread = jnp.where(lax.rem(lane8, PP) == row8, 1.0, 0.0)
        kind8 = pick(row8, [kinds_in[p] for p in range(PP)])

        def turned(x):
            return lax.dot_general(
                x.astype(F32), spread, (((0,), (0,)), ((), ())),
                precision=lax.Precision.HIGHEST, preferred_element_type=F32,
            )

        cscr[...] = turned(place)
        shift_x = pick(row8, [shifts[0, p] for p in range(PP)])
        shift_y = pick(row8, [shifts[1, p] for p in range(PP)])
        person = turned(pick(lane8, [kind8, shift_x, shift_y]))
        slot_one = (lax.broadcasted_iota(jnp.int32, (1, 128), 1) // PP) & 1

        def arrange(d, carry):
            base = d // 2 * KYB
            step = 6 * lax.rem(d, 2)
            for n in range(TILES + SHARED + 3):
                for_two = []
                for j in range(2):
                    if n < SHARED:
                        ky = base + step + 2 * n + 1 + j
                    elif n == LAST:
                        ky = base
                    elif n < TILES + SHARED:
                        ky = K - (base + step + 2 * (n - TILES) + 1 + j)
                    else:
                        ky = jnp.minimum(base + EXTRA + step + 2 * (n - TILES - SHARED) + j, K - 1)
                    for_two.append(cscr[pl.ds(ky, 1), :])
                cwide[n : n + 1, :] = jnp.where(slot_one == 0, for_two[0], for_two[1] + PL)
            codes[d] = cwide[...].astype(BF)
            return carry

        cwide[...] = jnp.zeros_like(cwide)
        cwide[10:13, :] = person[0:3]
        lax.fori_loop(0, 2 * NB, arrange, 0)

        def send_codes(q, carry):
            i = lax.rem(me + q, 32)
            to_plane(i // 2, lax.rem(i, 2), codes.at[i], crecv.at[me], code_s, code_r)
            return carry

        pltpu.make_async_copy(codes.at[me], crecv.at[me], code_r).start()
        lax.fori_loop(1, 32, send_codes, 0)


    def produce(t, carry):
        compute(t)

        @pl.when(t == 0)
        def _():
            pl.semaphore_wait(barrier, 31 + NS - 1)

        send_rows(t)
        pl.when(t == 0)(tell)
        return carry

    lax.fori_loop(0, 2, produce, 0)

    pltpu.make_async_copy(crecv, crecv, code_r).wait()

    def widen(i, carry):
        cf[pl.ds(pl.multiple_of(i * 16, 16), 16), :] = crecv[i].astype(F32)
        return carry

    lax.fori_loop(0, 32, widen, 0)

    lane = lax.broadcasted_iota(jnp.int32, (32, 128), 1)
    sub = lax.broadcasted_iota(jnp.int32, (32, 128), 0)
    mine = (lane // 16) == lax.rem(sub, 8)

    def pair_codes(row):
        got = cf[pl.ds(row, 32, stride=16), :]
        return jnp.sum(jnp.where(mine, got, 0.0).reshape(4, 8, 128), axis=1)

    spot = lax.broadcasted_iota(jnp.int32, (256, 128), 0).astype(F32)

    def one_hot(code4):
        return jnp.concatenate(
            [
                jnp.where(spot == code4[g : g + 1, :], 1.0, 0.0).astype(BF)
                for g in range(4)
            ],
            axis=1,
        )

    def to_slab(src, dst, send_sem, recv_sem):
        for dz, flip in HOPS:
            z = lax.rem(mz + jnp.where(core == 0, dz, 4 - dz), 4)
            peer = z * 2 + (1 - core if flip else core)
            pltpu.make_async_remote_copy(
                src_ref=src(peer), dst_ref=dst, send_sem=send_sem, recv_sem=recv_sem,
                device_id=(mb, peer), device_id_type=MESH,
            ).start()

    kind4 = pair_codes(10)

    def tally():
        spot_z = lax.broadcasted_iota(jnp.int32, (128, 128), 0).astype(F32)
        slot_k = ((lax.broadcasted_iota(jnp.int32, (4, 128), 1) // PP) & 1).astype(F32)
        which = kind4 + NDEF * slot_k

        def hot(code4):
            return jnp.concatenate(
                [
                    jnp.where(spot_z == code4[g : g + 1, :], 1.0, 0.0).astype(BF)
                    for g in range(4)
                ],
                axis=1,
            )

        def one(n, acc):
            code4 = pair_codes(jnp.where(n < TILES, n, n + SHARED))
            flat = code4 - 16.0 * jnp.floor(code4 * (1.0 / 16)) + 16.0 * jnp.floor(code4 * (1.0 / 32))
            group = ((n & 3) * 2 * NDEF).astype(F32)
            return acc + lax.dot_general(
                hot(flat), hot(which + group), (((1,), (1,)), ((), ())), preferred_element_type=F32
            )

        for half, (low, high) in enumerate(((0, 4), (4, NCNT))):
            acc = lax.fori_loop(low, high, one, jnp.zeros((128, 128), F32))
            nsend[:, :, pl.ds(half * 128, 128)] = acc.astype(BF).reshape(NS, PL, 128)
        to_slab(lambda peer: nsend.at[peer], nrecv.at[ms], n_s, n_r)
        pltpu.make_async_copy(nsend.at[ms], nrecv.at[ms], n_r).start()

    slot_of = (lane8 // 8) * 2 + (lane8 & 1)
    part = (lane8 // 2) & 3
    slot_ky = mb * KYB + jnp.where(slot_of < 2 * SHARED, 6 * core + 1 + slot_of, 0)
    slot_sq = square(slot_ky)
    every = [defocus[i] for i in range(NDEF)]

    def three(x):
        high = x.astype(BF)
        mid = (x - high.astype(F32)).astype(BF)
        low = (x - high.astype(F32) - mid.astype(F32)).astype(BF)
        return jnp.concatenate([high, mid, low], axis=0)

    def rows_of(shape, axis=0):
        return lax.broadcasted_iota(jnp.int32, shape, axis)

    def tabulate():
        turn = phase(rows_of((MOVES, K), 1), (rows_of((MOVES, K)) - 16).astype(F32))
        arg = pick(rows_of((NDEF, K)), every) * square(rows_of((NDEF, K), 1))
        spare = GROUP - MOVES - NDEF
        for n, (move, kind) in enumerate(
            (
                (jnp.cos(turn), None),
                (-jnp.sin(turn), None),
                (None, jnp.sin(arg)),
                (None, jnp.cos(arg)),
            )
        ):
            move = jnp.zeros((MOVES, K), F32) if move is None else move
            kind = jnp.zeros((NDEF, K), F32) if kind is None else kind
            full = jnp.concatenate([move, kind, jnp.zeros((spare, K), F32)], axis=0)
            table_x[:, pl.ds(n * K, K)] = three(full)
        turn = phase(slot_ky[0:1], (rows_of((MOVES, 128)) - 16).astype(F32))
        arg = pick(rows_of((NDEF, 128)), every) * slot_sq[0:1] + PHASE_OFFSET
        kind = part[0:1]
        move = jnp.where(kind == 2, -jnp.cos(turn), jnp.where(kind == 3, jnp.sin(turn), 0.0))
        tone = jnp.where(kind == 0, jnp.sin(arg), jnp.where(kind == 1, jnp.cos(arg), 0.0))
        table_s[...] = three(
            jnp.concatenate([move, tone, jnp.zeros((spare, 128), F32)], axis=0)
        )

    entry = (rows_of((3 * GROUP, 128)) & (GROUP - 1)).astype(F32)

    def chosen(move4, table):
        hot = jnp.concatenate(
            [
                jnp.where(
                    (entry == move4[g : g + 1, :] + 16.0)
                    | (entry == kind4[g : g + 1, :] + float(MOVES)),
                    1.0,
                    0.0,
                ).astype(BF)
                for g in range(4)
            ],
            axis=1,
        )
        return lax.dot_general(
            hot, table, (((0,), (0,)), ((), ())), preferred_element_type=F32
        )

    tabulate()
    vx[...] = chosen(pair_codes(11), table_x[...])
    scal = chosen(pair_codes(12), table_s[...])
    sc[0] = scal
    for t in range(1, TILES):
        sc[t] = pltpu.roll(scal, 128 - 8 * t, 1)

    load_right.wait()

    def process(t):
        pltpu.make_async_copy(recvb.at[t], recvb.at[t], row_r.at[t]).wait()

        def half(m, carry):
            block = recvb[t, pl.ds(m * 16, 16)].reshape(256, 2 * K)
            start = pl.multiple_of(m * 256, 256)
            pq[0, pl.ds(start, 256), :] = jnp.dot(
                block[:, :K], right[pl.ds(0, K), :], preferred_element_type=F32
            )
            pq[1, pl.ds(start, 256), :] = jnp.dot(
                block[:, K:], right[pl.ds(K, K), :], preferred_element_type=F32
            )
            return carry

        lax.fori_loop(0, 2, half, 0)

        def weigh(i, carry):
            got = [[], [], [], []]
            for j in range(2):
                rows = pl.ds(pl.multiple_of(i * 16 + j * 8, 8), 8)
                scal = sc[t, rows, :]
                sa, ca, er, ei = [scal[:, 2 * n + j : 2 * n + j + 1] for n in range(4)]
                exr, exi, sb, cb = [vx[rows, pl.ds(n * K, K)] for n in range(4)]
                pr, pi = pq[0, rows, pl.ds(0, K)], pq[0, rows, pl.ds(K, K)]
                qr, qi = pq[1, rows, pl.ds(0, K)], pq[1, rows, pl.ds(K, K)]
                ctf = sa * cb + ca * sb
                gr, gi = ctf * exr, ctf * exi
                fa, fb, fc, fd = er * gr, ei * gi, er * gi, ei * gr
                sr, si = pr + qr, pi + qi
                fr, fi = fa - fb, fc + fd
                got[0].append(sr * fr - si * fi)
                got[1].append(sr * fi + si * fr)
                sr, si = pr - qr, pi - qi
                fr, fi = fa + fb, fc - fd
                got[2].append(sr * fr - si * fi)
                got[3].append(sr * fi + si * fr)
            rows = pl.ds(pl.multiple_of(i * 16, 16), 16)
            for n in range(4):
                to = wp if n < 2 else wm
                to[rows, pl.ds((n % 2) * K, K)] = jnp.concatenate(got[n], axis=0).astype(BF)
            return carry

        lax.fori_loop(0, 32, weigh, 0, unroll=2)

        def total(hot, rows):
            return jnp.dot(hot, rows, preferred_element_type=F32).astype(BF).reshape(NS, 32, 2 * K)

        def give(start, size, dst):
            rows = pl.ds(start, size)
            to_slab(lambda peer: zsend.at[t, peer, rows], dst, z_s.at[t], z_r.at[t])
            pltpu.make_async_copy(zsend.at[t, ms, rows], dst, z_r.at[t]).start()

        @pl.when(t < LAST)
        def _():
            zsend[t, :, pl.ds(32, 32), :] = total(one_hot(pair_codes(TILES + t)), wm[...])
            whole = jnp.logical_or(t < SHARED - 1, core == 0)

            @pl.when(whole)
            def _():
                give(32, 32, zrecv.at[t, ms, pl.ds(32, 32)])

            @pl.when(jnp.logical_not(whole))
            def _():
                give(32, PL, zrecv.at[t, ms, pl.ds(32, PL)])

        zsend[t, :, pl.ds(0, 32), :] = total(one_hot(pair_codes(t)), wp[...])

        @pl.when(t < LAST)
        def _():
            give(0, 32, zrecv.at[t, ms, pl.ds(0, 32)])

        @pl.when(t == LAST)
        def _():
            give(0, PL, zgot.at[mz])

    def weights():
        lane_k = lax.broadcasted_iota(jnp.int32, (32, 128), 1)
        own_ky = mb * KYB + lax.broadcasted_iota(jnp.int32, (32, 128), 0)
        arg2_y = 2.0 * (pick(lane_k & (NDEF - 1), every) * square(own_ky) + PHASE_OFFSET)
        group = lane_k // NDEF
        tws[...] = jnp.where(
            group == 0,
            -0.5 * jnp.cos(arg2_y),
            jnp.where(group == 1, 0.5 * jnp.sin(arg2_y), jnp.where(group == 2, 0.5, 0.0)),
        )
        row_k = lax.broadcasted_iota(jnp.int32, (NDEF, K), 0)
        col_k = lax.broadcasted_iota(jnp.int32, (NDEF, K), 1)
        arg2_x = 2.0 * (pick(row_k, every) * square(col_k))
        rw = jnp.concatenate(
            [
                jnp.cos(arg2_x),
                jnp.sin(arg2_x),
                jnp.ones((NDEF, K), F32),
                jnp.zeros((128 - 3 * NDEF, K), F32),
            ],
            axis=0,
        )
        pltpu.make_async_copy(nrecv, nrecv, n_r).wait()

        def one(h, carry):
            x = nrecv[h].astype(F32)
            for z in range(1, NS // 2):
                x += nrecv[2 * z + h].astype(F32)
            own, more = 6 * h + 1, 6 * h + EXTRA
            lane = lax.broadcasted_iota(jnp.int32, (PL, 128), 1)
            blocks = []
            for g in range(2 * NCNT):
                part = x[:, g // 8 * 128 : g // 8 * 128 + 128]
                turn = [
                    pltpu.roll(part, (NDEF * (n - g)) % 128, 1) if (n - g) % 8 else part
                    for n in range(3)
                ]
                blocks.append(
                    jnp.where(lane < NDEF, turn[0], jnp.where(lane < 2 * NDEF, turn[1], turn[2]))
                )
            x = jnp.concatenate(blocks, axis=0)

            def times(part, i, rows):
                return (part.reshape(rows, PL, 128) * tws[pl.ds(i, rows), :][:, None, :]).reshape(
                    rows * PL, 128
                )

            scaled = jnp.concatenate(
                [times(x[:96], own, 6), times(x[96:128], 0, 2), times(x[128:], more, 6)], axis=0
            )
            res = jnp.dot(
                scaled, rw, precision=lax.Precision.HIGHEST, preferred_element_type=F32
            )
            res = 1.0 / (res + TAU_PRIOR)
            wts[pl.ds(pl.multiple_of(own * PL, PL), 96), :] = res[:96]
            wts[pl.ds(pl.multiple_of(more * PL, PL), 96), :] = res[128:]

            @pl.when(h == 0)
            def _():
                wts[pl.ds(0, PL), :] = res[96:112]

            return carry

        lax.fori_loop(0, 2, one, 0)

    def finish(i, sums):
        rows = pl.ds(pl.multiple_of(i * PL, PL), PL)
        inverse = wts[rows, :]
        for h in range(2):
            cols = pl.ds(h * K, K)
            top = TAU_PRIOR * ref[rows, cols].astype(F32) + sums[:, h * K : (h + 1) * K]
            out[rows, cols] = (top * inverse).astype(BF)

    def gather(t):
        @pl.when(t < SHARED - 1)
        def _():
            pltpu.make_async_copy(zrecv.at[t], zrecv.at[t], z_r.at[t]).wait()

        @pl.when(t == SHARED - 1)
        def _():
            some = zrecv.at[t, pl.ds(0, 7)]
            pltpu.make_async_copy(some, some, z_r.at[t]).wait()

        def over_z(h, start):
            rows = pl.ds(pl.multiple_of(start, PL), PL)
            x = zrecv[t, h, rows, :].astype(F32)
            for z in range(1, NS // 2):
                x += zrecv[t, 2 * z + h, rows, :].astype(F32)
            return x

        def mirror(m, carry):
            msend[t, m] = over_z(m // 2, 2 * PL + lax.rem(m, 2) * PL).astype(BF)
            return carry

        def pass_on(size):
            rows = pl.ds(0, size)
            lax.fori_loop(0, size, mirror, 0)
            pltpu.make_async_remote_copy(
                src_ref=msend.at[t, rows], dst_ref=mrecv.at[t, rows],
                send_sem=m_s.at[t], recv_sem=m_r.at[t],
                device_id=(NB - 1 - mb, ms), device_id_type=MESH,
            ).start()

        pl.when(t < SHARED - 1)(lambda: pass_on(4))
        pl.when(t == SHARED - 1)(lambda: pass_on(3))

        def own(m, carry):
            h, j = m // 2, lax.rem(m, 2)
            finish(6 * h + 2 * t + 1 + j, over_z(h, j * PL))
            return carry

        lax.fori_loop(0, 4, own, 0)

    def drain(src, send_sem, recv_sem):
        return pltpu.make_async_remote_copy(
            src_ref=src, dst_ref=src, send_sem=send_sem, recv_sem=recv_sem,
            device_id=(mb, ms), device_id_type=MESH,
        )

    def mirrored(t, carry):
        @pl.when(t < SHARED - 1)
        def _():
            drain(msend.at[t], m_s.at[t], m_r.at[t]).wait()

        @pl.when(t == SHARED - 1)
        def _():
            drain(msend.at[t, pl.ds(0, 3)], m_s.at[t], m_r.at[t]).wait()


        def one(m, inner):
            i = 6 * (m // 2) + 2 * t + 1 + lax.rem(m, 2)

            @pl.when(i < KYB // 2)
            def _():
                finish(KYB - i, mrecv[t, m].astype(F32))

            return inner

        lax.fori_loop(0, 4, one, 0)
        return carry

    def consume(t, carry):
        @pl.when(jnp.logical_or(t < LAST, core == 0))
        def _():
            process(t)

        @pl.when(t < 2)
        def _():
            compute(t + 2)

        @pl.when(t == 0)
        def _():
            send_rows(2)

        @pl.when(t == 1)
        def _():
            send_last()
            tally()
            weights()

        @pl.when(jnp.logical_or(t == 1, t == 2))
        def _():
            gather(t - 1)

        @pl.when(t == LAST)
        def _():
            lax.fori_loop(0, 2, mirrored, 0)

        return carry

    load_ref.wait()
    lax.fori_loop(0, TILES, consume, 0)

    gather(SHARED - 1)
    pltpu.make_async_copy(zgot, zgot, z_r.at[LAST]).wait()
    x = zgot[0].astype(F32)
    for z in range(1, NS // 2):
        x += zgot[z].astype(F32)
    finish(0, x)

    mirrored(SHARED - 1, 0)

    drain(crecv.at[pl.ds(0, 31)], code_s, code_r).wait_send()
    drain(nsend.at[pl.ds(0, 7)], n_s, n_r).wait_send()
    def drain_tile(t, carry):
        drain(sendb.at[t, pl.ds(0, 31)], row_s.at[t], row_r.at[t]).wait_send()
        whole = jnp.logical_or(t < SHARED - 1, core == 0)

        @pl.when(whole)
        def _():
            drain(zsend.at[t, pl.ds(0, 7)], z_s.at[t], z_r.at[t]).wait_send()

        @pl.when(jnp.logical_not(whole))
        def _():
            drain(zsend.at[t, pl.ds(0, 7), pl.ds(0, 48)], z_s.at[t], z_r.at[t]).wait_send()

        return carry

    lax.fori_loop(0, SHARED, drain_tile, 0)

    @pl.when(core == 0)
    def _():
        drain(sendb.at[LAST, pl.ds(0, 15)], row_s.at[LAST], row_r.at[LAST]).wait_send()
        drain(zsend.at[LAST, pl.ds(0, 7), pl.ds(0, PL)], z_s.at[LAST], z_r.at[LAST]).wait_send()

    @pl.when(core == 1)
    def _():
        drain(sendb.at[LAST, pl.ds(0, 16)], row_s.at[LAST], row_r.at[LAST]).wait_send()


def per_device(images, classes, shifts, defocus_class, defocus, run_counts, dest_map, ref):
    left, right = tables()
    vmem = pl.BlockSpec(memory_space=pltpu.VMEM)
    smem = pl.BlockSpec(memory_space=pltpu.SMEM)
    far = pl.BlockSpec(memory_space=pl.ANY)
    dma = pltpu.SemaphoreType.DMA
    out = pl.pallas_call(
        kernel,
        out_shape=jax.ShapeDtypeStruct((KYB * PL, 2 * K), BF),
        in_specs=[smem] * 4 + [vmem] * 2 + [far] * 4,
        out_specs=vmem,
        scratch_shapes=[
            pltpu.VMEM((PP, K, K), BF),
            pltpu.VMEM((2 * K, 2 * K), BF),
            pltpu.VMEM(dest_map.shape, jnp.int32),
            pltpu.VMEM((KYB * PL, 2 * K), BF),
            pltpu.VMEM((6, 64 * PP, 128), F32),
            pltpu.VMEM((K, 128), F32),
            pltpu.VMEM((16, 128), F32),
            pltpu.VMEM((32, 16, 128), BF),
            pltpu.VMEM((32 * 16, 128), F32),
            pltpu.VMEM((TILES, 512, 128), F32),
            pltpu.VMEM((512, 4 * K), F32),
            pltpu.VMEM((3 * GROUP, 4 * K), BF),
            pltpu.VMEM((3 * GROUP, 128), BF),
            pltpu.VMEM((2, 512, 2 * K), F32),
            pltpu.VMEM((512, 2 * K), BF),
            pltpu.VMEM((512, 2 * K), BF),
            pltpu.VMEM((TILES, 32, 16, 2 * K), BF),
            pltpu.VMEM((TILES, 32, 16, 2 * K), BF),
            pltpu.VMEM((32, 16, 128), BF),
            pltpu.VMEM((TILES, NS, 64, 2 * K), BF),
            pltpu.VMEM((SHARED, NS, 64, 2 * K), BF),
            pltpu.VMEM((NS // 2, PL, 2 * K), BF),
            pltpu.VMEM((NS, PL, 256), BF),
            pltpu.VMEM((NS, PL, 256), BF),
            pltpu.VMEM((SHARED, 4, PL, 2 * K), BF),
            pltpu.VMEM((SHARED, 4, PL, 2 * K), BF),
            pltpu.VMEM(((KYB + 1) * PL, K), F32),
            pltpu.VMEM((32, 128), F32),
            dma((PP,)), dma, dma, dma, dma, dma, dma((TILES,)), dma((TILES,)),
            dma((TILES,)), dma((TILES,)), dma, dma, dma((SHARED,)), dma((SHARED,)),
        ],
        compiler_params=pltpu.CompilerParams(
            collective_id=0, has_side_effects=True, vmem_limit_bytes=60 * 1024 * 1024
        ),
    )(
        classes, defocus_class, defocus, shifts.T, run_counts, jnp.asarray(left),
        images, jnp.asarray(right), dest_map,
        ref.reshape(KYB * PL, 2 * K),
    )
    return out.reshape(KYB, PL, 2 * K)


def solution(mesh):
    placed = (
        P(("batch", "slab"), None, None),
        P(("batch", "slab")),
        P(("batch", "slab"), None),
        P(("batch", "slab")),
        P(),
        P(("batch", "slab"), None),
        P(),
        P("batch", "slab", None),
    )
    return jax.shard_map(
        per_device, mesh=mesh, in_specs=placed, out_specs=P("batch", "slab", None), check_vma=False
    )
```

```python
import math

import jax
import jax.numpy as jnp
import ml_dtypes
import numpy as np
from jax import lax
from jax.experimental import pallas as pl
from jax.experimental.pallas import tpu as pltpu
from jax.sharding import PartitionSpec as P

TAU_PRIOR = 4.0
PHASE_OFFSET = 0.1
MESH = pl.DeviceIdType.MESH

K = 384
NB = 16
NS = 8
PP = 8
KYB = K // NB
SHARED = 3
TILES = SHARED + 1
PL = 16
NDEF = 16
BF = jnp.bfloat16
F32 = jnp.float32
LAST = SHARED
EXTRA = 13
HOPS = ((1, 0), (3, 1), (2, 0), (3, 0), (1, 1), (2, 1), (0, 1))
NCNT = TILES + 3
MOVES = 40
GROUP = 64
TURNS = (
    (0, 1), (1, 0), (0, 3), (3, 0), (1, 1), (1, 3), (3, 3), (3, 1),
    (1, 2), (2, 1), (3, 2), (2, 3), (0, 2), (2, 0), (2, 2),
)


def tables():
    index = np.arange(K)
    angle = 2.0 * np.pi / K * ((index[:, None] * index[None, :]) % K)
    cosine = (np.cos(angle) / math.sqrt(K)).astype(np.float32)
    sine = (np.sin(angle) / math.sqrt(K)).astype(np.float32)

    def left(t):
        rows = [
            KYB * b + (6 * h + 2 * t + 1 + j if t < LAST else 0)
            for h in range(2)
            for b in range(NB)
            for j in range(2)
        ]
        return np.concatenate([cosine[rows], -sine[rows]], axis=0)

    both = np.stack([left(t) for t in range(TILES)], axis=0)
    right = np.concatenate(
        [np.concatenate([cosine, -sine], 1), np.concatenate([sine, cosine], 1)], 0
    )
    kind = ml_dtypes.bfloat16
    return both.astype(kind), right.astype(kind)


def kernel(
    classes, kinds_in, defocus, shifts, counts, left, img_in, right_in, dest_in, ref_in,
    out,
    img, right, dest, ref, scr, cscr, cwide, codes, cf, sc, vx, table_x, table_s, pq, wp, wm,
    sendb, recvb, crecv, zsend, zrecv, zgot, nsend, nrecv, msend, mrecv, wts, tws,
    img_m, right_m, dest_m, ref_m, code_s, code_r, row_s, row_r, z_s, z_r, y_s, y_r, n_s, n_r, m_s, m_r,
):
    mb = lax.axis_index("batch")
    ms = lax.axis_index("slab")
    core = lax.rem(ms, 2)
    zbase = ms - core
    mz = ms // 2
    me = mb * 2 + core
    my = mb // 4
    mx = lax.rem(mb, 4)

    def peer_of(turn):
        dy, dx = turn
        py = lax.rem(my + jnp.where(core == 0, dy, dx), 4)
        px = lax.rem(mx + jnp.where(core == 0, dx, 4 - dy), 4)
        return py * 4 + px

    barrier = pltpu.get_barrier_semaphore()
    loads = [pltpu.make_async_copy(img_in.at[p], img.at[p], img_m.at[p]) for p in range(PP)]
    load_right = pltpu.make_async_copy(right_in, right, right_m)
    load_dest = pltpu.make_async_copy(dest_in, dest, dest_m)
    load_ref = pltpu.make_async_copy(ref_in, ref, ref_m)
    for load in (*loads, load_dest, load_right, load_ref):
        load.start()

    def greet_plane(q, carry):
        i = lax.rem(me + q, 32)
        pl.semaphore_signal(
            barrier, inc=1, device_id=(i // 2, zbase + lax.rem(i, 2)), device_id_type=MESH
        )
        return carry

    def greet_slab(q, carry):
        pl.semaphore_signal(
            barrier, inc=1, device_id=(mb, lax.rem(ms + q, NS)), device_id_type=MESH
        )
        return carry

    lax.fori_loop(1, 32, greet_plane, 0)
    lax.fori_loop(1, NS, greet_slab, 0)

    def pick(index, values):
        got = jnp.full(index.shape, values[0])
        for i, value in enumerate(values[1:], 1):
            got = jnp.where(index == i, value, got)
        return got

    def square(k):
        half = jnp.where(k >= K // 2, k - K, k).astype(F32) * (1.0 / K)
        return half * half

    def phase(k, shift):
        turn = k.astype(F32) * shift
        turn = turn - K * jnp.floor((turn + 0.5) * (1.0 / K))
        return turn * (2.0 * math.pi / K)

    def to_plane(b, h, src, dst, send_sem, recv_sem):
        pltpu.make_async_remote_copy(
            src_ref=src, dst_ref=dst, send_sem=send_sem, recv_sem=recv_sem,
            device_id=(b, zbase + h), device_id_type=MESH,
        ).start()

    def compute(t):
        table = left[t]

        def one(p, carry):
            @pl.when(t == 0)
            def _():
                pltpu.make_async_copy(img_in.at[p], img.at[p], img_m.at[p]).wait()

            sec = jnp.dot(table, img[p], preferred_element_type=F32)
            for g in range(3):
                cols = slice(g * 128, (g + 1) * 128)
                scr[g, pl.ds(p, 64, stride=8), :] = sec[:64, cols]
                scr[3 + g, pl.ds(p, 64, stride=8), :] = sec[64:, cols]
            return carry

        lax.fori_loop(0, PP, one, 0)

        def pack(i, carry):
            start = pl.multiple_of(i * 16, 16)
            target = lax.rem(i, NB) * 2 + i // NB
            for g in range(6):
                sendb[t, target, :, pl.ds(g * 128, 128)] = scr[g, pl.ds(start, 16), :].astype(BF)
            return carry

        lax.fori_loop(0, 32, pack, 0)

    other = 1 - core

    def send_rows(t):
        for h in range(2):
            own = recvb.at[t, me]

            @pl.when(core == h)
            def _():
                pltpu.make_async_copy(sendb.at[t, me], own, row_r.at[t]).start()

            @pl.when(core != h)
            def _():
                to_plane(mb, h, sendb.at[t, mb * 2 + h], own, row_s.at[t], row_r.at[t])

            for turn in TURNS:
                b = peer_of(turn)
                to_plane(b, h, sendb.at[t, b * 2 + h], own, row_s.at[t], row_r.at[t])

    def send_last():
        t = LAST

        @pl.when(core == 0)
        def _():
            pltpu.make_async_copy(sendb.at[t, me], recvb.at[t, me], row_r.at[t]).start()

        @pl.when(core == 1)
        def _():
            to_plane(mb, 0, sendb.at[t, mb * 2], recvb.at[t, me], row_s.at[t], row_r.at[t])

        for turn in TURNS:
            b = peer_of(turn)
            to_plane(b, 0, sendb.at[t, b * 2], recvb.at[t, me], row_s.at[t], row_r.at[t])

    sub_p = lax.broadcasted_iota(jnp.int32, (PP, K), 0)
    col = lax.broadcasted_iota(jnp.int32, (PP, K), 1)
    row8 = lax.broadcasted_iota(jnp.int32, (PP, 128), 0)
    lane8 = lax.broadcasted_iota(jnp.int32, (PP, 128), 1)

    def tell():
        load_dest.wait()
        end = counts[:, 0:1]
        slab = jnp.zeros((PP, K), jnp.int32)
        for i in range(1, NS):
            slab = slab + jnp.where(col >= end, 1, 0)
            end = end + counts[:, i : i + 1]
        plane = pick(sub_p, [dest[pl.ds(classes[p], 1), :] for p in range(PP)])
        place = slab * 32 + plane
        spread = jnp.where(lax.rem(lane8, PP) == row8, 1.0, 0.0)
        kind8 = pick(row8, [kinds_in[p] for p in range(PP)])

        def turned(x):
            return lax.dot_general(
                x.astype(F32), spread, (((0,), (0,)), ((), ())),
                precision=lax.Precision.HIGHEST, preferred_element_type=F32,
            )

        cscr[...] = turned(place)
        shift_x = pick(row8, [shifts[0, p] for p in range(PP)])
        shift_y = pick(row8, [shifts[1, p] for p in range(PP)])
        person = turned(pick(lane8, [kind8, shift_x, shift_y]))
        slot_one = (lax.broadcasted_iota(jnp.int32, (1, 128), 1) // PP) & 1

        def arrange(d, carry):
            base = d // 2 * KYB
            step = 6 * lax.rem(d, 2)
            for n in range(TILES + SHARED + 3):
                for_two = []
                for j in range(2):
                    if n < SHARED:
                        ky = base + step + 2 * n + 1 + j
                    elif n == LAST:
                        ky = base
                    elif n < TILES + SHARED:
                        ky = K - (base + step + 2 * (n - TILES) + 1 + j)
                    else:
                        ky = jnp.minimum(base + EXTRA + step + 2 * (n - TILES - SHARED) + j, K - 1)
                    for_two.append(cscr[pl.ds(ky, 1), :])
                cwide[n : n + 1, :] = jnp.where(slot_one == 0, for_two[0], for_two[1] + PL)
            codes[d] = cwide[...].astype(BF)
            return carry

        cwide[...] = jnp.zeros_like(cwide)
        cwide[10:13, :] = person[0:3]
        lax.fori_loop(0, 2 * NB, arrange, 0)

        def send_codes(q, carry):
            i = lax.rem(me + q, 32)
            to_plane(i // 2, lax.rem(i, 2), codes.at[i], crecv.at[me], code_s, code_r)
            return carry

        pltpu.make_async_copy(codes.at[me], crecv.at[me], code_r).start()
        lax.fori_loop(1, 32, send_codes, 0)


    def produce(t, carry):
        compute(t)

        @pl.when(t == 0)
        def _():
            pl.semaphore_wait(barrier, 31 + NS - 1)

        send_rows(t)
        pl.when(t == 0)(tell)
        return carry

    lax.fori_loop(0, 2, produce, 0)

    pltpu.make_async_copy(crecv, crecv, code_r).wait()

    def widen(i, carry):
        cf[pl.ds(pl.multiple_of(i * 16, 16), 16), :] = crecv[i].astype(F32)
        return carry

    lax.fori_loop(0, 32, widen, 0)

    lane = lax.broadcasted_iota(jnp.int32, (32, 128), 1)
    sub = lax.broadcasted_iota(jnp.int32, (32, 128), 0)
    mine = (lane // 16) == lax.rem(sub, 8)

    def pair_codes(row):
        got = cf[pl.ds(row, 32, stride=16), :]
        return jnp.sum(jnp.where(mine, got, 0.0).reshape(4, 8, 128), axis=1)

    spot = lax.broadcasted_iota(jnp.int32, (256, 128), 0).astype(F32)

    def one_hot(code4):
        return jnp.concatenate(
            [
                jnp.where(spot == code4[g : g + 1, :], 1.0, 0.0).astype(BF)
                for g in range(4)
            ],
            axis=1,
        )

    def to_slab(src, dst, send_sem, recv_sem):
        for dz, flip in HOPS:
            z = lax.rem(mz + jnp.where(core == 0, dz, 4 - dz), 4)
            peer = z * 2 + (1 - core if flip else core)
            pltpu.make_async_remote_copy(
                src_ref=src(peer), dst_ref=dst, send_sem=send_sem, recv_sem=recv_sem,
                device_id=(mb, peer), device_id_type=MESH,
            ).start()

    kind4 = pair_codes(10)

    def tally():
        spot_z = lax.broadcasted_iota(jnp.int32, (128, 128), 0).astype(F32)
        slot_k = ((lax.broadcasted_iota(jnp.int32, (4, 128), 1) // PP) & 1).astype(F32)
        which = kind4 + NDEF * slot_k

        def hot(code4):
            return jnp.concatenate(
                [
                    jnp.where(spot_z == code4[g : g + 1, :], 1.0, 0.0).astype(BF)
                    for g in range(4)
                ],
                axis=1,
            )

        def one(n, acc):
            code4 = pair_codes(jnp.where(n < TILES, n, n + SHARED))
            flat = code4 - 16.0 * jnp.floor(code4 * (1.0 / 16)) + 16.0 * jnp.floor(code4 * (1.0 / 32))
            group = ((n & 3) * 2 * NDEF).astype(F32)
            return acc + lax.dot_general(
                hot(flat), hot(which + group), (((1,), (1,)), ((), ())), preferred_element_type=F32
            )

        for half, (low, high) in enumerate(((0, 4), (4, NCNT))):
            acc = lax.fori_loop(low, high, one, jnp.zeros((128, 128), F32))
            nsend[:, :, pl.ds(half * 128, 128)] = acc.astype(BF).reshape(NS, PL, 128)
        to_slab(lambda peer: nsend.at[peer], nrecv.at[ms], n_s, n_r)
        pltpu.make_async_copy(nsend.at[ms], nrecv.at[ms], n_r).start()

    slot_of = (lane8 // 8) * 2 + (lane8 & 1)
    part = (lane8 // 2) & 3
    slot_ky = mb * KYB + jnp.where(slot_of < 2 * SHARED, 6 * core + 1 + slot_of, 0)
    slot_sq = square(slot_ky)
    every = [defocus[i] for i in range(NDEF)]

    def three(x):
        high = x.astype(BF)
        mid = (x - high.astype(F32)).astype(BF)
        low = (x - high.astype(F32) - mid.astype(F32)).astype(BF)
        return jnp.concatenate([high, mid, low], axis=0)

    def rows_of(shape, axis=0):
        return lax.broadcasted_iota(jnp.int32, shape, axis)

    def tabulate():
        turn = phase(rows_of((MOVES, K), 1), (rows_of((MOVES, K)) - 16).astype(F32))
        arg = pick(rows_of((NDEF, K)), every) * square(rows_of((NDEF, K), 1))
        spare = GROUP - MOVES - NDEF
        for n, (move, kind) in enumerate(
            (
                (jnp.cos(turn), None),
                (-jnp.sin(turn), None),
                (None, jnp.sin(arg)),
                (None, jnp.cos(arg)),
            )
        ):
            move = jnp.zeros((MOVES, K), F32) if move is None else move
            kind = jnp.zeros((NDEF, K), F32) if kind is None else kind
            full = jnp.concatenate([move, kind, jnp.zeros((spare, K), F32)], axis=0)
            table_x[:, pl.ds(n * K, K)] = three(full)
        turn = phase(slot_ky[0:1], (rows_of((MOVES, 128)) - 16).astype(F32))
        arg = pick(rows_of((NDEF, 128)), every) * slot_sq[0:1] + PHASE_OFFSET
        kind = part[0:1]
        move = jnp.where(kind == 2, -jnp.cos(turn), jnp.where(kind == 3, jnp.sin(turn), 0.0))
        tone = jnp.where(kind == 0, jnp.sin(arg), jnp.where(kind == 1, jnp.cos(arg), 0.0))
        table_s[...] = three(
            jnp.concatenate([move, tone, jnp.zeros((spare, 128), F32)], axis=0)
        )

    entry = (rows_of((3 * GROUP, 128)) & (GROUP - 1)).astype(F32)

    def chosen(move4, table):
        hot = jnp.concatenate(
            [
                jnp.where(
                    (entry == move4[g : g + 1, :] + 16.0)
                    | (entry == kind4[g : g + 1, :] + float(MOVES)),
                    1.0,
                    0.0,
                ).astype(BF)
                for g in range(4)
            ],
            axis=1,
        )
        return lax.dot_general(
            hot, table, (((0,), (0,)), ((), ())), preferred_element_type=F32
        )

    tabulate()
    vx[...] = chosen(pair_codes(11), table_x[...])
    scal = chosen(pair_codes(12), table_s[...])
    sc[0] = scal
    for t in range(1, TILES):
        sc[t] = pltpu.roll(scal, 128 - 8 * t, 1)

    load_right.wait()

    def process(t):
        pltpu.make_async_copy(recvb.at[t], recvb.at[t], row_r.at[t]).wait()

        def half(m, carry):
            block = recvb[t, pl.ds(m * 16, 16)].reshape(256, 2 * K)
            start = pl.multiple_of(m * 256, 256)
            pq[0, pl.ds(start, 256), :] = jnp.dot(
                block[:, :K], right[pl.ds(0, K), :], preferred_element_type=F32
            )
            pq[1, pl.ds(start, 256), :] = jnp.dot(
                block[:, K:], right[pl.ds(K, K), :], preferred_element_type=F32
            )
            return carry

        lax.fori_loop(0, 2, half, 0)

        def weigh(i, carry):
            got = [[], [], [], []]
            for j in range(2):
                rows = pl.ds(pl.multiple_of(i * 16 + j * 8, 8), 8)
                scal = sc[t, rows, :]
                sa, ca, er, ei = [scal[:, 2 * n + j : 2 * n + j + 1] for n in range(4)]
                exr, exi, sb, cb = [vx[rows, pl.ds(n * K, K)] for n in range(4)]
                pr, pi = pq[0, rows, pl.ds(0, K)], pq[0, rows, pl.ds(K, K)]
                qr, qi = pq[1, rows, pl.ds(0, K)], pq[1, rows, pl.ds(K, K)]
                ctf = sa * cb + ca * sb
                gr, gi = ctf * exr, ctf * exi
                fa, fb, fc, fd = er * gr, ei * gi, er * gi, ei * gr
                sr, si = pr + qr, pi + qi
                fr, fi = fa - fb, fc + fd
                got[0].append(sr * fr - si * fi)
                got[1].append(sr * fi + si * fr)
                sr, si = pr - qr, pi - qi
                fr, fi = fa + fb, fc - fd
                got[2].append(sr * fr - si * fi)
                got[3].append(sr * fi + si * fr)
            rows = pl.ds(pl.multiple_of(i * 16, 16), 16)
            for n in range(4):
                to = wp if n < 2 else wm
                to[rows, pl.ds((n % 2) * K, K)] = jnp.concatenate(got[n], axis=0).astype(BF)
            return carry

        lax.fori_loop(0, 32, weigh, 0, unroll=2)

        def total(hot, rows):
            return jnp.dot(hot, rows, preferred_element_type=F32).astype(BF).reshape(NS, 32, 2 * K)

        def give(start, size, dst, send_sem, recv_sem):
            rows = pl.ds(start, size)
            to_slab(lambda peer: zsend.at[t, peer, rows], dst, send_sem, recv_sem)
            pltpu.make_async_copy(zsend.at[t, ms, rows], dst, recv_sem).start()

        @pl.when(t < LAST)
        def _():
            zsend[t, :, pl.ds(32, 32), :] = total(one_hot(pair_codes(TILES + t)), wm[...])
            whole = jnp.logical_or(t < SHARED - 1, core == 0)

            @pl.when(whole)
            def _():
                give(32, 32, zrecv.at[t, ms, pl.ds(32, 32)], y_s.at[t], y_r.at[t])

            @pl.when(jnp.logical_not(whole))
            def _():
                give(32, PL, zrecv.at[t, ms, pl.ds(32, PL)], y_s.at[t], y_r.at[t])

        zsend[t, :, pl.ds(0, 32), :] = total(one_hot(pair_codes(t)), wp[...])

        @pl.when(t < LAST)
        def _():
            give(0, 32, zrecv.at[t, ms, pl.ds(0, 32)], z_s.at[t], z_r.at[t])

        @pl.when(t == LAST)
        def _():
            give(0, PL, zgot.at[mz], z_s.at[t], z_r.at[t])

    def weights():
        lane_k = lax.broadcasted_iota(jnp.int32, (32, 128), 1)
        own_ky = mb * KYB + lax.broadcasted_iota(jnp.int32, (32, 128), 0)
        arg2_y = 2.0 * (pick(lane_k & (NDEF - 1), every) * square(own_ky) + PHASE_OFFSET)
        group = lane_k // NDEF
        tws[...] = jnp.where(
            group == 0,
            -0.5 * jnp.cos(arg2_y),
            jnp.where(group == 1, 0.5 * jnp.sin(arg2_y), jnp.where(group == 2, 0.5, 0.0)),
        )
        row_k = lax.broadcasted_iota(jnp.int32, (NDEF, K), 0)
        col_k = lax.broadcasted_iota(jnp.int32, (NDEF, K), 1)
        arg2_x = 2.0 * (pick(row_k, every) * square(col_k))
        rw = jnp.concatenate(
            [
                jnp.cos(arg2_x),
                jnp.sin(arg2_x),
                jnp.ones((NDEF, K), F32),
                jnp.zeros((128 - 3 * NDEF, K), F32),
            ],
            axis=0,
        )
        pltpu.make_async_copy(nrecv, nrecv, n_r).wait()

        def one(h, carry):
            x = nrecv[h].astype(F32)
            for z in range(1, NS // 2):
                x += nrecv[2 * z + h].astype(F32)
            own, more = 6 * h + 1, 6 * h + EXTRA
            lane = lax.broadcasted_iota(jnp.int32, (PL, 128), 1)
            blocks = []
            for g in range(2 * NCNT):
                part = x[:, g // 8 * 128 : g // 8 * 128 + 128]
                turn = [
                    pltpu.roll(part, (NDEF * (n - g)) % 128, 1) if (n - g) % 8 else part
                    for n in range(3)
                ]
                blocks.append(
                    jnp.where(lane < NDEF, turn[0], jnp.where(lane < 2 * NDEF, turn[1], turn[2]))
                )
            x = jnp.concatenate(blocks, axis=0)

            def times(part, i, rows):
                return (part.reshape(rows, PL, 128) * tws[pl.ds(i, rows), :][:, None, :]).reshape(
                    rows * PL, 128
                )

            scaled = jnp.concatenate(
                [times(x[:96], own, 6), times(x[96:128], 0, 2), times(x[128:], more, 6)], axis=0
            )
            res = jnp.dot(
                scaled, rw, precision=lax.Precision.HIGHEST, preferred_element_type=F32
            )
            res = 1.0 / (res + TAU_PRIOR)
            wts[pl.ds(pl.multiple_of(own * PL, PL), 96), :] = res[:96]
            wts[pl.ds(pl.multiple_of(more * PL, PL), 96), :] = res[128:]

            @pl.when(h == 0)
            def _():
                wts[pl.ds(0, PL), :] = res[96:112]

            return carry

        lax.fori_loop(0, 2, one, 0)

    def finish(i, sums):
        rows = pl.ds(pl.multiple_of(i * PL, PL), PL)
        inverse = wts[rows, :]
        for h in range(2):
            cols = pl.ds(h * K, K)
            top = TAU_PRIOR * ref[rows, cols].astype(F32) + sums[:, h * K : (h + 1) * K]
            out[rows, cols] = (top * inverse).astype(BF)

    def gather(t):
        @pl.when(t < SHARED - 1)
        def _():
            some = zrecv.at[t, :, pl.ds(32, 32)]
            pltpu.make_async_copy(some, some, y_r.at[t]).wait()

        @pl.when(t == SHARED - 1)
        def _():
            some = zrecv.at[t, pl.ds(0, 6), pl.ds(32, 32)]
            pltpu.make_async_copy(some, some, y_r.at[t]).wait()

        def over_z(h, start):
            rows = pl.ds(pl.multiple_of(start, PL), PL)
            x = zrecv[t, h, rows, :].astype(F32)
            for z in range(1, NS // 2):
                x += zrecv[t, 2 * z + h, rows, :].astype(F32)
            return x

        def mirror(m, carry):
            msend[t, m] = over_z(m // 2, 2 * PL + lax.rem(m, 2) * PL).astype(BF)
            return carry

        def pass_on(size):
            rows = pl.ds(0, size)
            lax.fori_loop(0, size, mirror, 0)
            pltpu.make_async_remote_copy(
                src_ref=msend.at[t, rows], dst_ref=mrecv.at[t, rows],
                send_sem=m_s.at[t], recv_sem=m_r.at[t],
                device_id=(NB - 1 - mb, ms), device_id_type=MESH,
            ).start()

        pl.when(t < SHARED - 1)(lambda: pass_on(4))
        pl.when(t == SHARED - 1)(lambda: pass_on(3))

        some = zrecv.at[t, :, pl.ds(0, 32)]
        pltpu.make_async_copy(some, some, z_r.at[t]).wait()

        def own(m, carry):
            h, j = m // 2, lax.rem(m, 2)
            finish(6 * h + 2 * t + 1 + j, over_z(h, j * PL))
            return carry

        lax.fori_loop(0, 4, own, 0)

    def drain(src, send_sem, recv_sem):
        return pltpu.make_async_remote_copy(
            src_ref=src, dst_ref=src, send_sem=send_sem, recv_sem=recv_sem,
            device_id=(mb, ms), device_id_type=MESH,
        )

    def mirrored(t, carry):
        @pl.when(t < SHARED - 1)
        def _():
            drain(msend.at[t], m_s.at[t], m_r.at[t]).wait()

        @pl.when(t == SHARED - 1)
        def _():
            drain(msend.at[t, pl.ds(0, 3)], m_s.at[t], m_r.at[t]).wait()


        def one(m, inner):
            i = 6 * (m // 2) + 2 * t + 1 + lax.rem(m, 2)

            @pl.when(i < KYB // 2)
            def _():
                finish(KYB - i, mrecv[t, m].astype(F32))

            return inner

        lax.fori_loop(0, 4, one, 0)
        return carry

    def consume(t, carry):
        @pl.when(jnp.logical_or(t < LAST, core == 0))
        def _():
            process(t)

        @pl.when(t < 2)
        def _():
            compute(t + 2)

        @pl.when(t == 0)
        def _():
            send_rows(2)

        @pl.when(t == 1)
        def _():
            send_last()
            weights()

        @pl.when(jnp.logical_or(t == 1, t == 2))
        def _():
            gather(t - 1)

        @pl.when(t == LAST)
        def _():
            lax.fori_loop(0, 2, mirrored, 0)

        return carry

    tally()
    load_ref.wait()
    lax.fori_loop(0, TILES, consume, 0)

    gather(SHARED - 1)
    pltpu.make_async_copy(zgot, zgot, z_r.at[LAST]).wait()
    x = zgot[0].astype(F32)
    for z in range(1, NS // 2):
        x += zgot[z].astype(F32)
    finish(0, x)

    mirrored(SHARED - 1, 0)

    drain(crecv.at[pl.ds(0, 31)], code_s, code_r).wait_send()
    drain(nsend.at[pl.ds(0, 7)], n_s, n_r).wait_send()
    def drain_tile(t, carry):
        drain(sendb.at[t, pl.ds(0, 31)], row_s.at[t], row_r.at[t]).wait_send()
        whole = jnp.logical_or(t < SHARED - 1, core == 0)

        @pl.when(whole)
        def _():
            drain(zsend.at[t, pl.ds(0, 7), pl.ds(0, 32)], y_s.at[t], y_r.at[t]).wait_send()

        @pl.when(jnp.logical_not(whole))
        def _():
            drain(zsend.at[t, pl.ds(0, 7), pl.ds(0, PL)], y_s.at[t], y_r.at[t]).wait_send()

        drain(zsend.at[t, pl.ds(0, 7), pl.ds(0, 32)], z_s.at[t], z_r.at[t]).wait_send()
        return carry

    lax.fori_loop(0, SHARED, drain_tile, 0)

    @pl.when(core == 0)
    def _():
        drain(sendb.at[LAST, pl.ds(0, 15)], row_s.at[LAST], row_r.at[LAST]).wait_send()
        drain(zsend.at[LAST, pl.ds(0, 7), pl.ds(0, PL)], z_s.at[LAST], z_r.at[LAST]).wait_send()

    @pl.when(core == 1)
    def _():
        drain(sendb.at[LAST, pl.ds(0, 16)], row_s.at[LAST], row_r.at[LAST]).wait_send()


def per_device(images, classes, shifts, defocus_class, defocus, run_counts, dest_map, ref):
    left, right = tables()
    vmem = pl.BlockSpec(memory_space=pltpu.VMEM)
    smem = pl.BlockSpec(memory_space=pltpu.SMEM)
    far = pl.BlockSpec(memory_space=pl.ANY)
    dma = pltpu.SemaphoreType.DMA
    out = pl.pallas_call(
        kernel,
        out_shape=jax.ShapeDtypeStruct((KYB * PL, 2 * K), BF),
        in_specs=[smem] * 4 + [vmem] * 2 + [far] * 4,
        out_specs=vmem,
        scratch_shapes=[
            pltpu.VMEM((PP, K, K), BF),
            pltpu.VMEM((2 * K, 2 * K), BF),
            pltpu.VMEM(dest_map.shape, jnp.int32),
            pltpu.VMEM((KYB * PL, 2 * K), BF),
            pltpu.VMEM((6, 64 * PP, 128), F32),
            pltpu.VMEM((K, 128), F32),
            pltpu.VMEM((16, 128), F32),
            pltpu.VMEM((32, 16, 128), BF),
            pltpu.VMEM((32 * 16, 128), F32),
            pltpu.VMEM((TILES, 512, 128), F32),
            pltpu.VMEM((512, 4 * K), F32),
            pltpu.VMEM((3 * GROUP, 4 * K), BF),
            pltpu.VMEM((3 * GROUP, 128), BF),
            pltpu.VMEM((2, 512, 2 * K), F32),
            pltpu.VMEM((512, 2 * K), BF),
            pltpu.VMEM((512, 2 * K), BF),
            pltpu.VMEM((TILES, 32, 16, 2 * K), BF),
            pltpu.VMEM((TILES, 32, 16, 2 * K), BF),
            pltpu.VMEM((32, 16, 128), BF),
            pltpu.VMEM((TILES, NS, 64, 2 * K), BF),
            pltpu.VMEM((SHARED, NS, 64, 2 * K), BF),
            pltpu.VMEM((NS // 2, PL, 2 * K), BF),
            pltpu.VMEM((NS, PL, 256), BF),
            pltpu.VMEM((NS, PL, 256), BF),
            pltpu.VMEM((SHARED, 4, PL, 2 * K), BF),
            pltpu.VMEM((SHARED, 4, PL, 2 * K), BF),
            pltpu.VMEM(((KYB + 1) * PL, K), F32),
            pltpu.VMEM((32, 128), F32),
            dma((PP,)), dma, dma, dma, dma, dma, dma((TILES,)), dma((TILES,)),
            dma((TILES,)), dma((TILES,)), dma((SHARED,)), dma((SHARED,)), dma, dma,
            dma((SHARED,)), dma((SHARED,)),
        ],
        compiler_params=pltpu.CompilerParams(
            collective_id=0, has_side_effects=True, vmem_limit_bytes=60 * 1024 * 1024
        ),
    )(
        classes, defocus_class, defocus, shifts.T, run_counts, jnp.asarray(left),
        images, jnp.asarray(right), dest_map,
        ref.reshape(KYB * PL, 2 * K),
    )
    return out.reshape(KYB, PL, 2 * K)


def solution(mesh):
    placed = (
        P(("batch", "slab"), None, None),
        P(("batch", "slab")),
        P(("batch", "slab"), None),
        P(("batch", "slab")),
        P(),
        P(("batch", "slab"), None),
        P(),
        P("batch", "slab", None),
    )
    return jax.shard_map(
        per_device, mesh=mesh, in_specs=placed, out_specs=P("batch", "slab", None), check_vma=False
    )
```

```python
import math

import jax
import jax.numpy as jnp
import ml_dtypes
import numpy as np
from jax import lax
from jax.experimental import pallas as pl
from jax.experimental.pallas import tpu as pltpu
from jax.sharding import PartitionSpec as P

TAU_PRIOR = 4.0
PHASE_OFFSET = 0.1
MESH = pl.DeviceIdType.MESH

K = 384
NB = 16
NS = 8
PP = 8
KYB = K // NB
SHARED = 3
TILES = SHARED + 1
PL = 16
NDEF = 16
BF = jnp.bfloat16
F32 = jnp.float32
LAST = SHARED
EXTRA = 13
HOPS = ((1, 0), (3, 1), (2, 0), (3, 0), (1, 1), (2, 1), (0, 1))
NCNT = TILES + 3
MOVES = 40
GROUP = 64
TURNS = (
    (0, 1), (1, 0), (0, 3), (3, 0), (1, 1), (1, 3), (3, 3), (3, 1),
    (1, 2), (2, 1), (3, 2), (2, 3), (0, 2), (2, 0), (2, 2),
)


def tables():
    index = np.arange(K)
    angle = 2.0 * np.pi / K * ((index[:, None] * index[None, :]) % K)
    cosine = (np.cos(angle) / math.sqrt(K)).astype(np.float32)
    sine = (np.sin(angle) / math.sqrt(K)).astype(np.float32)

    def left(t):
        rows = [
            KYB * b + (6 * h + 2 * t + 1 + j if t < LAST else 0)
            for h in range(2)
            for b in range(NB)
            for j in range(2)
        ]
        return np.concatenate([cosine[rows], -sine[rows]], axis=0)

    both = np.stack([left(t) for t in range(TILES)], axis=0)
    right = np.concatenate(
        [np.concatenate([cosine, -sine], 1), np.concatenate([sine, cosine], 1)], 0
    )
    kind = ml_dtypes.bfloat16
    return both.astype(kind), right.astype(kind)


def kernel(
    classes, kinds_in, defocus, shifts, counts, left, img_in, right_in, dest_in, ref_in,
    out,
    img, right, dest, ref, scr, cscr, cwide, codes, cf, sc, vx, table_x, table_s, pq, wp, wm,
    sendb, recvb, crecv, zsend, zrecv, zgot, nsend, nrecv, msend, mrecv, wts, tws,
    img_m, right_m, dest_m, ref_m, code_s, code_r, row_s, row_r, z_s, z_r, y_s, y_r, n_s, n_r, m_s, m_r,
):
    mb = lax.axis_index("batch")
    ms = lax.axis_index("slab")
    core = lax.rem(ms, 2)
    zbase = ms - core
    mz = ms // 2
    me = mb * 2 + core
    my = mb // 4
    mx = lax.rem(mb, 4)

    def peer_of(turn):
        dy, dx = turn
        py = lax.rem(my + jnp.where(core == 0, dy, dx), 4)
        px = lax.rem(mx + jnp.where(core == 0, dx, 4 - dy), 4)
        return py * 4 + px

    barrier = pltpu.get_barrier_semaphore()
    loads = [pltpu.make_async_copy(img_in.at[p], img.at[p], img_m.at[p]) for p in range(PP)]
    load_right = pltpu.make_async_copy(right_in, right, right_m)
    load_dest = pltpu.make_async_copy(dest_in, dest, dest_m)
    load_ref = pltpu.make_async_copy(ref_in, ref, ref_m)
    for load in (load_dest, *loads, load_right, load_ref):
        load.start()

    def greet_plane(q, carry):
        i = lax.rem(me + q, 32)
        pl.semaphore_signal(
            barrier, inc=1, device_id=(i // 2, zbase + lax.rem(i, 2)), device_id_type=MESH
        )
        return carry

    def greet_slab(q, carry):
        pl.semaphore_signal(
            barrier, inc=1, device_id=(mb, lax.rem(ms + q, NS)), device_id_type=MESH
        )
        return carry

    lax.fori_loop(1, 32, greet_plane, 0)
    lax.fori_loop(1, NS, greet_slab, 0)

    def pick(index, values):
        got = jnp.full(index.shape, values[0])
        for i, value in enumerate(values[1:], 1):
            got = jnp.where(index == i, value, got)
        return got

    def square(k):
        half = jnp.where(k >= K // 2, k - K, k).astype(F32) * (1.0 / K)
        return half * half

    def phase(k, shift):
        turn = k.astype(F32) * shift
        turn = turn - K * jnp.floor((turn + 0.5) * (1.0 / K))
        return turn * (2.0 * math.pi / K)

    def to_plane(b, h, src, dst, send_sem, recv_sem):
        pltpu.make_async_remote_copy(
            src_ref=src, dst_ref=dst, send_sem=send_sem, recv_sem=recv_sem,
            device_id=(b, zbase + h), device_id_type=MESH,
        ).start()

    def compute(t):
        table = left[t]

        def one(p, carry):
            @pl.when(t == 0)
            def _():
                pltpu.make_async_copy(img_in.at[p], img.at[p], img_m.at[p]).wait()

            sec = jnp.dot(table, img[p], preferred_element_type=F32)
            for g in range(3):
                cols = slice(g * 128, (g + 1) * 128)
                scr[g, pl.ds(p, 64, stride=8), :] = sec[:64, cols]
                scr[3 + g, pl.ds(p, 64, stride=8), :] = sec[64:, cols]
            return carry

        lax.fori_loop(0, PP, one, 0)

        def pack(i, carry):
            start = pl.multiple_of(i * 16, 16)
            target = lax.rem(i, NB) * 2 + i // NB
            for g in range(6):
                sendb[t, target, :, pl.ds(g * 128, 128)] = scr[g, pl.ds(start, 16), :].astype(BF)
            return carry

        lax.fori_loop(0, 32, pack, 0)

    other = 1 - core

    def send_rows(t):
        for h in range(2):
            own = recvb.at[t, me]

            @pl.when(core == h)
            def _():
                pltpu.make_async_copy(sendb.at[t, me], own, row_r.at[t]).start()

            @pl.when(core != h)
            def _():
                to_plane(mb, h, sendb.at[t, mb * 2 + h], own, row_s.at[t], row_r.at[t])

            for turn in TURNS:
                b = peer_of(turn)
                to_plane(b, h, sendb.at[t, b * 2 + h], own, row_s.at[t], row_r.at[t])

    def send_last():
        t = LAST

        @pl.when(core == 0)
        def _():
            pltpu.make_async_copy(sendb.at[t, me], recvb.at[t, me], row_r.at[t]).start()

        @pl.when(core == 1)
        def _():
            to_plane(mb, 0, sendb.at[t, mb * 2], recvb.at[t, me], row_s.at[t], row_r.at[t])

        for turn in TURNS:
            b = peer_of(turn)
            to_plane(b, 0, sendb.at[t, b * 2], recvb.at[t, me], row_s.at[t], row_r.at[t])

    sub_p = lax.broadcasted_iota(jnp.int32, (PP, K), 0)
    col = lax.broadcasted_iota(jnp.int32, (PP, K), 1)
    row8 = lax.broadcasted_iota(jnp.int32, (PP, 128), 0)
    lane8 = lax.broadcasted_iota(jnp.int32, (PP, 128), 1)

    def tell():
        load_dest.wait()
        end = counts[:, 0:1]
        slab = jnp.zeros((PP, K), jnp.int32)
        for i in range(1, NS):
            slab = slab + jnp.where(col >= end, 1, 0)
            end = end + counts[:, i : i + 1]
        plane = pick(sub_p, [dest[pl.ds(classes[p], 1), :] for p in range(PP)])
        place = slab * 32 + plane
        spread = jnp.where(lax.rem(lane8, PP) == row8, 1.0, 0.0)
        kind8 = pick(row8, [kinds_in[p] for p in range(PP)])

        def turned(x):
            return lax.dot_general(
                x.astype(F32), spread, (((0,), (0,)), ((), ())),
                precision=lax.Precision.HIGHEST, preferred_element_type=F32,
            )

        cscr[...] = turned(place)
        shift_x = pick(row8, [shifts[0, p] for p in range(PP)])
        shift_y = pick(row8, [shifts[1, p] for p in range(PP)])
        person = turned(pick(lane8, [kind8, shift_x, shift_y]))
        slot_one = (lax.broadcasted_iota(jnp.int32, (1, 128), 1) // PP) & 1

        def arrange(d, carry):
            base = d // 2 * KYB
            step = 6 * lax.rem(d, 2)
            for n in range(TILES + SHARED + 3):
                for_two = []
                for j in range(2):
                    if n < SHARED:
                        ky = base + step + 2 * n + 1 + j
                    elif n == LAST:
                        ky = base
                    elif n < TILES + SHARED:
                        ky = K - (base + step + 2 * (n - TILES) + 1 + j)
                    else:
                        ky = jnp.minimum(base + EXTRA + step + 2 * (n - TILES - SHARED) + j, K - 1)
                    for_two.append(cscr[pl.ds(ky, 1), :])
                cwide[n : n + 1, :] = jnp.where(slot_one == 0, for_two[0], for_two[1] + PL)
            codes[d] = cwide[...].astype(BF)
            return carry

        cwide[...] = jnp.zeros_like(cwide)
        cwide[10:13, :] = person[0:3]
        lax.fori_loop(0, 2 * NB, arrange, 0)

    def tell_send():
        def send_codes(q, carry):
            i = lax.rem(me + q, 32)
            to_plane(i // 2, lax.rem(i, 2), codes.at[i], crecv.at[me], code_s, code_r)
            return carry

        pltpu.make_async_copy(codes.at[me], crecv.at[me], code_r).start()
        lax.fori_loop(1, 32, send_codes, 0)


    slot_of = (lane8 // 8) * 2 + (lane8 & 1)
    part = (lane8 // 2) & 3
    slot_ky = mb * KYB + jnp.where(slot_of < 2 * SHARED, 6 * core + 1 + slot_of, 0)
    slot_sq = square(slot_ky)
    every = [defocus[i] for i in range(NDEF)]

    def three(x):
        high = x.astype(BF)
        mid = (x - high.astype(F32)).astype(BF)
        low = (x - high.astype(F32) - mid.astype(F32)).astype(BF)
        return jnp.concatenate([high, mid, low], axis=0)

    def rows_of(shape, axis=0):
        return lax.broadcasted_iota(jnp.int32, shape, axis)

    def tabulate():
        turn = phase(rows_of((MOVES, K), 1), (rows_of((MOVES, K)) - 16).astype(F32))
        arg = pick(rows_of((NDEF, K)), every) * square(rows_of((NDEF, K), 1))
        spare = GROUP - MOVES - NDEF
        for n, (move, kind) in enumerate(
            (
                (jnp.cos(turn), None),
                (-jnp.sin(turn), None),
                (None, jnp.sin(arg)),
                (None, jnp.cos(arg)),
            )
        ):
            move = jnp.zeros((MOVES, K), F32) if move is None else move
            kind = jnp.zeros((NDEF, K), F32) if kind is None else kind
            full = jnp.concatenate([move, kind, jnp.zeros((spare, K), F32)], axis=0)
            table_x[:, pl.ds(n * K, K)] = three(full)
        turn = phase(slot_ky[0:1], (rows_of((MOVES, 128)) - 16).astype(F32))
        arg = pick(rows_of((NDEF, 128)), every) * slot_sq[0:1] + PHASE_OFFSET
        kind = part[0:1]
        move = jnp.where(kind == 2, -jnp.cos(turn), jnp.where(kind == 3, jnp.sin(turn), 0.0))
        tone = jnp.where(kind == 0, jnp.sin(arg), jnp.where(kind == 1, jnp.cos(arg), 0.0))
        table_s[...] = three(
            jnp.concatenate([move, tone, jnp.zeros((spare, 128), F32)], axis=0)
        )

    tell()
    tabulate()

    def produce(t, carry):
        compute(t)

        @pl.when(t == 0)
        def _():
            pl.semaphore_wait(barrier, 31 + NS - 1)
            tell_send()

        send_rows(t)
        return carry

    lax.fori_loop(0, 2, produce, 0)

    pltpu.make_async_copy(crecv, crecv, code_r).wait()

    def widen(i, carry):
        cf[pl.ds(pl.multiple_of(i * 16, 16), 16), :] = crecv[i].astype(F32)
        return carry

    lax.fori_loop(0, 32, widen, 0)

    lane = lax.broadcasted_iota(jnp.int32, (32, 128), 1)
    sub = lax.broadcasted_iota(jnp.int32, (32, 128), 0)
    mine = (lane // 16) == lax.rem(sub, 8)

    def pair_codes(row):
        got = cf[pl.ds(row, 32, stride=16), :]
        return jnp.sum(jnp.where(mine, got, 0.0).reshape(4, 8, 128), axis=1)

    spot = lax.broadcasted_iota(jnp.int32, (256, 128), 0).astype(F32)

    def one_hot(code4):
        return jnp.concatenate(
            [
                jnp.where(spot == code4[g : g + 1, :], 1.0, 0.0).astype(BF)
                for g in range(4)
            ],
            axis=1,
        )

    def to_slab(src, dst, send_sem, recv_sem):
        for dz, flip in HOPS:
            z = lax.rem(mz + jnp.where(core == 0, dz, 4 - dz), 4)
            peer = z * 2 + (1 - core if flip else core)
            pltpu.make_async_remote_copy(
                src_ref=src(peer), dst_ref=dst, send_sem=send_sem, recv_sem=recv_sem,
                device_id=(mb, peer), device_id_type=MESH,
            ).start()

    kind4 = pair_codes(10)

    def tally():
        spot_z = lax.broadcasted_iota(jnp.int32, (128, 128), 0).astype(F32)
        slot_k = ((lax.broadcasted_iota(jnp.int32, (4, 128), 1) // PP) & 1).astype(F32)
        which = kind4 + NDEF * slot_k

        def hot(code4):
            return jnp.concatenate(
                [
                    jnp.where(spot_z == code4[g : g + 1, :], 1.0, 0.0).astype(BF)
                    for g in range(4)
                ],
                axis=1,
            )

        def one(n, acc):
            code4 = pair_codes(jnp.where(n < TILES, n, n + SHARED))
            flat = code4 - 16.0 * jnp.floor(code4 * (1.0 / 16)) + 16.0 * jnp.floor(code4 * (1.0 / 32))
            group = ((n & 3) * 2 * NDEF).astype(F32)
            return acc + lax.dot_general(
                hot(flat), hot(which + group), (((1,), (1,)), ((), ())), preferred_element_type=F32
            )

        for half, (low, high) in enumerate(((0, 4), (4, NCNT))):
            acc = lax.fori_loop(low, high, one, jnp.zeros((128, 128), F32))
            nsend[:, :, pl.ds(half * 128, 128)] = acc.astype(BF).reshape(NS, PL, 128)
        to_slab(lambda peer: nsend.at[peer], nrecv.at[ms], n_s, n_r)
        pltpu.make_async_copy(nsend.at[ms], nrecv.at[ms], n_r).start()

    entry = (rows_of((3 * GROUP, 128)) & (GROUP - 1)).astype(F32)

    def chosen(move4, table):
        hot = jnp.concatenate(
            [
                jnp.where(
                    (entry == move4[g : g + 1, :] + 16.0)
                    | (entry == kind4[g : g + 1, :] + float(MOVES)),
                    1.0,
                    0.0,
                ).astype(BF)
                for g in range(4)
            ],
            axis=1,
        )
        return lax.dot_general(
            hot, table, (((0,), (0,)), ((), ())), preferred_element_type=F32
        )

    vx[...] = chosen(pair_codes(11), table_x[...])
    scal = chosen(pair_codes(12), table_s[...])
    sc[0] = scal
    for t in range(1, TILES):
        sc[t] = pltpu.roll(scal, 128 - 8 * t, 1)

    load_right.wait()

    def process(t):
        pltpu.make_async_copy(recvb.at[t], recvb.at[t], row_r.at[t]).wait()

        def half(m, carry):
            block = recvb[t, pl.ds(m * 16, 16)].reshape(256, 2 * K)
            start = pl.multiple_of(m * 256, 256)
            pq[0, pl.ds(start, 256), :] = jnp.dot(
                block[:, :K], right[pl.ds(0, K), :], preferred_element_type=F32
            )
            pq[1, pl.ds(start, 256), :] = jnp.dot(
                block[:, K:], right[pl.ds(K, K), :], preferred_element_type=F32
            )
            return carry

        lax.fori_loop(0, 2, half, 0)

        def weigh(i, carry):
            got = [[], [], [], []]
            for j in range(2):
                rows = pl.ds(pl.multiple_of(i * 16 + j * 8, 8), 8)
                scal = sc[t, rows, :]
                sa, ca, er, ei = [scal[:, 2 * n + j : 2 * n + j + 1] for n in range(4)]
                exr, exi, sb, cb = [vx[rows, pl.ds(n * K, K)] for n in range(4)]
                pr, pi = pq[0, rows, pl.ds(0, K)], pq[0, rows, pl.ds(K, K)]
                qr, qi = pq[1, rows, pl.ds(0, K)], pq[1, rows, pl.ds(K, K)]
                ctf = sa * cb + ca * sb
                gr, gi = ctf * exr, ctf * exi
                fa, fb, fc, fd = er * gr, ei * gi, er * gi, ei * gr
                sr, si = pr + qr, pi + qi
                fr, fi = fa - fb, fc + fd
                got[0].append(sr * fr - si * fi)
                got[1].append(sr * fi + si * fr)
                sr, si = pr - qr, pi - qi
                fr, fi = fa + fb, fc - fd
                got[2].append(sr * fr - si * fi)
                got[3].append(sr * fi + si * fr)
            rows = pl.ds(pl.multiple_of(i * 16, 16), 16)
            for n in range(4):
                to = wp if n < 2 else wm
                to[rows, pl.ds((n % 2) * K, K)] = jnp.concatenate(got[n], axis=0).astype(BF)
            return carry

        lax.fori_loop(0, 32, weigh, 0, unroll=4)

        def total(hot, rows):
            return jnp.dot(hot, rows, preferred_element_type=F32).astype(BF).reshape(NS, 32, 2 * K)

        def give(start, size, dst, send_sem, recv_sem):
            rows = pl.ds(start, size)
            to_slab(lambda peer: zsend.at[t, peer, rows], dst, send_sem, recv_sem)
            pltpu.make_async_copy(zsend.at[t, ms, rows], dst, recv_sem).start()

        @pl.when(t < LAST)
        def _():
            zsend[t, :, pl.ds(32, 32), :] = total(one_hot(pair_codes(TILES + t)), wm[...])
            whole = jnp.logical_or(t < SHARED - 1, core == 0)

            @pl.when(whole)
            def _():
                give(32, 32, zrecv.at[t, ms, pl.ds(32, 32)], y_s.at[t], y_r.at[t])

            @pl.when(jnp.logical_not(whole))
            def _():
                give(32, PL, zrecv.at[t, ms, pl.ds(32, PL)], y_s.at[t], y_r.at[t])

        zsend[t, :, pl.ds(0, 32), :] = total(one_hot(pair_codes(t)), wp[...])

        @pl.when(t < LAST)
        def _():
            give(0, 32, zrecv.at[t, ms, pl.ds(0, 32)], z_s.at[t], z_r.at[t])

        @pl.when(t == LAST)
        def _():
            give(0, PL, zgot.at[mz], z_s.at[t], z_r.at[t])

    def weights():
        lane_k = lax.broadcasted_iota(jnp.int32, (32, 128), 1)
        own_ky = mb * KYB + lax.broadcasted_iota(jnp.int32, (32, 128), 0)
        arg2_y = 2.0 * (pick(lane_k & (NDEF - 1), every) * square(own_ky) + PHASE_OFFSET)
        group = lane_k // NDEF
        tws[...] = jnp.where(
            group == 0,
            -0.5 * jnp.cos(arg2_y),
            jnp.where(group == 1, 0.5 * jnp.sin(arg2_y), jnp.where(group == 2, 0.5, 0.0)),
        )
        row_k = lax.broadcasted_iota(jnp.int32, (NDEF, K), 0)
        col_k = lax.broadcasted_iota(jnp.int32, (NDEF, K), 1)
        arg2_x = 2.0 * (pick(row_k, every) * square(col_k))
        rw = jnp.concatenate(
            [
                jnp.cos(arg2_x),
                jnp.sin(arg2_x),
                jnp.ones((NDEF, K), F32),
                jnp.zeros((128 - 3 * NDEF, K), F32),
            ],
            axis=0,
        )
        pltpu.make_async_copy(nrecv, nrecv, n_r).wait()

        def one(h, carry):
            x = nrecv[h].astype(F32)
            for z in range(1, NS // 2):
                x += nrecv[2 * z + h].astype(F32)
            own, more = 6 * h + 1, 6 * h + EXTRA
            lane = lax.broadcasted_iota(jnp.int32, (PL, 128), 1)
            blocks = []
            for g in range(2 * NCNT):
                part = x[:, g // 8 * 128 : g // 8 * 128 + 128]
                turn = [
                    pltpu.roll(part, (NDEF * (n - g)) % 128, 1) if (n - g) % 8 else part
                    for n in range(3)
                ]
                blocks.append(
                    jnp.where(lane < NDEF, turn[0], jnp.where(lane < 2 * NDEF, turn[1], turn[2]))
                )
            x = jnp.concatenate(blocks, axis=0)

            def times(part, i, rows):
                return (part.reshape(rows, PL, 128) * tws[pl.ds(i, rows), :][:, None, :]).reshape(
                    rows * PL, 128
                )

            scaled = jnp.concatenate(
                [times(x[:96], own, 6), times(x[96:128], 0, 2), times(x[128:], more, 6)], axis=0
            )
            res = jnp.dot(
                scaled, rw, precision=lax.Precision.HIGHEST, preferred_element_type=F32
            )
            res = 1.0 / (res + TAU_PRIOR)
            wts[pl.ds(pl.multiple_of(own * PL, PL), 96), :] = res[:96]
            wts[pl.ds(pl.multiple_of(more * PL, PL), 96), :] = res[128:]

            @pl.when(h == 0)
            def _():
                wts[pl.ds(0, PL), :] = res[96:112]

            return carry

        lax.fori_loop(0, 2, one, 0)

    def finish(i, sums):
        rows = pl.ds(pl.multiple_of(i * PL, PL), PL)
        inverse = wts[rows, :]
        for h in range(2):
            cols = pl.ds(h * K, K)
            top = TAU_PRIOR * ref[rows, cols].astype(F32) + sums[:, h * K : (h + 1) * K]
            out[rows, cols] = (top * inverse).astype(BF)

    def gather(t):
        @pl.when(t < SHARED - 1)
        def _():
            some = zrecv.at[t, :, pl.ds(32, 32)]
            pltpu.make_async_copy(some, some, y_r.at[t]).wait()

        @pl.when(t == SHARED - 1)
        def _():
            some = zrecv.at[t, pl.ds(0, 6), pl.ds(32, 32)]
            pltpu.make_async_copy(some, some, y_r.at[t]).wait()

        def over_z(h, start):
            rows = pl.ds(pl.multiple_of(start, PL), PL)
            x = zrecv[t, h, rows, :].astype(F32)
            for z in range(1, NS // 2):
                x += zrecv[t, 2 * z + h, rows, :].astype(F32)
            return x

        def mirror(m, carry):
            msend[t, m] = over_z(m // 2, 2 * PL + lax.rem(m, 2) * PL).astype(BF)
            return carry

        def pass_on(size):
            rows = pl.ds(0, size)
            lax.fori_loop(0, size, mirror, 0)
            pltpu.make_async_remote_copy(
                src_ref=msend.at[t, rows], dst_ref=mrecv.at[t, rows],
                send_sem=m_s.at[t], recv_sem=m_r.at[t],
                device_id=(NB - 1 - mb, ms), device_id_type=MESH,
            ).start()

        pl.when(t < SHARED - 1)(lambda: pass_on(4))
        pl.when(t == SHARED - 1)(lambda: pass_on(3))

        some = zrecv.at[t, :, pl.ds(0, 32)]
        pltpu.make_async_copy(some, some, z_r.at[t]).wait()

        def own(m, carry):
            h, j = m // 2, lax.rem(m, 2)
            finish(6 * h + 2 * t + 1 + j, over_z(h, j * PL))
            return carry

        lax.fori_loop(0, 4, own, 0)

    def drain(src, send_sem, recv_sem):
        return pltpu.make_async_remote_copy(
            src_ref=src, dst_ref=src, send_sem=send_sem, recv_sem=recv_sem,
            device_id=(mb, ms), device_id_type=MESH,
        )

    def mirrored(t, carry):
        @pl.when(t < SHARED - 1)
        def _():
            drain(msend.at[t], m_s.at[t], m_r.at[t]).wait()

        @pl.when(t == SHARED - 1)
        def _():
            drain(msend.at[t, pl.ds(0, 3)], m_s.at[t], m_r.at[t]).wait()


        def one(m, inner):
            i = 6 * (m // 2) + 2 * t + 1 + lax.rem(m, 2)

            @pl.when(i < KYB // 2)
            def _():
                finish(KYB - i, mrecv[t, m].astype(F32))

            return inner

        lax.fori_loop(0, 4, one, 0)
        return carry

    def consume(t, carry):
        @pl.when(jnp.logical_or(t < LAST, core == 0))
        def _():
            process(t)

        @pl.when(t < 2)
        def _():
            compute(t + 2)

        @pl.when(t == 0)
        def _():
            send_rows(2)

        @pl.when(t == 1)
        def _():
            send_last()
            weights()

        @pl.when(jnp.logical_or(t == 1, t == 2))
        def _():
            gather(t - 1)

        @pl.when(t == LAST)
        def _():
            lax.fori_loop(0, 2, mirrored, 0)

        return carry

    tally()
    load_ref.wait()
    lax.fori_loop(0, TILES, consume, 0)

    gather(SHARED - 1)
    pltpu.make_async_copy(zgot, zgot, z_r.at[LAST]).wait()
    x = zgot[0].astype(F32)
    for z in range(1, NS // 2):
        x += zgot[z].astype(F32)
    finish(0, x)

    mirrored(SHARED - 1, 0)

    drain(crecv.at[pl.ds(0, 31)], code_s, code_r).wait_send()
    drain(nsend.at[pl.ds(0, 7)], n_s, n_r).wait_send()
    def drain_tile(t, carry):
        drain(sendb.at[t, pl.ds(0, 31)], row_s.at[t], row_r.at[t]).wait_send()
        whole = jnp.logical_or(t < SHARED - 1, core == 0)

        @pl.when(whole)
        def _():
            drain(zsend.at[t, pl.ds(0, 7), pl.ds(0, 32)], y_s.at[t], y_r.at[t]).wait_send()

        @pl.when(jnp.logical_not(whole))
        def _():
            drain(zsend.at[t, pl.ds(0, 7), pl.ds(0, PL)], y_s.at[t], y_r.at[t]).wait_send()

        drain(zsend.at[t, pl.ds(0, 7), pl.ds(0, 32)], z_s.at[t], z_r.at[t]).wait_send()
        return carry

    lax.fori_loop(0, SHARED, drain_tile, 0)

    @pl.when(core == 0)
    def _():
        drain(sendb.at[LAST, pl.ds(0, 15)], row_s.at[LAST], row_r.at[LAST]).wait_send()
        drain(zsend.at[LAST, pl.ds(0, 7), pl.ds(0, PL)], z_s.at[LAST], z_r.at[LAST]).wait_send()

    @pl.when(core == 1)
    def _():
        drain(sendb.at[LAST, pl.ds(0, 16)], row_s.at[LAST], row_r.at[LAST]).wait_send()


def per_device(images, classes, shifts, defocus_class, defocus, run_counts, dest_map, ref):
    left, right = tables()
    vmem = pl.BlockSpec(memory_space=pltpu.VMEM)
    smem = pl.BlockSpec(memory_space=pltpu.SMEM)
    far = pl.BlockSpec(memory_space=pl.ANY)
    dma = pltpu.SemaphoreType.DMA
    out = pl.pallas_call(
        kernel,
        out_shape=jax.ShapeDtypeStruct((KYB * PL, 2 * K), BF),
        in_specs=[smem] * 4 + [vmem] * 2 + [far] * 4,
        out_specs=vmem,
        scratch_shapes=[
            pltpu.VMEM((PP, K, K), BF),
            pltpu.VMEM((2 * K, 2 * K), BF),
            pltpu.VMEM(dest_map.shape, jnp.int32),
            pltpu.VMEM((KYB * PL, 2 * K), BF),
            pltpu.VMEM((6, 64 * PP, 128), F32),
            pltpu.VMEM((K, 128), F32),
            pltpu.VMEM((16, 128), F32),
            pltpu.VMEM((32, 16, 128), BF),
            pltpu.VMEM((32 * 16, 128), F32),
            pltpu.VMEM((TILES, 512, 128), F32),
            pltpu.VMEM((512, 4 * K), F32),
            pltpu.VMEM((3 * GROUP, 4 * K), BF),
            pltpu.VMEM((3 * GROUP, 128), BF),
            pltpu.VMEM((2, 512, 2 * K), F32),
            pltpu.VMEM((512, 2 * K), BF),
            pltpu.VMEM((512, 2 * K), BF),
            pltpu.VMEM((TILES, 32, 16, 2 * K), BF),
            pltpu.VMEM((TILES, 32, 16, 2 * K), BF),
            pltpu.VMEM((32, 16, 128), BF),
            pltpu.VMEM((TILES, NS, 64, 2 * K), BF),
            pltpu.VMEM((SHARED, NS, 64, 2 * K), BF),
            pltpu.VMEM((NS // 2, PL, 2 * K), BF),
            pltpu.VMEM((NS, PL, 256), BF),
            pltpu.VMEM((NS, PL, 256), BF),
            pltpu.VMEM((SHARED, 4, PL, 2 * K), BF),
            pltpu.VMEM((SHARED, 4, PL, 2 * K), BF),
            pltpu.VMEM(((KYB + 1) * PL, K), F32),
            pltpu.VMEM((32, 128), F32),
            dma((PP,)), dma, dma, dma, dma, dma, dma((TILES,)), dma((TILES,)),
            dma((TILES,)), dma((TILES,)), dma((SHARED,)), dma((SHARED,)), dma, dma,
            dma((SHARED,)), dma((SHARED,)),
        ],
        compiler_params=pltpu.CompilerParams(
            collective_id=0, has_side_effects=True, vmem_limit_bytes=60 * 1024 * 1024
        ),
    )(
        classes, defocus_class, defocus, shifts.T, run_counts, jnp.asarray(left),
        images, jnp.asarray(right), dest_map,
        ref.reshape(KYB * PL, 2 * K),
    )
    return out.reshape(KYB, PL, 2 * K)


def solution(mesh):
    placed = (
        P(("batch", "slab"), None, None),
        P(("batch", "slab")),
        P(("batch", "slab"), None),
        P(("batch", "slab")),
        P(),
        P(("batch", "slab"), None),
        P(),
        P("batch", "slab", None),
    )
    return jax.shard_map(
        per_device, mesh=mesh, in_specs=placed, out_specs=P("batch", "slab", None), check_vma=False
    )
```

```python
import math

import jax
import jax.numpy as jnp
import ml_dtypes
import numpy as np
from jax import lax
from jax.experimental import pallas as pl
from jax.experimental.pallas import tpu as pltpu
from jax.sharding import PartitionSpec as P

TAU_PRIOR = 4.0
PHASE_OFFSET = 0.1
MESH = pl.DeviceIdType.MESH

K = 384
NB = 16
NS = 8
PP = 8
KYB = K // NB
SHARED = 3
TILES = SHARED + 1
PL = 16
NDEF = 16
BF = jnp.bfloat16
F32 = jnp.float32
LAST = SHARED
EXTRA = 13
HOPS = ((1, 0), (3, 1), (2, 0), (3, 0), (1, 1), (2, 1), (0, 1))
NCNT = TILES + 3
MOVES = 40
GROUP = 64
TURNS = (
    (0, 1), (1, 0), (0, 3), (3, 0), (1, 1), (1, 3), (3, 3), (3, 1),
    (1, 2), (2, 1), (3, 2), (2, 3), (0, 2), (2, 0), (2, 2),
)


def tables():
    index = np.arange(K)
    angle = 2.0 * np.pi / K * ((index[:, None] * index[None, :]) % K)
    cosine = (np.cos(angle) / math.sqrt(K)).astype(np.float32)
    sine = (np.sin(angle) / math.sqrt(K)).astype(np.float32)

    def left(t):
        rows = [
            KYB * b + (6 * h + 2 * t + 1 + j if t < LAST else 0)
            for h in range(2)
            for b in range(NB)
            for j in range(2)
        ]
        return np.concatenate([cosine[rows], -sine[rows]], axis=0)

    both = np.stack([left(t) for t in range(TILES)], axis=0)
    right = np.concatenate(
        [np.concatenate([cosine, -sine], 1), np.concatenate([sine, cosine], 1)], 0
    )
    kind = ml_dtypes.bfloat16
    return both.astype(kind), right.astype(kind)


def kernel(
    classes, kinds_in, defocus, shifts, counts, left, img_in, right_in, dest_in, ref_in,
    out,
    img, right, dest, ref, scr, cscr, cwide, codes, cf, sc, vx, table_x, table_s, pq, wp, wm,
    sendb, recvb, crecv, zsend, zrecv, zgot, nsend, nrecv, msend, mrecv, wts, tws, held,
    out_m, img_m, right_m, dest_m, ref_m, code_s, code_r, row_s, row_r, z_s, z_r, y_s, y_r, n_s, n_r, m_s, m_r,
):
    mb = lax.axis_index("batch")
    ms = lax.axis_index("slab")
    core = lax.rem(ms, 2)
    zbase = ms - core
    mz = ms // 2
    me = mb * 2 + core
    my = mb // 4
    mx = lax.rem(mb, 4)

    def peer_of(turn):
        dy, dx = turn
        py = lax.rem(my + jnp.where(core == 0, dy, dx), 4)
        px = lax.rem(mx + jnp.where(core == 0, dx, 4 - dy), 4)
        return py * 4 + px

    barrier = pltpu.get_barrier_semaphore()
    loads = [pltpu.make_async_copy(img_in.at[p], img.at[p], img_m.at[p]) for p in range(PP)]
    load_right = pltpu.make_async_copy(right_in, right, right_m)
    load_dest = pltpu.make_async_copy(dest_in, dest, dest_m)
    load_ref = pltpu.make_async_copy(ref_in, ref, ref_m)
    for load in (load_dest, *loads, load_right, load_ref):
        load.start()

    def greet_plane(q, carry):
        i = lax.rem(me + q, 32)
        pl.semaphore_signal(
            barrier, inc=1, device_id=(i // 2, zbase + lax.rem(i, 2)), device_id_type=MESH
        )
        return carry

    def greet_slab(q, carry):
        pl.semaphore_signal(
            barrier, inc=1, device_id=(mb, lax.rem(ms + q, NS)), device_id_type=MESH
        )
        return carry

    lax.fori_loop(1, 32, greet_plane, 0)
    lax.fori_loop(1, NS, greet_slab, 0)

    def pick(index, values):
        got = jnp.full(index.shape, values[0])
        for i, value in enumerate(values[1:], 1):
            got = jnp.where(index == i, value, got)
        return got

    def square(k):
        half = jnp.where(k >= K // 2, k - K, k).astype(F32) * (1.0 / K)
        return half * half

    def phase(k, shift):
        turn = k.astype(F32) * shift
        turn = turn - K * jnp.floor((turn + 0.5) * (1.0 / K))
        return turn * (2.0 * math.pi / K)

    def to_plane(b, h, src, dst, send_sem, recv_sem):
        pltpu.make_async_remote_copy(
            src_ref=src, dst_ref=dst, send_sem=send_sem, recv_sem=recv_sem,
            device_id=(b, zbase + h), device_id_type=MESH,
        ).start()

    def compute(t):
        table = left[t]

        def one(p, carry):
            @pl.when(t == 0)
            def _():
                pltpu.make_async_copy(img_in.at[p], img.at[p], img_m.at[p]).wait()

            sec = jnp.dot(table, img[p], preferred_element_type=F32)
            for g in range(3):
                cols = slice(g * 128, (g + 1) * 128)
                scr[g, pl.ds(p, 64, stride=8), :] = sec[:64, cols]
                scr[3 + g, pl.ds(p, 64, stride=8), :] = sec[64:, cols]
            return carry

        lax.fori_loop(0, PP, one, 0)

        def pack(i, carry):
            start = pl.multiple_of(i * 16, 16)
            target = lax.rem(i, NB) * 2 + i // NB
            for g in range(6):
                sendb[t, target, :, pl.ds(g * 128, 128)] = scr[g, pl.ds(start, 16), :].astype(BF)
            return carry

        lax.fori_loop(0, 32, pack, 0)

    other = 1 - core

    def send_rows(t):
        for h in range(2):
            own = recvb.at[t, me]

            @pl.when(core == h)
            def _():
                pltpu.make_async_copy(sendb.at[t, me], own, row_r.at[t]).start()

            @pl.when(core != h)
            def _():
                to_plane(mb, h, sendb.at[t, mb * 2 + h], own, row_s.at[t], row_r.at[t])

            for turn in TURNS:
                b = peer_of(turn)
                to_plane(b, h, sendb.at[t, b * 2 + h], own, row_s.at[t], row_r.at[t])

    def send_last():
        t = LAST

        @pl.when(core == 0)
        def _():
            pltpu.make_async_copy(sendb.at[t, me], recvb.at[t, me], row_r.at[t]).start()

        @pl.when(core == 1)
        def _():
            to_plane(mb, 0, sendb.at[t, mb * 2], recvb.at[t, me], row_s.at[t], row_r.at[t])

        for turn in TURNS:
            b = peer_of(turn)
            to_plane(b, 0, sendb.at[t, b * 2], recvb.at[t, me], row_s.at[t], row_r.at[t])

    sub_p = lax.broadcasted_iota(jnp.int32, (PP, K), 0)
    col = lax.broadcasted_iota(jnp.int32, (PP, K), 1)
    row8 = lax.broadcasted_iota(jnp.int32, (PP, 128), 0)
    lane8 = lax.broadcasted_iota(jnp.int32, (PP, 128), 1)

    def tell():
        load_dest.wait()
        end = counts[:, 0:1]
        slab = jnp.zeros((PP, K), jnp.int32)
        for i in range(1, NS):
            slab = slab + jnp.where(col >= end, 1, 0)
            end = end + counts[:, i : i + 1]
        plane = pick(sub_p, [dest[pl.ds(classes[p], 1), :] for p in range(PP)])
        place = slab * 32 + plane
        spread = jnp.where(lax.rem(lane8, PP) == row8, 1.0, 0.0)
        kind8 = pick(row8, [kinds_in[p] for p in range(PP)])

        def turned(x):
            return lax.dot_general(
                x.astype(F32), spread, (((0,), (0,)), ((), ())),
                precision=lax.Precision.HIGHEST, preferred_element_type=F32,
            )

        cscr[...] = turned(place)
        shift_x = pick(row8, [shifts[0, p] for p in range(PP)])
        shift_y = pick(row8, [shifts[1, p] for p in range(PP)])
        person = turned(pick(lane8, [kind8, shift_x, shift_y]))
        slot_one = (lax.broadcasted_iota(jnp.int32, (1, 128), 1) // PP) & 1

        def arrange(d, carry):
            base = d // 2 * KYB
            step = 6 * lax.rem(d, 2)
            for n in range(TILES + SHARED + 3):
                for_two = []
                for j in range(2):
                    if n < SHARED:
                        ky = base + step + 2 * n + 1 + j
                    elif n == LAST:
                        ky = base
                    elif n < TILES + SHARED:
                        ky = K - (base + step + 2 * (n - TILES) + 1 + j)
                    else:
                        ky = jnp.minimum(base + EXTRA + step + 2 * (n - TILES - SHARED) + j, K - 1)
                    for_two.append(cscr[pl.ds(ky, 1), :])
                cwide[n : n + 1, :] = jnp.where(slot_one == 0, for_two[0], for_two[1] + PL)
            codes[d] = cwide[...].astype(BF)
            return carry

        cwide[...] = jnp.zeros_like(cwide)
        cwide[10:13, :] = person[0:3]
        lax.fori_loop(0, 2 * NB, arrange, 0)

    def tell_send():
        def send_codes(q, carry):
            i = lax.rem(me + q, 32)
            to_plane(i // 2, lax.rem(i, 2), codes.at[i], crecv.at[me], code_s, code_r)
            return carry

        pltpu.make_async_copy(codes.at[me], crecv.at[me], code_r).start()
        lax.fori_loop(1, 32, send_codes, 0)


    slot_of = (lane8 // 8) * 2 + (lane8 & 1)
    part = (lane8 // 2) & 3
    slot_ky = mb * KYB + jnp.where(slot_of < 2 * SHARED, 6 * core + 1 + slot_of, 0)
    slot_sq = square(slot_ky)
    every = [defocus[i] for i in range(NDEF)]

    def three(x):
        high = x.astype(BF)
        mid = (x - high.astype(F32)).astype(BF)
        low = (x - high.astype(F32) - mid.astype(F32)).astype(BF)
        return jnp.concatenate([high, mid, low], axis=0)

    def rows_of(shape, axis=0):
        return lax.broadcasted_iota(jnp.int32, shape, axis)

    def tabulate():
        turn = phase(rows_of((MOVES, K), 1), (rows_of((MOVES, K)) - 16).astype(F32))
        arg = pick(rows_of((NDEF, K)), every) * square(rows_of((NDEF, K), 1))
        spare = GROUP - MOVES - NDEF
        for n, (move, kind) in enumerate(
            (
                (jnp.cos(turn), None),
                (-jnp.sin(turn), None),
                (None, jnp.sin(arg)),
                (None, jnp.cos(arg)),
            )
        ):
            move = jnp.zeros((MOVES, K), F32) if move is None else move
            kind = jnp.zeros((NDEF, K), F32) if kind is None else kind
            full = jnp.concatenate([move, kind, jnp.zeros((spare, K), F32)], axis=0)
            table_x[:, pl.ds(n * K, K)] = three(full)
        turn = phase(slot_ky[0:1], (rows_of((MOVES, 128)) - 16).astype(F32))
        arg = pick(rows_of((NDEF, 128)), every) * slot_sq[0:1] + PHASE_OFFSET
        kind = part[0:1]
        move = jnp.where(kind == 2, -jnp.cos(turn), jnp.where(kind == 3, jnp.sin(turn), 0.0))
        tone = jnp.where(kind == 0, jnp.sin(arg), jnp.where(kind == 1, jnp.cos(arg), 0.0))
        table_s[...] = three(
            jnp.concatenate([move, tone, jnp.zeros((spare, 128), F32)], axis=0)
        )

    tell()
    tabulate()

    def produce(t, carry):
        compute(t)

        @pl.when(t == 0)
        def _():
            pl.semaphore_wait(barrier, 31 + NS - 1)
            tell_send()

        send_rows(t)
        return carry

    lax.fori_loop(0, 2, produce, 0)

    pltpu.make_async_copy(crecv, crecv, code_r).wait()

    def widen(i, carry):
        cf[pl.ds(pl.multiple_of(i * 16, 16), 16), :] = crecv[i].astype(F32)
        return carry

    lax.fori_loop(0, 32, widen, 0)

    lane = lax.broadcasted_iota(jnp.int32, (32, 128), 1)
    sub = lax.broadcasted_iota(jnp.int32, (32, 128), 0)
    mine = (lane // 16) == lax.rem(sub, 8)

    def pair_codes(row):
        got = cf[pl.ds(row, 32, stride=16), :]
        return jnp.sum(jnp.where(mine, got, 0.0).reshape(4, 8, 128), axis=1)

    spot = lax.broadcasted_iota(jnp.int32, (256, 128), 0).astype(F32)

    def one_hot(code4):
        return jnp.concatenate(
            [
                jnp.where(spot == code4[g : g + 1, :], 1.0, 0.0).astype(BF)
                for g in range(4)
            ],
            axis=1,
        )

    def to_slab(src, dst, send_sem, recv_sem):
        for dz, flip in HOPS:
            z = lax.rem(mz + jnp.where(core == 0, dz, 4 - dz), 4)
            peer = z * 2 + (1 - core if flip else core)
            pltpu.make_async_remote_copy(
                src_ref=src(peer), dst_ref=dst, send_sem=send_sem, recv_sem=recv_sem,
                device_id=(mb, peer), device_id_type=MESH,
            ).start()

    kind4 = pair_codes(10)

    def tally():
        spot_z = lax.broadcasted_iota(jnp.int32, (128, 128), 0).astype(F32)
        slot_k = ((lax.broadcasted_iota(jnp.int32, (4, 128), 1) // PP) & 1).astype(F32)
        which = kind4 + NDEF * slot_k

        def hot(code4):
            return jnp.concatenate(
                [
                    jnp.where(spot_z == code4[g : g + 1, :], 1.0, 0.0).astype(BF)
                    for g in range(4)
                ],
                axis=1,
            )

        def one(n, acc):
            code4 = pair_codes(jnp.where(n < TILES, n, n + SHARED))
            flat = code4 - 16.0 * jnp.floor(code4 * (1.0 / 16)) + 16.0 * jnp.floor(code4 * (1.0 / 32))
            group = ((n & 3) * 2 * NDEF).astype(F32)
            return acc + lax.dot_general(
                hot(flat), hot(which + group), (((1,), (1,)), ((), ())), preferred_element_type=F32
            )

        for half, (low, high) in enumerate(((0, 4), (4, NCNT))):
            acc = lax.fori_loop(low, high, one, jnp.zeros((128, 128), F32))
            nsend[:, :, pl.ds(half * 128, 128)] = acc.astype(BF).reshape(NS, PL, 128)
        to_slab(lambda peer: nsend.at[peer], nrecv.at[ms], n_s, n_r)
        pltpu.make_async_copy(nsend.at[ms], nrecv.at[ms], n_r).start()

    entry = (rows_of((3 * GROUP, 128)) & (GROUP - 1)).astype(F32)

    def chosen(move4, table):
        hot = jnp.concatenate(
            [
                jnp.where(
                    (entry == move4[g : g + 1, :] + 16.0)
                    | (entry == kind4[g : g + 1, :] + float(MOVES)),
                    1.0,
                    0.0,
                ).astype(BF)
                for g in range(4)
            ],
            axis=1,
        )
        return lax.dot_general(
            hot, table, (((0,), (0,)), ((), ())), preferred_element_type=F32
        )

    vx[...] = chosen(pair_codes(11), table_x[...])
    scal = chosen(pair_codes(12), table_s[...])
    sc[0] = scal
    for t in range(1, TILES):
        sc[t] = pltpu.roll(scal, 128 - 8 * t, 1)

    load_right.wait()

    def process(t):
        pltpu.make_async_copy(recvb.at[t], recvb.at[t], row_r.at[t]).wait()

        def half(m, carry):
            block = recvb[t, pl.ds(m * 16, 16)].reshape(256, 2 * K)
            start = pl.multiple_of(m * 256, 256)
            pq[0, pl.ds(start, 256), :] = jnp.dot(
                block[:, :K], right[pl.ds(0, K), :], preferred_element_type=F32
            )
            pq[1, pl.ds(start, 256), :] = jnp.dot(
                block[:, K:], right[pl.ds(K, K), :], preferred_element_type=F32
            )
            return carry

        lax.fori_loop(0, 2, half, 0)

        def weigh(i, carry):
            got = [[], [], [], []]
            for j in range(2):
                rows = pl.ds(pl.multiple_of(i * 16 + j * 8, 8), 8)
                scal = sc[t, rows, :]
                sa, ca, er, ei = [scal[:, 2 * n + j : 2 * n + j + 1] for n in range(4)]
                exr, exi, sb, cb = [vx[rows, pl.ds(n * K, K)] for n in range(4)]
                pr, pi = pq[0, rows, pl.ds(0, K)], pq[0, rows, pl.ds(K, K)]
                qr, qi = pq[1, rows, pl.ds(0, K)], pq[1, rows, pl.ds(K, K)]
                ctf = sa * cb + ca * sb
                gr, gi = ctf * exr, ctf * exi
                fa, fb, fc, fd = er * gr, ei * gi, er * gi, ei * gr
                sr, si = pr + qr, pi + qi
                fr, fi = fa - fb, fc + fd
                got[0].append(sr * fr - si * fi)
                got[1].append(sr * fi + si * fr)
                sr, si = pr - qr, pi - qi
                fr, fi = fa + fb, fc - fd
                got[2].append(sr * fr - si * fi)
                got[3].append(sr * fi + si * fr)
            rows = pl.ds(pl.multiple_of(i * 16, 16), 16)
            for n in range(4):
                to = wp if n < 2 else wm
                to[rows, pl.ds((n % 2) * K, K)] = jnp.concatenate(got[n], axis=0).astype(BF)
            return carry

        lax.fori_loop(0, 32, weigh, 0, unroll=4)

        def total(hot, rows):
            return jnp.dot(hot, rows, preferred_element_type=F32).astype(BF).reshape(NS, 32, 2 * K)

        def give(start, size, dst, send_sem, recv_sem):
            rows = pl.ds(start, size)
            to_slab(lambda peer: zsend.at[t, peer, rows], dst, send_sem, recv_sem)
            pltpu.make_async_copy(zsend.at[t, ms, rows], dst, recv_sem).start()

        @pl.when(t < LAST)
        def _():
            zsend[t, :, pl.ds(32, 32), :] = total(one_hot(pair_codes(TILES + t)), wm[...])
            whole = jnp.logical_or(t < SHARED - 1, core == 0)

            @pl.when(whole)
            def _():
                give(32, 32, zrecv.at[t, ms, pl.ds(32, 32)], y_s.at[t], y_r.at[t])

            @pl.when(jnp.logical_not(whole))
            def _():
                give(32, PL, zrecv.at[t, ms, pl.ds(32, PL)], y_s.at[t], y_r.at[t])

        zsend[t, :, pl.ds(0, 32), :] = total(one_hot(pair_codes(t)), wp[...])

        @pl.when(t < LAST)
        def _():
            give(0, 32, zrecv.at[t, ms, pl.ds(0, 32)], z_s.at[t], z_r.at[t])

        @pl.when(t == LAST)
        def _():
            give(0, PL, zgot.at[mz], z_s.at[t], z_r.at[t])

    def weights():
        lane_k = lax.broadcasted_iota(jnp.int32, (32, 128), 1)
        own_ky = mb * KYB + lax.broadcasted_iota(jnp.int32, (32, 128), 0)
        arg2_y = 2.0 * (pick(lane_k & (NDEF - 1), every) * square(own_ky) + PHASE_OFFSET)
        group = lane_k // NDEF
        tws[...] = jnp.where(
            group == 0,
            -0.5 * jnp.cos(arg2_y),
            jnp.where(group == 1, 0.5 * jnp.sin(arg2_y), jnp.where(group == 2, 0.5, 0.0)),
        )
        row_k = lax.broadcasted_iota(jnp.int32, (NDEF, K), 0)
        col_k = lax.broadcasted_iota(jnp.int32, (NDEF, K), 1)
        arg2_x = 2.0 * (pick(row_k, every) * square(col_k))
        rw = jnp.concatenate(
            [
                jnp.cos(arg2_x),
                jnp.sin(arg2_x),
                jnp.ones((NDEF, K), F32),
                jnp.zeros((128 - 3 * NDEF, K), F32),
            ],
            axis=0,
        )
        pltpu.make_async_copy(nrecv, nrecv, n_r).wait()

        def one(h, carry):
            x = nrecv[h].astype(F32)
            for z in range(1, NS // 2):
                x += nrecv[2 * z + h].astype(F32)
            own, more = 6 * h + 1, 6 * h + EXTRA
            lane = lax.broadcasted_iota(jnp.int32, (PL, 128), 1)
            blocks = []
            for g in range(2 * NCNT):
                part = x[:, g // 8 * 128 : g // 8 * 128 + 128]
                turn = [
                    pltpu.roll(part, (NDEF * (n - g)) % 128, 1) if (n - g) % 8 else part
                    for n in range(3)
                ]
                blocks.append(
                    jnp.where(lane < NDEF, turn[0], jnp.where(lane < 2 * NDEF, turn[1], turn[2]))
                )
            x = jnp.concatenate(blocks, axis=0)

            def times(part, i, rows):
                return (part.reshape(rows, PL, 128) * tws[pl.ds(i, rows), :][:, None, :]).reshape(
                    rows * PL, 128
                )

            scaled = jnp.concatenate(
                [times(x[:96], own, 6), times(x[96:128], 0, 2), times(x[128:], more, 6)], axis=0
            )
            res = jnp.dot(
                scaled, rw, precision=lax.Precision.HIGHEST, preferred_element_type=F32
            )
            res = 1.0 / (res + TAU_PRIOR)
            wts[pl.ds(pl.multiple_of(own * PL, PL), 96), :] = res[:96]
            wts[pl.ds(pl.multiple_of(more * PL, PL), 96), :] = res[128:]

            @pl.when(h == 0)
            def _():
                wts[pl.ds(0, PL), :] = res[96:112]

            return carry

        lax.fori_loop(0, 2, one, 0)

    def finish(i, sums):
        rows = pl.ds(pl.multiple_of(i * PL, PL), PL)
        inverse = wts[rows, :]
        for h in range(2):
            cols = pl.ds(h * K, K)
            top = TAU_PRIOR * ref[rows, cols].astype(F32) + sums[:, h * K : (h + 1) * K]
            held[rows, cols] = (top * inverse).astype(BF)
        pltpu.make_async_copy(held.at[rows], out.at[rows], out_m).start()

    def gather(t):
        @pl.when(t < SHARED - 1)
        def _():
            some = zrecv.at[t, :, pl.ds(32, 32)]
            pltpu.make_async_copy(some, some, y_r.at[t]).wait()

        @pl.when(t == SHARED - 1)
        def _():
            some = zrecv.at[t, pl.ds(0, 6), pl.ds(32, 32)]
            pltpu.make_async_copy(some, some, y_r.at[t]).wait()

        def over_z(h, start):
            rows = pl.ds(pl.multiple_of(start, PL), PL)
            x = zrecv[t, h, rows, :].astype(F32)
            for z in range(1, NS // 2):
                x += zrecv[t, 2 * z + h, rows, :].astype(F32)
            return x

        def mirror(m, carry):
            msend[t, m] = over_z(m // 2, 2 * PL + lax.rem(m, 2) * PL).astype(BF)
            return carry

        def pass_on(size):
            rows = pl.ds(0, size)
            lax.fori_loop(0, size, mirror, 0)
            pltpu.make_async_remote_copy(
                src_ref=msend.at[t, rows], dst_ref=mrecv.at[t, rows],
                send_sem=m_s.at[t], recv_sem=m_r.at[t],
                device_id=(NB - 1 - mb, ms), device_id_type=MESH,
            ).start()

        pl.when(t < SHARED - 1)(lambda: pass_on(4))
        pl.when(t == SHARED - 1)(lambda: pass_on(3))

        some = zrecv.at[t, :, pl.ds(0, 32)]
        pltpu.make_async_copy(some, some, z_r.at[t]).wait()

        def own(m, carry):
            h, j = m // 2, lax.rem(m, 2)
            finish(6 * h + 2 * t + 1 + j, over_z(h, j * PL))
            return carry

        lax.fori_loop(0, 4, own, 0)

    def drain(src, send_sem, recv_sem):
        return pltpu.make_async_remote_copy(
            src_ref=src, dst_ref=src, send_sem=send_sem, recv_sem=recv_sem,
            device_id=(mb, ms), device_id_type=MESH,
        )

    def mirrored(t, carry):
        @pl.when(t < SHARED - 1)
        def _():
            drain(msend.at[t], m_s.at[t], m_r.at[t]).wait()

        @pl.when(t == SHARED - 1)
        def _():
            drain(msend.at[t, pl.ds(0, 3)], m_s.at[t], m_r.at[t]).wait()


        def one(m, inner):
            i = 6 * (m // 2) + 2 * t + 1 + lax.rem(m, 2)

            @pl.when(i < KYB // 2)
            def _():
                finish(KYB - i, mrecv[t, m].astype(F32))

            return inner

        lax.fori_loop(0, 4, one, 0)
        return carry

    def consume(t, carry):
        @pl.when(jnp.logical_or(t < LAST, core == 0))
        def _():
            process(t)

        @pl.when(t < 2)
        def _():
            compute(t + 2)

        @pl.when(t == 0)
        def _():
            send_rows(2)

        @pl.when(t == 1)
        def _():
            send_last()
            weights()

        @pl.when(jnp.logical_or(t == 1, t == 2))
        def _():
            gather(t - 1)

        @pl.when(t == LAST)
        def _():
            lax.fori_loop(0, 2, mirrored, 0)

        return carry

    tally()
    load_ref.wait()
    lax.fori_loop(0, TILES, consume, 0)

    gather(SHARED - 1)
    pltpu.make_async_copy(zgot, zgot, z_r.at[LAST]).wait()
    x = zgot[0].astype(F32)
    for z in range(1, NS // 2):
        x += zgot[z].astype(F32)
    finish(0, x)

    mirrored(SHARED - 1, 0)

    drain(crecv.at[pl.ds(0, 31)], code_s, code_r).wait_send()
    pltpu.make_async_copy(held, out, out_m).wait()
    drain(nsend.at[pl.ds(0, 7)], n_s, n_r).wait_send()
    def drain_tile(t, carry):
        drain(sendb.at[t, pl.ds(0, 31)], row_s.at[t], row_r.at[t]).wait_send()
        whole = jnp.logical_or(t < SHARED - 1, core == 0)

        @pl.when(whole)
        def _():
            drain(zsend.at[t, pl.ds(0, 7), pl.ds(0, 32)], y_s.at[t], y_r.at[t]).wait_send()

        @pl.when(jnp.logical_not(whole))
        def _():
            drain(zsend.at[t, pl.ds(0, 7), pl.ds(0, PL)], y_s.at[t], y_r.at[t]).wait_send()

        drain(zsend.at[t, pl.ds(0, 7), pl.ds(0, 32)], z_s.at[t], z_r.at[t]).wait_send()
        return carry

    lax.fori_loop(0, SHARED, drain_tile, 0)

    @pl.when(core == 0)
    def _():
        drain(sendb.at[LAST, pl.ds(0, 15)], row_s.at[LAST], row_r.at[LAST]).wait_send()
        drain(zsend.at[LAST, pl.ds(0, 7), pl.ds(0, PL)], z_s.at[LAST], z_r.at[LAST]).wait_send()

    @pl.when(core == 1)
    def _():
        drain(sendb.at[LAST, pl.ds(0, 16)], row_s.at[LAST], row_r.at[LAST]).wait_send()


def per_device(images, classes, shifts, defocus_class, defocus, run_counts, dest_map, ref):
    left, right = tables()
    vmem = pl.BlockSpec(memory_space=pltpu.VMEM)
    smem = pl.BlockSpec(memory_space=pltpu.SMEM)
    far = pl.BlockSpec(memory_space=pl.ANY)
    dma = pltpu.SemaphoreType.DMA
    out = pl.pallas_call(
        kernel,
        out_shape=jax.ShapeDtypeStruct((KYB * PL, 2 * K), BF),
        in_specs=[smem] * 4 + [vmem] * 2 + [far] * 4,
        out_specs=far,
        scratch_shapes=[
            pltpu.VMEM((PP, K, K), BF),
            pltpu.VMEM((2 * K, 2 * K), BF),
            pltpu.VMEM(dest_map.shape, jnp.int32),
            pltpu.VMEM((KYB * PL, 2 * K), BF),
            pltpu.VMEM((6, 64 * PP, 128), F32),
            pltpu.VMEM((K, 128), F32),
            pltpu.VMEM((16, 128), F32),
            pltpu.VMEM((32, 16, 128), BF),
            pltpu.VMEM((32 * 16, 128), F32),
            pltpu.VMEM((TILES, 512, 128), F32),
            pltpu.VMEM((512, 4 * K), F32),
            pltpu.VMEM((3 * GROUP, 4 * K), BF),
            pltpu.VMEM((3 * GROUP, 128), BF),
            pltpu.VMEM((2, 512, 2 * K), F32),
            pltpu.VMEM((512, 2 * K), BF),
            pltpu.VMEM((512, 2 * K), BF),
            pltpu.VMEM((TILES, 32, 16, 2 * K), BF),
            pltpu.VMEM((TILES, 32, 16, 2 * K), BF),
            pltpu.VMEM((32, 16, 128), BF),
            pltpu.VMEM((TILES, NS, 64, 2 * K), BF),
            pltpu.VMEM((SHARED, NS, 64, 2 * K), BF),
            pltpu.VMEM((NS // 2, PL, 2 * K), BF),
            pltpu.VMEM((NS, PL, 256), BF),
            pltpu.VMEM((NS, PL, 256), BF),
            pltpu.VMEM((SHARED, 4, PL, 2 * K), BF),
            pltpu.VMEM((SHARED, 4, PL, 2 * K), BF),
            pltpu.VMEM(((KYB + 1) * PL, K), F32),
            pltpu.VMEM((32, 128), F32),
            pltpu.VMEM((KYB * PL, 2 * K), BF),
            dma, dma((PP,)), dma, dma, dma, dma, dma, dma((TILES,)), dma((TILES,)),
            dma((TILES,)), dma((TILES,)), dma((SHARED,)), dma((SHARED,)), dma, dma,
            dma((SHARED,)), dma((SHARED,)),
        ],
        compiler_params=pltpu.CompilerParams(
            collective_id=0, has_side_effects=True, vmem_limit_bytes=60 * 1024 * 1024
        ),
    )(
        classes, defocus_class, defocus, shifts.T, run_counts, jnp.asarray(left),
        images, jnp.asarray(right), dest_map,
        ref.reshape(KYB * PL, 2 * K),
    )
    return out.reshape(KYB, PL, 2 * K)


def solution(mesh):
    placed = (
        P(("batch", "slab"), None, None),
        P(("batch", "slab")),
        P(("batch", "slab"), None),
        P(("batch", "slab")),
        P(),
        P(("batch", "slab"), None),
        P(),
        P("batch", "slab", None),
    )
    return jax.shard_map(
        per_device, mesh=mesh, in_specs=placed, out_specs=P("batch", "slab", None), check_vma=False
    )
```

```python
import math

import jax
import jax.numpy as jnp
import ml_dtypes
import numpy as np
from jax import lax
from jax.experimental import pallas as pl
from jax.experimental.pallas import tpu as pltpu
from jax.sharding import PartitionSpec as P

TAU_PRIOR = 4.0
PHASE_OFFSET = 0.1
MESH = pl.DeviceIdType.MESH

K = 384
NB = 16
NS = 8
PP = 8
KYB = K // NB
SHARED = 3
TILES = SHARED + 1
PL = 16
NDEF = 16
BF = jnp.bfloat16
F32 = jnp.float32
LAST = SHARED
EXTRA = 13
HOPS = ((1, 0), (3, 1), (2, 0), (3, 0), (1, 1), (2, 1), (0, 1))
NCNT = TILES + 3
MOVES = 40
GROUP = 64
TURNS = (
    (0, 1), (1, 0), (0, 3), (3, 0), (1, 1), (1, 3), (3, 3), (3, 1),
    (1, 2), (2, 1), (3, 2), (2, 3), (0, 2), (2, 0), (2, 2),
)


def tables():
    index = np.arange(K)
    angle = 2.0 * np.pi / K * ((index[:, None] * index[None, :]) % K)
    cosine = (np.cos(angle) / math.sqrt(K)).astype(np.float32)
    sine = (np.sin(angle) / math.sqrt(K)).astype(np.float32)

    def left(t):
        rows = [
            KYB * b + (6 * h + 2 * t + 1 + j if t < LAST else 0)
            for h in range(2)
            for b in range(NB)
            for j in range(2)
        ]
        return np.concatenate([cosine[rows], -sine[rows]], axis=0)

    both = np.stack([left(t) for t in range(TILES)], axis=0)
    right = np.concatenate(
        [np.concatenate([cosine, -sine], 1), np.concatenate([sine, cosine], 1)], 0
    )
    kind = ml_dtypes.bfloat16
    return both.astype(kind), right.astype(kind)


def kernel(
    classes, kinds_in, defocus, shifts, counts, left, img_in, right_in, dest_in, ref_in,
    out,
    img, right, dest, ref, scr, cscr, cwide, codes, cf, sc, vx, table_x, table_s, pq, wp, wm,
    sendb, recvb, crecv, zsend, zrecv, zgot, nsend, nrecv, msend, mrecv, wts, tws, held,
    out_m, img_m, right_m, dest_m, ref_m, code_s, code_r, row_s, row_r, z_s, z_r, y_s, y_r, n_s, n_r, m_s, m_r,
):
    mb = lax.axis_index("batch")
    ms = lax.axis_index("slab")
    core = lax.rem(ms, 2)
    zbase = ms - core
    mz = ms // 2
    me = mb * 2 + core
    my = mb // 4
    mx = lax.rem(mb, 4)

    def peer_of(turn):
        dy, dx = turn
        py = lax.rem(my + jnp.where(core == 0, dy, dx), 4)
        px = lax.rem(mx + jnp.where(core == 0, dx, 4 - dy), 4)
        return py * 4 + px

    barrier = pltpu.get_barrier_semaphore()
    loads = [pltpu.make_async_copy(img_in.at[p], img.at[p], img_m.at[p]) for p in range(PP)]
    load_right = pltpu.make_async_copy(right_in, right, right_m)
    load_dest = pltpu.make_async_copy(dest_in, dest, dest_m)
    load_ref = pltpu.make_async_copy(ref_in, ref, ref_m)
    for load in (load_dest, *loads, load_right, load_ref):
        load.start()

    def greet_plane(q, carry):
        i = lax.rem(me + q, 32)
        pl.semaphore_signal(
            barrier, inc=1, device_id=(i // 2, zbase + lax.rem(i, 2)), device_id_type=MESH
        )
        return carry

    def greet_slab(q, carry):
        pl.semaphore_signal(
            barrier, inc=1, device_id=(mb, lax.rem(ms + q, NS)), device_id_type=MESH
        )
        return carry

    lax.fori_loop(1, 32, greet_plane, 0)
    lax.fori_loop(1, NS, greet_slab, 0)

    def pick(index, values):
        got = jnp.full(index.shape, values[0])
        for i, value in enumerate(values[1:], 1):
            got = jnp.where(index == i, value, got)
        return got

    def square(k):
        half = jnp.where(k >= K // 2, k - K, k).astype(F32) * (1.0 / K)
        return half * half

    def phase(k, shift):
        turn = k.astype(F32) * shift
        turn = turn - K * jnp.floor((turn + 0.5) * (1.0 / K))
        return turn * (2.0 * math.pi / K)

    def to_plane(b, h, src, dst, send_sem, recv_sem):
        pltpu.make_async_remote_copy(
            src_ref=src, dst_ref=dst, send_sem=send_sem, recv_sem=recv_sem,
            device_id=(b, zbase + h), device_id_type=MESH,
        ).start()

    def compute(t):
        table = left[t]

        def one(p, carry):
            @pl.when(t == 0)
            def _():
                pltpu.make_async_copy(img_in.at[p], img.at[p], img_m.at[p]).wait()

            sec = jnp.dot(table, img[p], preferred_element_type=F32)
            for g in range(3):
                cols = slice(g * 128, (g + 1) * 128)
                scr[g, pl.ds(p, 64, stride=8), :] = sec[:64, cols]
                scr[3 + g, pl.ds(p, 64, stride=8), :] = sec[64:, cols]
            return carry

        lax.fori_loop(0, PP, one, 0)

        def pack(i, carry):
            start = pl.multiple_of(i * 16, 16)
            target = lax.rem(i, NB) * 2 + i // NB
            for g in range(6):
                sendb[t, target, :, pl.ds(g * 128, 128)] = scr[g, pl.ds(start, 16), :].astype(BF)
            return carry

        lax.fori_loop(0, 32, pack, 0)

    other = 1 - core

    def send_rows(t):
        for h in range(2):
            own = recvb.at[t, me]

            @pl.when(core == h)
            def _():
                pltpu.make_async_copy(sendb.at[t, me], own, row_r.at[t]).start()

            @pl.when(core != h)
            def _():
                to_plane(mb, h, sendb.at[t, mb * 2 + h], own, row_s.at[t], row_r.at[t])

            for turn in TURNS:
                b = peer_of(turn)
                to_plane(b, h, sendb.at[t, b * 2 + h], own, row_s.at[t], row_r.at[t])

    def send_last():
        t = LAST

        @pl.when(core == 0)
        def _():
            pltpu.make_async_copy(sendb.at[t, me], recvb.at[t, me], row_r.at[t]).start()

        @pl.when(core == 1)
        def _():
            to_plane(mb, 0, sendb.at[t, mb * 2], recvb.at[t, me], row_s.at[t], row_r.at[t])

        for turn in TURNS:
            b = peer_of(turn)
            to_plane(b, 0, sendb.at[t, b * 2], recvb.at[t, me], row_s.at[t], row_r.at[t])

    sub_p = lax.broadcasted_iota(jnp.int32, (PP, K), 0)
    col = lax.broadcasted_iota(jnp.int32, (PP, K), 1)
    row8 = lax.broadcasted_iota(jnp.int32, (PP, 128), 0)
    lane8 = lax.broadcasted_iota(jnp.int32, (PP, 128), 1)

    def tell():
        load_dest.wait()
        end = counts[:, 0:1]
        slab = jnp.zeros((PP, K), jnp.int32)
        for i in range(1, NS):
            slab = slab + jnp.where(col >= end, 1, 0)
            end = end + counts[:, i : i + 1]
        plane = pick(sub_p, [dest[pl.ds(classes[p], 1), :] for p in range(PP)])
        place = slab * 32 + plane
        spread = jnp.where(lax.rem(lane8, PP) == row8, 1.0, 0.0)
        kind8 = pick(row8, [kinds_in[p] for p in range(PP)])

        def turned(x):
            return lax.dot_general(
                x.astype(F32), spread, (((0,), (0,)), ((), ())),
                precision=lax.Precision.HIGHEST, preferred_element_type=F32,
            )

        cscr[...] = turned(place)
        shift_x = pick(row8, [shifts[0, p] for p in range(PP)])
        shift_y = pick(row8, [shifts[1, p] for p in range(PP)])
        person = turned(pick(lane8, [kind8, shift_x, shift_y]))
        slot_one = (lax.broadcasted_iota(jnp.int32, (1, 128), 1) // PP) & 1

        def arrange(d, carry):
            base = d // 2 * KYB
            step = 6 * lax.rem(d, 2)
            for n in range(TILES + SHARED + 3):
                for_two = []
                for j in range(2):
                    if n < SHARED:
                        ky = base + step + 2 * n + 1 + j
                    elif n == LAST:
                        ky = base
                    elif n < TILES + SHARED:
                        ky = K - (base + step + 2 * (n - TILES) + 1 + j)
                    else:
                        ky = jnp.minimum(base + EXTRA + step + 2 * (n - TILES - SHARED) + j, K - 1)
                    for_two.append(cscr[pl.ds(ky, 1), :])
                cwide[n : n + 1, :] = jnp.where(slot_one == 0, for_two[0], for_two[1] + PL)
            codes[d] = cwide[...].astype(BF)
            return carry

        cwide[...] = jnp.zeros_like(cwide)
        cwide[10:13, :] = person[0:3]
        lax.fori_loop(0, 2 * NB, arrange, 0)

    def tell_send():
        def send_codes(q, carry):
            i = lax.rem(me + q, 32)
            to_plane(i // 2, lax.rem(i, 2), codes.at[i], crecv.at[me], code_s, code_r)
            return carry

        pltpu.make_async_copy(codes.at[me], crecv.at[me], code_r).start()
        lax.fori_loop(1, 32, send_codes, 0)


    slot_of = (lane8 // 8) * 2 + (lane8 & 1)
    part = (lane8 // 2) & 3
    slot_ky = mb * KYB + jnp.where(slot_of < 2 * SHARED, 6 * core + 1 + slot_of, 0)
    slot_sq = square(slot_ky)
    every = [defocus[i] for i in range(NDEF)]

    def three(x):
        high = x.astype(BF)
        mid = (x - high.astype(F32)).astype(BF)
        low = (x - high.astype(F32) - mid.astype(F32)).astype(BF)
        return jnp.concatenate([high, mid, low], axis=0)

    def rows_of(shape, axis=0):
        return lax.broadcasted_iota(jnp.int32, shape, axis)

    def tabulate():
        turn = phase(rows_of((MOVES, K), 1), (rows_of((MOVES, K)) - 16).astype(F32))
        arg = pick(rows_of((NDEF, K)), every) * square(rows_of((NDEF, K), 1))
        spare = GROUP - MOVES - NDEF
        for n, (move, kind) in enumerate(
            (
                (jnp.cos(turn), None),
                (-jnp.sin(turn), None),
                (None, jnp.sin(arg)),
                (None, jnp.cos(arg)),
            )
        ):
            move = jnp.zeros((MOVES, K), F32) if move is None else move
            kind = jnp.zeros((NDEF, K), F32) if kind is None else kind
            full = jnp.concatenate([move, kind, jnp.zeros((spare, K), F32)], axis=0)
            table_x[:, pl.ds(n * K, K)] = three(full)
        turn = phase(slot_ky[0:1], (rows_of((MOVES, 128)) - 16).astype(F32))
        arg = pick(rows_of((NDEF, 128)), every) * slot_sq[0:1] + PHASE_OFFSET
        kind = part[0:1]
        move = jnp.where(kind == 2, -jnp.cos(turn), jnp.where(kind == 3, jnp.sin(turn), 0.0))
        tone = jnp.where(kind == 0, jnp.sin(arg), jnp.where(kind == 1, jnp.cos(arg), 0.0))
        table_s[...] = three(
            jnp.concatenate([move, tone, jnp.zeros((spare, 128), F32)], axis=0)
        )

    tell()
    tabulate()

    def produce(t, carry):
        compute(t)

        @pl.when(t == 0)
        def _():
            pl.semaphore_wait(barrier, 31 + NS - 1)
            tell_send()

        send_rows(t)
        return carry

    lax.fori_loop(0, 2, produce, 0)

    pltpu.make_async_copy(crecv, crecv, code_r).wait()

    def widen(i, carry):
        cf[pl.ds(pl.multiple_of(i * 16, 16), 16), :] = crecv[i].astype(F32)
        return carry

    lax.fori_loop(0, 32, widen, 0)

    lane = lax.broadcasted_iota(jnp.int32, (32, 128), 1)
    sub = lax.broadcasted_iota(jnp.int32, (32, 128), 0)
    mine = (lane // 16) == lax.rem(sub, 8)

    def pair_codes(row):
        got = cf[pl.ds(row, 32, stride=16), :]
        return jnp.sum(jnp.where(mine, got, 0.0).reshape(4, 8, 128), axis=1)

    spot = lax.broadcasted_iota(jnp.int32, (256, 128), 0).astype(F32)

    def one_hot(code4):
        return jnp.concatenate(
            [
                jnp.where(spot == code4[g : g + 1, :], 1.0, 0.0).astype(BF)
                for g in range(4)
            ],
            axis=1,
        )

    def to_slab(src, dst, send_sem, recv_sem):
        for dz, flip in HOPS:
            z = lax.rem(mz + jnp.where(core == 0, dz, 4 - dz), 4)
            peer = z * 2 + (1 - core if flip else core)
            pltpu.make_async_remote_copy(
                src_ref=src(peer), dst_ref=dst, send_sem=send_sem, recv_sem=recv_sem,
                device_id=(mb, peer), device_id_type=MESH,
            ).start()

    kind4 = pair_codes(10)

    def tally():
        spot_z = lax.broadcasted_iota(jnp.int32, (128, 128), 0).astype(F32)
        slot_k = ((lax.broadcasted_iota(jnp.int32, (4, 128), 1) // PP) & 1).astype(F32)
        which = kind4 + NDEF * slot_k

        def hot(code4):
            return jnp.concatenate(
                [
                    jnp.where(spot_z == code4[g : g + 1, :], 1.0, 0.0).astype(BF)
                    for g in range(4)
                ],
                axis=1,
            )

        def one(n, acc):
            code4 = pair_codes(jnp.where(n < TILES, n, n + SHARED))
            flat = code4 - 16.0 * jnp.floor(code4 * (1.0 / 16)) + 16.0 * jnp.floor(code4 * (1.0 / 32))
            group = ((n & 3) * 2 * NDEF).astype(F32)
            return acc + lax.dot_general(
                hot(flat), hot(which + group), (((1,), (1,)), ((), ())), preferred_element_type=F32
            )

        for half, (low, high) in enumerate(((0, 4), (4, NCNT))):
            acc = lax.fori_loop(low, high, one, jnp.zeros((128, 128), F32))
            nsend[:, :, pl.ds(half * 128, 128)] = acc.astype(BF).reshape(NS, PL, 128)
        to_slab(lambda peer: nsend.at[peer], nrecv.at[ms], n_s, n_r)
        pltpu.make_async_copy(nsend.at[ms], nrecv.at[ms], n_r).start()

    entry = (rows_of((3 * GROUP, 128)) & (GROUP - 1)).astype(F32)

    def chosen(move4, table):
        hot = jnp.concatenate(
            [
                jnp.where(
                    (entry == move4[g : g + 1, :] + 16.0)
                    | (entry == kind4[g : g + 1, :] + float(MOVES)),
                    1.0,
                    0.0,
                ).astype(BF)
                for g in range(4)
            ],
            axis=1,
        )
        return lax.dot_general(
            hot, table, (((0,), (0,)), ((), ())), preferred_element_type=F32
        )

    vx[...] = chosen(pair_codes(11), table_x[...])
    scal = chosen(pair_codes(12), table_s[...])
    sc[0] = scal
    for t in range(1, TILES):
        sc[t] = pltpu.roll(scal, 128 - 8 * t, 1)

    load_right.wait()

    def process(t):
        pltpu.make_async_copy(recvb.at[t], recvb.at[t], row_r.at[t]).wait()

        def half(m, carry):
            block = recvb[t, pl.ds(m * 16, 16)].reshape(256, 2 * K)
            start = pl.multiple_of(m * 256, 256)
            pq[0, pl.ds(start, 256), :] = jnp.dot(
                block[:, :K], right[pl.ds(0, K), :], preferred_element_type=F32
            )
            pq[1, pl.ds(start, 256), :] = jnp.dot(
                block[:, K:], right[pl.ds(K, K), :], preferred_element_type=F32
            )
            return carry

        lax.fori_loop(0, 2, half, 0)

        def weigh(i, carry, mirrored=True):
            got = [[], [], [], []]
            for j in range(2):
                rows = pl.ds(pl.multiple_of(i * 16 + j * 8, 8), 8)
                scal = sc[t, rows, :]
                sa, ca, er, ei = [scal[:, 2 * n + j : 2 * n + j + 1] for n in range(4)]
                exr, exi, sb, cb = [vx[rows, pl.ds(n * K, K)] for n in range(4)]
                pr, pi = pq[0, rows, pl.ds(0, K)], pq[0, rows, pl.ds(K, K)]
                qr, qi = pq[1, rows, pl.ds(0, K)], pq[1, rows, pl.ds(K, K)]
                ctf = sa * cb + ca * sb
                gr, gi = ctf * exr, ctf * exi
                fa, fb, fc, fd = er * gr, ei * gi, er * gi, ei * gr
                sr, si = pr + qr, pi + qi
                fr, fi = fa - fb, fc + fd
                got[0].append(sr * fr - si * fi)
                got[1].append(sr * fi + si * fr)
                if not mirrored:
                    continue
                sr, si = pr - qr, pi - qi
                fr, fi = fa + fb, fc - fd
                got[2].append(sr * fr - si * fi)
                got[3].append(sr * fi + si * fr)
            rows = pl.ds(pl.multiple_of(i * 16, 16), 16)
            for n in range(4 if mirrored else 2):
                to = wp if n < 2 else wm
                to[rows, pl.ds((n % 2) * K, K)] = jnp.concatenate(got[n], axis=0).astype(BF)
            return carry

        @pl.when(t < LAST)
        def _():
            lax.fori_loop(0, 32, weigh, 0, unroll=4)

        @pl.when(t == LAST)
        def _():
            lax.fori_loop(0, 32, lambda i, carry: weigh(i, carry, False), 0, unroll=4)


        def total(hot, rows):
            return jnp.dot(hot, rows, preferred_element_type=F32).astype(BF).reshape(NS, 32, 2 * K)

        def give(start, size, dst, send_sem, recv_sem):
            rows = pl.ds(start, size)
            to_slab(lambda peer: zsend.at[t, peer, rows], dst, send_sem, recv_sem)
            pltpu.make_async_copy(zsend.at[t, ms, rows], dst, recv_sem).start()

        @pl.when(t < LAST)
        def _():
            zsend[t, :, pl.ds(32, 32), :] = total(one_hot(pair_codes(TILES + t)), wm[...])
            whole = jnp.logical_or(t < SHARED - 1, core == 0)

            @pl.when(whole)
            def _():
                give(32, 32, zrecv.at[t, ms, pl.ds(32, 32)], y_s.at[t], y_r.at[t])

            @pl.when(jnp.logical_not(whole))
            def _():
                give(32, PL, zrecv.at[t, ms, pl.ds(32, PL)], y_s.at[t], y_r.at[t])

        zsend[t, :, pl.ds(0, 32), :] = total(one_hot(pair_codes(t)), wp[...])

        @pl.when(t < LAST)
        def _():
            give(0, 32, zrecv.at[t, ms, pl.ds(0, 32)], z_s.at[t], z_r.at[t])

        @pl.when(t == LAST)
        def _():
            give(0, PL, zgot.at[mz], z_s.at[t], z_r.at[t])

    def weights():
        lane_k = lax.broadcasted_iota(jnp.int32, (32, 128), 1)
        own_ky = mb * KYB + lax.broadcasted_iota(jnp.int32, (32, 128), 0)
        arg2_y = 2.0 * (pick(lane_k & (NDEF - 1), every) * square(own_ky) + PHASE_OFFSET)
        group = lane_k // NDEF
        tws[...] = jnp.where(
            group == 0,
            -0.5 * jnp.cos(arg2_y),
            jnp.where(group == 1, 0.5 * jnp.sin(arg2_y), jnp.where(group == 2, 0.5, 0.0)),
        )
        row_k = lax.broadcasted_iota(jnp.int32, (NDEF, K), 0)
        col_k = lax.broadcasted_iota(jnp.int32, (NDEF, K), 1)
        arg2_x = 2.0 * (pick(row_k, every) * square(col_k))
        rw = jnp.concatenate(
            [
                jnp.cos(arg2_x),
                jnp.sin(arg2_x),
                jnp.ones((NDEF, K), F32),
                jnp.zeros((128 - 3 * NDEF, K), F32),
            ],
            axis=0,
        )
        pltpu.make_async_copy(nrecv, nrecv, n_r).wait()

        def one(h, carry):
            x = nrecv[h].astype(F32)
            for z in range(1, NS // 2):
                x += nrecv[2 * z + h].astype(F32)
            own, more = 6 * h + 1, 6 * h + EXTRA
            lane = lax.broadcasted_iota(jnp.int32, (PL, 128), 1)
            blocks = []
            for g in range(2 * NCNT):
                part = x[:, g // 8 * 128 : g // 8 * 128 + 128]
                turn = [
                    pltpu.roll(part, (NDEF * (n - g)) % 128, 1) if (n - g) % 8 else part
                    for n in range(3)
                ]
                blocks.append(
                    jnp.where(lane < NDEF, turn[0], jnp.where(lane < 2 * NDEF, turn[1], turn[2]))
                )
            x = jnp.concatenate(blocks, axis=0)

            def times(part, i, rows):
                return (part.reshape(rows, PL, 128) * tws[pl.ds(i, rows), :][:, None, :]).reshape(
                    rows * PL, 128
                )

            scaled = jnp.concatenate(
                [times(x[:96], own, 6), times(x[96:128], 0, 2), times(x[128:], more, 6)], axis=0
            )
            res = jnp.dot(
                scaled, rw, precision=lax.Precision.HIGHEST, preferred_element_type=F32
            )
            res = 1.0 / (res + TAU_PRIOR)
            wts[pl.ds(pl.multiple_of(own * PL, PL), 96), :] = res[:96]
            wts[pl.ds(pl.multiple_of(more * PL, PL), 96), :] = res[128:]

            @pl.when(h == 0)
            def _():
                wts[pl.ds(0, PL), :] = res[96:112]

            return carry

        lax.fori_loop(0, 2, one, 0)

    def finish(i, sums):
        rows = pl.ds(pl.multiple_of(i * PL, PL), PL)
        inverse = wts[rows, :]
        for h in range(2):
            cols = pl.ds(h * K, K)
            top = TAU_PRIOR * ref[rows, cols].astype(F32) + sums[:, h * K : (h + 1) * K]
            held[rows, cols] = (top * inverse).astype(BF)
        pltpu.make_async_copy(held.at[rows], out.at[rows], out_m).start()

    def gather(t):
        @pl.when(t < SHARED - 1)
        def _():
            some = zrecv.at[t, :, pl.ds(32, 32)]
            pltpu.make_async_copy(some, some, y_r.at[t]).wait()

        @pl.when(t == SHARED - 1)
        def _():
            some = zrecv.at[t, pl.ds(0, 6), pl.ds(32, 32)]
            pltpu.make_async_copy(some, some, y_r.at[t]).wait()

        def over_z(h, start):
            rows = pl.ds(pl.multiple_of(start, PL), PL)
            x = zrecv[t, h, rows, :].astype(F32)
            for z in range(1, NS // 2):
                x += zrecv[t, 2 * z + h, rows, :].astype(F32)
            return x

        def mirror(m, carry):
            msend[t, m] = over_z(m // 2, 2 * PL + lax.rem(m, 2) * PL).astype(BF)
            return carry

        def pass_on(size):
            rows = pl.ds(0, size)
            lax.fori_loop(0, size, mirror, 0)
            pltpu.make_async_remote_copy(
                src_ref=msend.at[t, rows], dst_ref=mrecv.at[t, rows],
                send_sem=m_s.at[t], recv_sem=m_r.at[t],
                device_id=(NB - 1 - mb, ms), device_id_type=MESH,
            ).start()

        pl.when(t < SHARED - 1)(lambda: pass_on(4))
        pl.when(t == SHARED - 1)(lambda: pass_on(3))

        some = zrecv.at[t, :, pl.ds(0, 32)]
        pltpu.make_async_copy(some, some, z_r.at[t]).wait()

        def own(m, carry):
            h, j = m // 2, lax.rem(m, 2)
            finish(6 * h + 2 * t + 1 + j, over_z(h, j * PL))
            return carry

        lax.fori_loop(0, 4, own, 0)

    def drain(src, send_sem, recv_sem):
        return pltpu.make_async_remote_copy(
            src_ref=src, dst_ref=src, send_sem=send_sem, recv_sem=recv_sem,
            device_id=(mb, ms), device_id_type=MESH,
        )

    def mirrored(t, carry):
        @pl.when(t < SHARED - 1)
        def _():
            drain(msend.at[t], m_s.at[t], m_r.at[t]).wait()

        @pl.when(t == SHARED - 1)
        def _():
            drain(msend.at[t, pl.ds(0, 3)], m_s.at[t], m_r.at[t]).wait()


        def one(m, inner):
            i = 6 * (m // 2) + 2 * t + 1 + lax.rem(m, 2)

            @pl.when(i < KYB // 2)
            def _():
                finish(KYB - i, mrecv[t, m].astype(F32))

            return inner

        lax.fori_loop(0, 4, one, 0)
        return carry

    def consume(t, carry):
        @pl.when(jnp.logical_or(t < LAST, core == 0))
        def _():
            process(t)

        @pl.when(t < 2)
        def _():
            compute(t + 2)

        @pl.when(t == 0)
        def _():
            send_rows(2)

        @pl.when(t == 1)
        def _():
            send_last()
            weights()

        @pl.when(jnp.logical_or(t == 1, t == 2))
        def _():
            gather(t - 1)

        return carry

    tally()
    load_ref.wait()
    lax.fori_loop(0, TILES, consume, 0)

    gather(SHARED - 1)
    pltpu.make_async_copy(zgot, zgot, z_r.at[LAST]).wait()
    x = zgot[0].astype(F32)
    for z in range(1, NS // 2):
        x += zgot[z].astype(F32)
    finish(0, x)

    lax.fori_loop(0, SHARED, mirrored, 0)

    drain(crecv.at[pl.ds(0, 31)], code_s, code_r).wait_send()
    pltpu.make_async_copy(held, out, out_m).wait()
    drain(nsend.at[pl.ds(0, 7)], n_s, n_r).wait_send()
    def drain_tile(t, carry):
        drain(sendb.at[t, pl.ds(0, 31)], row_s.at[t], row_r.at[t]).wait_send()
        whole = jnp.logical_or(t < SHARED - 1, core == 0)

        @pl.when(whole)
        def _():
            drain(zsend.at[t, pl.ds(0, 7), pl.ds(0, 32)], y_s.at[t], y_r.at[t]).wait_send()

        @pl.when(jnp.logical_not(whole))
        def _():
            drain(zsend.at[t, pl.ds(0, 7), pl.ds(0, PL)], y_s.at[t], y_r.at[t]).wait_send()

        drain(zsend.at[t, pl.ds(0, 7), pl.ds(0, 32)], z_s.at[t], z_r.at[t]).wait_send()
        return carry

    lax.fori_loop(0, SHARED, drain_tile, 0)

    @pl.when(core == 0)
    def _():
        drain(sendb.at[LAST, pl.ds(0, 15)], row_s.at[LAST], row_r.at[LAST]).wait_send()
        drain(zsend.at[LAST, pl.ds(0, 7), pl.ds(0, PL)], z_s.at[LAST], z_r.at[LAST]).wait_send()

    @pl.when(core == 1)
    def _():
        drain(sendb.at[LAST, pl.ds(0, 16)], row_s.at[LAST], row_r.at[LAST]).wait_send()


def per_device(images, classes, shifts, defocus_class, defocus, run_counts, dest_map, ref):
    left, right = tables()
    vmem = pl.BlockSpec(memory_space=pltpu.VMEM)
    smem = pl.BlockSpec(memory_space=pltpu.SMEM)
    far = pl.BlockSpec(memory_space=pl.ANY)
    dma = pltpu.SemaphoreType.DMA
    out = pl.pallas_call(
        kernel,
        out_shape=jax.ShapeDtypeStruct((KYB * PL, 2 * K), BF),
        in_specs=[smem] * 4 + [vmem] * 2 + [far] * 4,
        out_specs=far,
        scratch_shapes=[
            pltpu.VMEM((PP, K, K), BF),
            pltpu.VMEM((2 * K, 2 * K), BF),
            pltpu.VMEM(dest_map.shape, jnp.int32),
            pltpu.VMEM((KYB * PL, 2 * K), BF),
            pltpu.VMEM((6, 64 * PP, 128), F32),
            pltpu.VMEM((K, 128), F32),
            pltpu.VMEM((16, 128), F32),
            pltpu.VMEM((32, 16, 128), BF),
            pltpu.VMEM((32 * 16, 128), F32),
            pltpu.VMEM((TILES, 512, 128), F32),
            pltpu.VMEM((512, 4 * K), F32),
            pltpu.VMEM((3 * GROUP, 4 * K), BF),
            pltpu.VMEM((3 * GROUP, 128), BF),
            pltpu.VMEM((2, 512, 2 * K), F32),
            pltpu.VMEM((512, 2 * K), BF),
            pltpu.VMEM((512, 2 * K), BF),
            pltpu.VMEM((TILES, 32, 16, 2 * K), BF),
            pltpu.VMEM((TILES, 32, 16, 2 * K), BF),
            pltpu.VMEM((32, 16, 128), BF),
            pltpu.VMEM((TILES, NS, 64, 2 * K), BF),
            pltpu.VMEM((SHARED, NS, 64, 2 * K), BF),
            pltpu.VMEM((NS // 2, PL, 2 * K), BF),
            pltpu.VMEM((NS, PL, 256), BF),
            pltpu.VMEM((NS, PL, 256), BF),
            pltpu.VMEM((SHARED, 4, PL, 2 * K), BF),
            pltpu.VMEM((SHARED, 4, PL, 2 * K), BF),
            pltpu.VMEM(((KYB + 1) * PL, K), F32),
            pltpu.VMEM((32, 128), F32),
            pltpu.VMEM((KYB * PL, 2 * K), BF),
            dma, dma((PP,)), dma, dma, dma, dma, dma, dma((TILES,)), dma((TILES,)),
            dma((TILES,)), dma((TILES,)), dma((SHARED,)), dma((SHARED,)), dma, dma,
            dma((SHARED,)), dma((SHARED,)),
        ],
        compiler_params=pltpu.CompilerParams(
            collective_id=0, has_side_effects=True, vmem_limit_bytes=60 * 1024 * 1024
        ),
    )(
        classes, defocus_class, defocus, shifts.T, run_counts, jnp.asarray(left),
        images, jnp.asarray(right), dest_map,
        ref.reshape(KYB * PL, 2 * K),
    )
    return out.reshape(KYB, PL, 2 * K)


def solution(mesh):
    placed = (
        P(("batch", "slab"), None, None),
        P(("batch", "slab")),
        P(("batch", "slab"), None),
        P(("batch", "slab")),
        P(),
        P(("batch", "slab"), None),
        P(),
        P("batch", "slab", None),
    )
    return jax.shard_map(
        per_device, mesh=mesh, in_specs=placed, out_specs=P("batch", "slab", None), check_vma=False
    )
```
